256 devices in a mesh: tile: 64 (over z, x, core), mem: 4 (over y).
Axes of the slice: x: 4, y: 4, z: 8, core: 2. Of those that a mesh axis runs over, the one named last changes fastest.
Arguments:
- footprints: bfloat16 [8192, 128, 128], P('tile'), may hold values from -0.1875 to 0.1875
- tile_row: int32 [8192], P('tile'), may hold values from 0 to 1023, as said below
- tile_col: int32 [8192], P('tile'), may hold values from 0 to 511, as said below
- prior_flux: bfloat16 [256, 65536], P('mem', 'tile'), may hold values from -12 to 12
- observed: float32 [256, 131072], P('mem', 'tile'), may hold values from -6 to 6
- precision_weight: int32 [131072], P('tile'), may hold values from 1 to 16
Outputs:
- gradient: float32 [256, 65536], P('mem', 'tile')
The draws below stay inside these ranges and needn't reach their ends.
Inputs may be any that keep to these rules, and one draw needn't show every extreme that they name: Among the 128 tiles of each index of tile, at most 3 have a row block of one owner (owner = tile_row // 16); in every draw one owner gets exactly 3 from every index. Likewise with owner = tile_col // 8: at most 3 from one index of tile to one owner, and one owner gets exactly 3 from every index.
All inputs are finite; a program needn't handle non-finite values.
Results may differ from the reference program's by a relative error of at most 0.0052.
Values may be sent and summed in bfloat16 or wider, within the bound.
A program may use at most 64 MiB of HBM per device.

```python
import jax
import jax.numpy as jnp
from jax import lax

B = 128
MEMBERS = 256
TILE_DEV = 128
FLUX_DEV = 8
SOUND_DEV = 16
TILES = 8192
SOUNDINGS = 131072
N_TILE = 64


def spread_blocks(key, per_owner):
    capacity = TILE_DEV // N_TILE + max(1, TILE_DEV // (2 * N_TILE))
    slot_count = N_TILE * capacity
    key_perm, key_hot, key_local = jax.random.split(key, 3)
    hottest = jax.random.randint(key_hot, (), 0, N_TILE)
    key_list = jax.random.split(key_perm, N_TILE)
    ranking = jax.vmap(lambda random_subkey: jax.random.permutation(random_subkey, slot_count))(key_list)
    slot_owner = jnp.arange(slot_count) // capacity
    priority = ranking + slot_count * (slot_owner == hottest).astype(jnp.int32)[None, :]
    top_values, chosen = lax.top_k(priority, TILE_DEV)
    owners = chosen // capacity
    local_block = jax.random.randint(key_local, (N_TILE, TILE_DEV), 0, per_owner)
    return (owners * per_owner + local_block).reshape(-1).astype(jnp.int32)


def draw_tile_row(key, part):
    return spread_blocks(jax.random.fold_in(key, 11), SOUND_DEV)


def draw_tile_col(key, part):
    return spread_blocks(jax.random.fold_in(key, 23), FLUX_DEV)


def draw_prior_flux(key, part):
    key_center, key_noise = jax.random.split(jax.random.fold_in(key, 37))
    cells = FLUX_DEV * B * N_TILE
    background = 2.0 * jax.random.normal(key_center, (1, cells), jnp.float32)
    member_noise = jax.random.normal(key_noise, (MEMBERS, cells), jnp.float32)
    return jnp.clip(background + member_noise, -12.0, 12.0).astype(jnp.bfloat16)


def plant(array, rng, low, largest):
    extent = array.shape
    spot = [jax.random.randint(jax.random.fold_in(rng, axis), (), 0, extent[axis]) for axis in range(len(extent))]
    array = array.at[tuple(spot)].set(low)
    longest = extent.index(max(extent))
    spot[longest] = (spot[longest] + 1) % extent[longest]
    return array.at[tuple(spot)].set(largest)


def level_of(stream_key, shape, cuts, smallest, largest):
    level, own = 1.0, jax.random.fold_in(stream_key, 6)
    for dim, blocks in cuts:
        steps = jnp.exp(jax.random.uniform(jax.random.fold_in(own, dim), (blocks,), jnp.float32, smallest / len(cuts), largest / len(cuts)))
        level = level * jnp.repeat(steps, shape[dim] // blocks).reshape([-1 if axis == dim else 1 for axis in range(len(shape))])
    return level


def scatter_about(key, shape, scale, bound, shards=(), dtype=jnp.bfloat16):
    result = scale * jax.random.normal(key, shape, jnp.float32)
    if shards:
        result = result * level_of(key, shape, shards, -0.22, 0.18)
    return jnp.clip(result, -bound, bound).astype(dtype)


def setup_inputs(seed: int = 0) -> dict:
    key_of = jax.random.split(jax.random.key(seed), 7)
    return {
        "footprints": scatter_about(key_of[0], (TILES, B, B), (B * TILE_DEV // SOUND_DEV) ** -0.5, 0.1875, ((0, 64),)),
        "tile_row": draw_tile_row(jax.random.fold_in(key_of[6], 71), 0),
        "tile_col": draw_tile_col(jax.random.fold_in(key_of[6], 71), 0),
        "prior_flux": draw_prior_flux(jax.random.fold_in(key_of[6], 71), 0),
        "observed": scatter_about(key_of[4], (MEMBERS, SOUNDINGS), 1.0, 6.0, ((0, 4), (1, 64)), jnp.float32),
        "precision_weight": plant(jax.random.randint(key_of[5], (SOUNDINGS,), 1, 17), jax.random.fold_in(key_of[5], 1), 1, 16).astype(jnp.int32),
    }


def reference(footprints, tile_row, tile_col, prior_flux, observed, precision_weight):
    ensemble_mean = jnp.sum(prior_flux.astype(jnp.float32), axis=0, keepdims=True) / MEMBERS
    member_deviations = (prior_flux.astype(jnp.float32) - ensemble_mean).astype(jnp.bfloat16)
    flux_count = FLUX_DEV * N_TILE
    sound_blocks = SOUND_DEV * N_TILE
    flux_blocks = member_deviations.reshape(MEMBERS, flux_count, B).transpose(1, 0, 2)
    grouped = footprints.reshape(N_TILE, TILE_DEV, B, B)
    row_groups = tile_row.reshape(N_TILE, TILE_DEV).astype(jnp.int32)
    col_groups = tile_col.reshape(N_TILE, TILE_DEV).astype(jnp.int32)

    def forward(totals, inputs):
        footprint_block_grid, block_rows, block_cols = inputs
        retrieved_blocks = jnp.take(flux_blocks, block_cols, axis=0).astype(jnp.float32)
        tile_products = jnp.einsum("cuz,cdz->cud", retrieved_blocks, footprint_block_grid.astype(jnp.float32))
        return totals.at[block_rows].add(tile_products), None

    modelled = lax.scan(forward, jnp.zeros((sound_blocks, MEMBERS, B), jnp.float32), (grouped, row_groups, col_groups))[0]
    obs_blocks = observed.reshape(MEMBERS, sound_blocks, B).transpose(1, 0, 2)
    weight_factor = (precision_weight.astype(jnp.float32) / 8.0).reshape(sound_blocks, 1, B)
    weighted = (weight_factor * (modelled - obs_blocks)).astype(jnp.bfloat16)

    def backward(totals, inputs):
        footprint_block_grid, block_rows, block_cols = inputs
        retrieved_blocks = jnp.take(weighted, block_rows, axis=0).astype(jnp.float32)
        tile_products = jnp.einsum("bnh,bhd->bnd", retrieved_blocks, footprint_block_grid.astype(jnp.float32))
        return totals.at[block_cols].add(tile_products), None

    flux_totals = lax.scan(backward, jnp.zeros((flux_count, MEMBERS, B), jnp.float32), (grouped, row_groups, col_groups))[0]
    return flux_totals.transpose(1, 0, 2).reshape(MEMBERS, flux_count * B)
```

```python
import functools

import jax
import jax.numpy as jnp
from jax import lax
from jax.experimental import pallas as pl
from jax.experimental.pallas import tpu as pltpu
from jax.sharding import PartitionSpec as P

MEMBERS = 256
FLUX_DEV = 8
SOUND_DEV = 16
NZ, NX, NY, NT = 8, 4, 4, 64
CAP = 3
B = 128
LM = 64
MESH = pl.DeviceIdType.MESH
F32, BF16 = jnp.float32, jnp.bfloat16


def route(tile_row, tile_col):
    count = tile_row.shape[0]
    owner = tile_row // SOUND_DEV
    position = jnp.arange(count)
    earlier = (owner[:, None] == owner[None, :]) & (position[None, :] < position[:, None])
    slot = owner * CAP + jnp.sum(earlier.astype(jnp.int32), axis=1)
    match = slot[None, :] == jnp.arange(NT * CAP)[:, None]
    source = jnp.sum(jnp.where(match, position[None, :], 0), axis=1)
    blocks = (tile_row % SOUND_DEV) * 512 + tile_col
    coded = jnp.sum(jnp.where(match, blocks[None, :] + 1, 0), axis=1)
    coded = jnp.where(coded == 0, SOUND_DEV * 512, coded - 1)
    coded = jnp.pad(coded.reshape(NT, CAP), ((0, 0), (0, B - CAP))).reshape(NT, 1, B)
    return source, coded


def spread_kernel(
    source, coded, footprints, prior, tiles, anoms, codes,
    quarter, staged, sums, shard,
    s_fp, s_sum, r_sum, s_tile, r_tile, s_code, r_code, s_y, r_y, r_y2,
    s_local, s_z, r_z, s_x, r_x, r_x2, s_sib, r_sib,
):
    me = lax.axis_index("tile")
    q = lax.axis_index("mem")
    core = lax.rem(me, 2)
    x = lax.rem(me // 2, NX)
    z = me // 8

    def at_z(o):
        return lax.rem(z + o + NZ, NZ)

    def at_x(o):
        return lax.rem(x + o + NX, NX)

    def at_y(o):
        return lax.rem(q + o + NY, NY)

    def index(zz, xx, cc):
        return zz * 8 + xx * 2 + cc

    def remote(src, dst, ssem, rsem, tile=None, mem=None):
        return pltpu.make_async_remote_copy(
            src_ref=src, dst_ref=dst, send_sem=ssem, recv_sem=rsem,
            device_id={"tile": me if tile is None else tile, "mem": q if mem is None else mem},
            device_id_type=MESH,
        )

    def wait_for(ref, sem):
        pltpu.make_async_copy(ref, ref, sem).wait()

    fp_copy = pltpu.make_async_copy(
        footprints.at[:, pl.ds(pl.multiple_of(q * 32, 32), 32), :], quarter, s_fp
    )
    fp_copy.start()

    barrier = pltpu.get_barrier_semaphore()

    @pl.loop(1, NT)
    def _(o):
        pl.semaphore_signal(
            barrier, inc=1, device_id={"tile": lax.rem(me + o, NT), "mem": q}, device_id_type=MESH
        )

    for o in range(1, NY):
        pl.semaphore_signal(
            barrier, inc=1, device_id={"tile": me, "mem": at_y(o)}, device_id_type=MESH
        )

    for j in range(FLUX_DEV):
        part = jnp.sum(prior[:, j * B : (j + 1) * B].astype(F32), axis=0, keepdims=True)
        sums[0, j : j + 1, :] = part
    pl.semaphore_wait(barrier, NT - 1 + NY - 1)

    sum_sends = []
    for o in range(1, NY):
        cp = remote(sums.at[0], sums.at[o], s_sum.at[o], r_sum.at[o], mem=at_y(o))
        cp.start()
        sum_sends.append(cp)
    fp_copy.wait()

    def send_tiles(dz):
        first = 1 if dz == 0 else 0

        @pl.loop(first, 8)
        def _(o):
            t = at_z(dz) * 8 + lax.rem(me + o, 8)
            for s in range(CAP):
                staged[t, s] = quarter[source[t * CAP + s]]
            remote(staged.at[t], tiles.at[q, me], s_tile, r_tile.at[dz], tile=t).start()
            remote(coded.at[t], codes.at[me], s_code, r_code, tile=t).start()

        if dz == 0:
            for s in range(CAP):
                staged[me, s] = quarter[source[me * CAP + s]]
            pltpu.make_async_copy(staged.at[me], tiles.at[q, me], r_tile.at[0]).start()
            pltpu.make_async_copy(coded.at[me], codes.at[me], r_code).start()

    def group(quarter_index, dz, first=0, size=8):
        zs = at_z(-dz)
        return tiles.at[quarter_index, pl.ds(zs * 8 + first, size)]

    pending = []

    def go(cp):
        cp.start()
        pending.append(cp)

    def y_first(dz):
        wait_for(group(q, dz), r_tile.at[dz])
        go(remote(group(q, dz), group(q, dz), s_y.at[0, dz], r_y.at[0, dz], mem=at_y(1)))
        go(remote(group(q, dz), group(q, dz), s_y.at[1, dz], r_y.at[1, dz], mem=at_y(-1)))

    def y_second(dz):
        back = group(at_y(-1), dz)
        wait_for(back, r_y.at[0, dz])
        part = group(at_y(-1), dz, 0, 4)
        go(remote(part, part, s_y.at[2, dz], r_y2.at[0, dz], mem=at_y(1)))
        fore = group(at_y(1), dz)
        wait_for(fore, r_y.at[1, dz])
        part = group(at_y(1), dz, 4, 4)
        go(remote(part, part, s_y.at[3, dz], r_y2.at[1, dz], mem=at_y(-1)))

    def y_last(dz):
        wait_for(group(at_y(2), dz, 0, 4), r_y2.at[0, dz])
        wait_for(group(at_y(2), dz, 4, 4), r_y2.at[1, dz])

    def block(oz, ox, own_core=True):
        return anoms.at[index(at_z(oz), at_x(ox), core if own_core else 1 - core)]

    def to_sibling(oz, ox):
        go(
            remote(
                block(oz, ox), block(oz, ox), s_sib.at[ox % NX, oz % NZ], r_sib.at[ox % NX, oz % NZ],
                tile=index(z, x, 1 - core),
            )
        )

    def x_first(oz, src=None):
        b = block(oz, 0)
        src = b if src is None else src
        k = oz % NZ
        go(remote(src, b, s_x.at[0, k], r_x.at[0, k], tile=index(z, at_x(1), core)))
        go(remote(src, b, s_x.at[1, k], r_x.at[1, k], tile=index(z, at_x(-1), core)))
        go(remote(src, b, s_sib.at[0, k], r_sib.at[0, k], tile=index(z, x, 1 - core)))

    def x_second(oz):
        k = oz % NZ
        b = block(oz, -1)
        wait_for(b, r_x.at[0, k])
        h = b.at[pl.ds(0, 4)]
        go(remote(h, h, s_x.at[2, k], r_x2.at[0, k], tile=index(z, at_x(1), core)))
        to_sibling(oz, -1)
        b = block(oz, 1)
        wait_for(b, r_x.at[1, k])
        h = b.at[pl.ds(4, 4)]
        go(remote(h, h, s_x.at[3, k], r_x2.at[1, k], tile=index(z, at_x(-1), core)))
        to_sibling(oz, 1)

    def x_last(oz):
        k = oz % NZ
        b = block(oz, 2)
        wait_for(b.at[pl.ds(0, 4)], r_x2.at[0, k])
        wait_for(b.at[pl.ds(4, 4)], r_x2.at[1, k])
        to_sibling(oz, 2)

    def z_step(k):
        up, down = index(at_z(1), x, core), index(at_z(-1), x, core)
        if k < 4:
            b = block(-k, 0)
            wait_for(b, r_z.at[0, k])
            h = b if k < 3 else b.at[pl.ds(0, 4)]
            go(remote(h, h, s_z.at[0, k + 1], r_z.at[0, k + 1], tile=up))
            x_first(-k)
            b = block(k, 0)
            wait_for(b, r_z.at[1, k])
            h = b if k < 3 else b.at[pl.ds(4, 4)]
            go(remote(h, h, s_z.at[1, k + 1], r_z.at[1, k + 1], tile=down))
            x_first(k)
        else:
            b = block(4, 0)
            wait_for(b.at[pl.ds(0, 4)], r_z.at[0, 4])
            wait_for(b.at[pl.ds(4, 4)], r_z.at[1, 4])
            x_first(4)

    send_tiles(0)

    for cp in sum_sends:
        cp.wait()
    mean = (sums[0] + sums[1] + sums[2] + sums[3]) / MEMBERS
    for j in range(FLUX_DEV):
        shard[j] = (prior[:, j * B : (j + 1) * B].astype(F32) - mean[j : j + 1, :]).astype(BF16)
    own_copy = pltpu.make_async_copy(shard, anoms.at[me], s_local)
    own_copy.start()
    go(remote(shard, anoms.at[me], s_z.at[0, 1], r_z.at[0, 1], tile=index(at_z(1), x, core)))
    go(remote(shard, anoms.at[me], s_z.at[1, 1], r_z.at[1, 1], tile=index(at_z(-1), x, core)))
    x_first(0, shard)

    send_tiles(1)
    send_tiles(7)
    y_first(0)
    z_step(1)
    send_tiles(2)
    send_tiles(6)
    x_second(0)
    y_first(1)
    y_first(7)
    z_step(2)
    send_tiles(3)
    send_tiles(5)
    y_second(0)
    x_second(-1)
    x_second(1)
    z_step(3)
    send_tiles(4)
    y_second(1)
    y_second(7)
    y_first(2)
    y_first(6)
    x_last(0)
    x_second(-2)
    x_second(2)
    z_step(4)
    y_first(3)
    y_first(5)
    y_second(2)
    y_second(6)
    x_last(-1)
    x_last(1)
    x_second(-3)
    x_second(3)
    y_first(4)
    y_second(3)
    y_second(5)
    x_last(-2)
    x_last(2)
    x_second(4)
    y_second(4)
    x_last(-3)
    x_last(3)
    x_last(4)
    for dz in (0, 1, 7, 2, 6, 3, 5, 4):
        y_last(dz)
    for oz in (0, 1, 7, 2, 6, 3, 5, 4):
        for ox in range(NX):
            wait_for(block(oz, ox, False), r_sib.at[ox, oz])
    wait_for(codes, r_code)
    own_copy.wait()
    for cp in pending:
        cp.wait_send()
    wait_for(staged.at[pl.ds(0, NT - 1)], s_tile)
    wait_for(codes.at[pl.ds(0, NT - 1)], s_code)


def spread(source, coded, footprints, prior):
    any_spec = pl.BlockSpec(memory_space=pl.ANY)
    vmem = pl.BlockSpec(memory_space=pltpu.VMEM)
    dma = pltpu.SemaphoreType.DMA
    return pl.pallas_call(
        spread_kernel,
        out_shape=(
            jax.ShapeDtypeStruct((NY, NT, CAP, 32, B), BF16),
            jax.ShapeDtypeStruct((NT, FLUX_DEV, LM, B), BF16),
            jax.ShapeDtypeStruct((NT, 1, B), jnp.int32),
        ),
        in_specs=[pl.BlockSpec(memory_space=pltpu.SMEM), vmem, any_spec, vmem],
        out_specs=(any_spec, any_spec, any_spec),
        scratch_shapes=[
            pltpu.VMEM((B, 32, B), BF16),
            pltpu.VMEM((NT, CAP, 32, B), BF16),
            pltpu.VMEM((NY, FLUX_DEV, B), F32),
            pltpu.VMEM((FLUX_DEV, LM, B), BF16),
            dma, dma((NY,)), dma((NY,)), dma, dma((NZ,)), dma, dma,
            dma((4, NZ)), dma((2, NZ)), dma((2, NZ)),
            dma, dma((2, 5)), dma((2, 5)), dma((4, NZ)), dma((2, NZ)), dma((2, NZ)),
            dma((NX, NZ)), dma((NX, NZ)),
        ],
        compiler_params=pltpu.CompilerParams(
            collective_id=0, has_side_effects=True, vmem_limit_bytes=16 * 2**20
        ),
        name="spread",
    )(source, coded, footprints, prior)


def local_kernel(
    codes, tiles_h, anoms_h, observed, weight, out_h,
    tiles, anoms, modelled, weighted, total, packed, s_tiles, s_anoms, s_out,
):
    anoms_in = pltpu.make_async_copy(anoms_h, anoms, s_anoms)
    anoms_in.start()
    tiles_in = pltpu.make_async_copy(tiles_h, tiles, s_tiles)
    tiles_in.start()
    modelled[...] = jnp.zeros_like(modelled)

    @pl.loop(0, 64)
    def _(i):
        total[pl.ds(i * 8, 8)] = jnp.zeros((8, LM, B), F32)

    anoms_in.wait()
    tiles_in.wait()
    step = 2

    def fetch(i, o, s):
        src = i * step + o
        code = codes[src, 0, s]
        return tiles[:, src, s].reshape(B, B), code // 512, lax.rem(code, 512)

    @pl.loop(0, NT // step)
    def _(i):
        terms = []
        for o in range(step):
            for s in range(CAP):
                tile, row, col = fetch(i, o, s)
                term = lax.dot_general(
                    anoms[col], tile, (((1,), (1,)), ((), ())), preferred_element_type=F32
                )
                terms.append((row, term))
        for row, term in terms:
            modelled[row] += term

    for r in range(SOUND_DEV):
        factor = weight[r].astype(F32) / 8.0
        gap = modelled[r] - observed[:, r * B : (r + 1) * B]
        weighted[r] = (factor * gap).astype(BF16)
    weighted[SOUND_DEV] = jnp.zeros((LM, B), BF16)

    @pl.loop(0, NT // step)
    def _(i):
        terms = []
        for o in range(step):
            for s in range(CAP):
                tile, row, col = fetch(i, o, s)
                term = lax.dot_general(
                    weighted[row], tile, (((1,), (0,)), ((), ())), preferred_element_type=F32
                )
                terms.append((col, term))
        for col, term in terms:
            total[col] += term

    @pl.loop(0, 8)
    def _(i):
        @pl.loop(0, 8)
        def _(j):
            packed[pl.ds((i * 8 + j) * 8, 8)] = total[pl.ds((i * 8 + j) * 8, 8)].astype(BF16)

        pltpu.make_async_copy(
            packed.at[pl.ds(i * 64, 64)], out_h.at[pl.ds(i * 64, 64)], s_out
        ).start()

    pltpu.make_async_copy(packed, out_h, s_out).wait()


def local(codes, tiles, anoms, observed, weight):
    any_spec = pl.BlockSpec(memory_space=pl.ANY)
    vmem = pl.BlockSpec(memory_space=pltpu.VMEM)
    dma = pltpu.SemaphoreType.DMA
    return pl.pallas_call(
        local_kernel,
        out_shape=jax.ShapeDtypeStruct((NT * FLUX_DEV, LM, B), BF16),
        in_specs=[pl.BlockSpec(memory_space=pltpu.SMEM), any_spec, any_spec, vmem, vmem],
        out_specs=any_spec,
        scratch_shapes=[
            pltpu.VMEM((NY, NT, CAP, 32, B), BF16),
            pltpu.VMEM((NT * FLUX_DEV, LM, B), BF16),
            pltpu.VMEM((SOUND_DEV + 1, LM, B), F32),
            pltpu.VMEM((SOUND_DEV + 1, LM, B), BF16),
            pltpu.VMEM((NT * FLUX_DEV, LM, B), F32),
            pltpu.VMEM((NT * FLUX_DEV, LM, B), BF16),
            dma, dma, dma,
        ],
        compiler_params=pltpu.CompilerParams(vmem_limit_bytes=50 * 2**20),
        name="local",
    )(codes, tiles, anoms.reshape(NT * FLUX_DEV, LM, B), observed, weight)


def gather_kernel(
    part, out,
    pa, pb, ra, rb, xa1, xa2, zb1, zb2, za1, za2, xb1, xb2,
    s_own_a, s_own_b, s_sib_a, r_sib_a, s_sib_b, r_sib_b,
    s_xa, r_xa, s_zb, r_zb, s_za, r_za, s_xb, r_xb,
):
    me = lax.axis_index("tile")
    q = lax.axis_index("mem")
    core = lax.rem(me, 2)
    x = lax.rem(me // 2, NX)
    z = me // 8

    def at_z(o):
        return lax.rem(z + o + NZ, NZ)

    def at_x(o):
        return lax.rem(x + o + NX, NX)

    def index(zz, xx, cc):
        return zz * 8 + xx * 2 + cc

    sibling = index(z, x, 1 - core)
    x_next = (index(z, at_x(1), core), index(z, at_x(-1), core))
    z_next = (index(at_z(1), x, core), index(at_z(-1), x, core))

    pending = []

    def send(src, dst, ssem, rsem, tile):
        cp = pltpu.make_async_remote_copy(
            src_ref=src, dst_ref=dst, send_sem=ssem, recv_sem=rsem,
            device_id={"tile": tile, "mem": q}, device_id_type=MESH,
        )
        cp.start()
        pending.append(cp)

    def wait_for(ref, sem):
        pltpu.make_async_copy(ref, ref, sem).wait()

    def own(kind, d):
        if kind == "a":
            return part.at[:, at_x(d), core, pl.ds(0, 4)], pa.at[d], s_own_a.at[d]
        return part.at[at_z(d), :, core, pl.ds(4, 4)], pb.at[d], s_own_b.at[d]

    order = [("a", 2), ("b", 4), ("b", 3), ("b", 5), ("a", 1), ("a", 3),
             ("b", 2), ("b", 6), ("b", 1), ("b", 7), ("b", 0), ("a", 0)]
    for kind, d in order:
        pltpu.make_async_copy(*own(kind, d)).start()

    barrier = pltpu.get_barrier_semaphore()
    for t in (sibling, *x_next, *z_next):
        pl.semaphore_signal(barrier, inc=1, device_id={"tile": t, "mem": q}, device_id_type=MESH)
    pl.semaphore_wait(barrier, 5)

    for kind, d in order:
        if kind == "a":
            send(part.at[:, at_x(d), 1 - core, pl.ds(0, 4)], ra.at[d], s_sib_a.at[d], r_sib_a.at[d], sibling)
        else:
            send(part.at[at_z(d), :, 1 - core, pl.ds(4, 4)], rb.at[d], s_sib_b.at[d], r_sib_b.at[d], sibling)

    def add(dst, *srcs):
        @pl.loop(0, dst.shape[0])
        def _(i):
            for b in range(dst.shape[1]):
                value = dst[i, b].astype(F32)
                for s in srcs:
                    value = value + s[i, b].astype(F32)
                dst[i, b] = value.astype(BF16)

    def settle(kind, d):
        pltpu.make_async_copy(*own(kind, d)).wait()
        if kind == "a":
            wait_for(ra.at[d], r_sib_a.at[d])
        else:
            wait_for(rb.at[d], r_sib_b.at[d])

    def pair(kind, d):
        settle(kind, d)
        if kind == "a":
            add(pa.at[d], ra.at[d])
        else:
            add(pb.at[d], rb.at[d])

    pair("a", 2)
    for i in range(2):
        send(pa.at[2, pl.ds(4 * i, 4)], xa1.at[i], s_xa.at[i, 0], r_xa.at[i, 0], x_next[i])
    pair("b", 4)
    for i in range(2):
        send(pb.at[4, pl.ds(2 * i, 2)], zb1.at[i], s_zb.at[i, 0], r_zb.at[i, 0], z_next[i])
    pair("b", 3)
    pair("b", 5)
    for i, d in enumerate((3, 5)):
        wait_for(zb1.at[i], r_zb.at[i, 0])
        add(pb.at[d, pl.ds(2 * i, 2)], zb1.at[i])
        send(pb.at[d], zb2.at[i, 0], s_zb.at[i, 1], r_zb.at[i, 1], z_next[i])
    pair("a", 1)
    pair("a", 3)
    for i, d in enumerate((1, 3)):
        wait_for(xa1.at[i], r_xa.at[i, 0])
        add(pa.at[d, pl.ds(4 * i, 4)], xa1.at[i])
        send(pa.at[d], xa2.at[i], s_xa.at[i, 1], r_xa.at[i, 1], x_next[i])
    for step in (1, 2):
        pair("b", 3 - step)
        pair("b", 5 + step)
        for i, d in enumerate((3 - step, 5 + step)):
            wait_for(zb2.at[i, step - 1], r_zb.at[i, step])
            add(pb.at[d], zb2.at[i, step - 1])
            send(pb.at[d], zb2.at[i, step], s_zb.at[i, step + 1], r_zb.at[i, step + 1], z_next[i])

    settle("a", 0)
    for i in range(2):
        wait_for(xa2.at[i], r_xa.at[i, 1])
    add(pa.at[0], ra.at[0], xa2.at[0], xa2.at[1])
    for i in range(2):
        send(pa.at[0, at_z(4), pl.ds(2 * i, 2)], za1.at[i], s_za.at[i, 0], r_za.at[i, 0], z_next[i])

    def add3(dst, src):
        for b in range(dst.shape[0]):
            dst[b] = (dst[b].astype(F32) + src[b].astype(F32)).astype(BF16)

    for i, d in enumerate((3, 5)):
        wait_for(za1.at[i], r_za.at[i, 0])
        add3(pa.at[0, at_z(d), pl.ds(2 * i, 2)], za1.at[i])
        send(pa.at[0, at_z(d)], za2.at[i, 0], s_za.at[i, 1], r_za.at[i, 1], z_next[i])

    settle("b", 0)
    for i in range(2):
        wait_for(zb2.at[i, 2], r_zb.at[i, 3])
    add(pb.at[0], rb.at[0], zb2.at[0, 2], zb2.at[1, 2])
    for i in range(2):
        send(pb.at[0, at_x(2), pl.ds(2 * i, 2)], xb1.at[i], s_xb.at[i, 0], r_xb.at[i, 0], x_next[i])

    for i, d in enumerate((2, 6)):
        wait_for(za2.at[i, 0], r_za.at[i, 1])
        add3(pa.at[0, at_z(d)], za2.at[i, 0])
        send(pa.at[0, at_z(d)], za2.at[i, 1], s_za.at[i, 2], r_za.at[i, 2], z_next[i])
    for i, d in enumerate((1, 3)):
        wait_for(xb1.at[i], r_xb.at[i, 0])
        add3(pb.at[0, at_x(d), pl.ds(2 * i, 2)], xb1.at[i])
        send(pb.at[0, at_x(d)], xb2.at[i], s_xb.at[i, 1], r_xb.at[i, 1], x_next[i])
    for i, d in enumerate((1, 7)):
        wait_for(za2.at[i, 1], r_za.at[i, 2])
        add3(pa.at[0, at_z(d)], za2.at[i, 1])
        send(pa.at[0, at_z(d)], za2.at[i, 2], s_za.at[i, 3], r_za.at[i, 3], z_next[i])

    for i in range(2):
        wait_for(xb2.at[i], r_xb.at[i, 1])
    for b in range(4):
        out[:, (4 + b) * B : (5 + b) * B] = (
            pb[0, x, b].astype(F32) + xb2[0, b].astype(F32) + xb2[1, b].astype(F32)
        )
    for i in range(2):
        wait_for(za2.at[i, 2], r_za.at[i, 3])
    for b in range(4):
        out[:, b * B : (b + 1) * B] = (
            pa[0, z, b].astype(F32) + za2[0, 2, b].astype(F32) + za2[1, 2, b].astype(F32)
        )
    for cp in pending:
        cp.wait_send()


def gather(part):
    any_spec = pl.BlockSpec(memory_space=pl.ANY)
    vmem = pl.BlockSpec(memory_space=pltpu.VMEM)
    dma = pltpu.SemaphoreType.DMA
    return pl.pallas_call(
        gather_kernel,
        out_shape=jax.ShapeDtypeStruct((LM, FLUX_DEV * B), F32),
        in_specs=[any_spec],
        out_specs=vmem,
        scratch_shapes=[
            pltpu.VMEM((NX, NZ, 4, LM, B), BF16),
            pltpu.VMEM((NZ, NX, 4, LM, B), BF16),
            pltpu.VMEM((NX, NZ, 4, LM, B), BF16),
            pltpu.VMEM((NZ, NX, 4, LM, B), BF16),
            pltpu.VMEM((2, 4, 4, LM, B), BF16),
            pltpu.VMEM((2, NZ, 4, LM, B), BF16),
            pltpu.VMEM((2, 2, 4, LM, B), BF16),
            pltpu.VMEM((2, 3, NX, 4, LM, B), BF16),
            pltpu.VMEM((2, 2, LM, B), BF16),
            pltpu.VMEM((2, 3, 4, LM, B), BF16),
            pltpu.VMEM((2, 2, LM, B), BF16),
            pltpu.VMEM((2, 4, LM, B), BF16),
            dma((NX,)), dma((NZ,)), dma((NX,)), dma((NX,)), dma((NZ,)), dma((NZ,)),
            dma((2, 2)), dma((2, 2)), dma((2, 4)), dma((2, 4)),
            dma((2, 4)), dma((2, 4)), dma((2, 2)), dma((2, 2)),
        ],
        compiler_params=pltpu.CompilerParams(
            collective_id=1, has_side_effects=True, vmem_limit_bytes=40 * 2**20
        ),
        name="gather",
    )(part.reshape(NZ, NX, 2, FLUX_DEV, LM, B))


def body(footprints, tile_row, tile_col, prior_flux, observed, precision_weight):
    source, coded = route(tile_row, tile_col)
    tiles, anoms, codes = spread(source, coded, footprints, prior_flux)
    weight = precision_weight.reshape(SOUND_DEV, 1, B)
    part = local(codes, tiles, anoms, observed, weight)
    return gather(part)


def solution(mesh):
    in_specs = (
        P("tile", None, None),
        P("tile"),
        P("tile"),
        P("mem", "tile"),
        P("mem", "tile"),
        P("tile"),
    )
    out_specs = P("mem", "tile")
    return jax.shard_map(body, mesh=mesh, in_specs=in_specs, out_specs=out_specs, check_vma=False)
```

```python
import functools

import jax
import jax.numpy as jnp
from jax import lax
from jax.experimental import pallas as pl
from jax.experimental.pallas import tpu as pltpu
from jax.sharding import PartitionSpec as P

MEMBERS = 256
FLUX_DEV = 8
SOUND_DEV = 16
NZ, NX, NY, NT = 8, 4, 4, 64
CAP = 3
B = 128
LM = 64
MESH = pl.DeviceIdType.MESH
F32, BF16 = jnp.float32, jnp.bfloat16


def route(tile_row, tile_col):
    count = tile_row.shape[0]
    owner = tile_row // SOUND_DEV
    position = jnp.arange(count)
    earlier = (owner[:, None] == owner[None, :]) & (position[None, :] < position[:, None])
    slot = owner * CAP + jnp.sum(earlier.astype(jnp.int32), axis=1)
    match = slot[None, :] == jnp.arange(NT * CAP)[:, None]
    source = jnp.sum(jnp.where(match, position[None, :], 0), axis=1)
    blocks = (tile_row % SOUND_DEV) * 512 + tile_col
    coded = jnp.sum(jnp.where(match, blocks[None, :] + 1, 0), axis=1)
    coded = jnp.where(coded == 0, SOUND_DEV * 512, coded - 1)
    coded = jnp.pad(coded.reshape(NT, CAP), ((0, 0), (0, B - CAP))).reshape(NT, 1, B)
    return source, coded


def spread_kernel(
    source, coded, footprints, prior_h, tiles, anoms, codes,
    prior, quarter, staged, sums, shard,
    s_fp, s_prior, s_sum, r_sum, s_tile, r_tile, s_code, r_code, s_y, r_y, r_y2,
    s_local, s_z, r_z, s_x, r_x, r_x2, s_sib, r_sib,
):
    me = lax.axis_index("tile")
    q = lax.axis_index("mem")
    core = lax.rem(me, 2)
    x = lax.rem(me // 2, NX)
    z = me // 8

    def at_z(o):
        return lax.rem(z + o + NZ, NZ)

    def at_x(o):
        return lax.rem(x + o + NX, NX)

    def at_y(o):
        return lax.rem(q + o + NY, NY)

    def index(zz, xx, cc):
        return zz * 8 + xx * 2 + cc

    def remote(src, dst, ssem, rsem, tile=None, mem=None):
        return pltpu.make_async_remote_copy(
            src_ref=src, dst_ref=dst, send_sem=ssem, recv_sem=rsem,
            device_id={"tile": me if tile is None else tile, "mem": q if mem is None else mem},
            device_id_type=MESH,
        )

    def wait_for(ref, sem):
        pltpu.make_async_copy(ref, ref, sem).wait()

    prior_copy = pltpu.make_async_copy(prior_h, prior, s_prior)
    prior_copy.start()
    fp_copy = pltpu.make_async_copy(
        footprints.at[:, pl.ds(pl.multiple_of(q * 32, 32), 32), :], quarter, s_fp
    )
    fp_copy.start()

    barrier = pltpu.get_barrier_semaphore()

    @pl.loop(1, NT)
    def _(o):
        pl.semaphore_signal(
            barrier, inc=1, device_id={"tile": lax.rem(me + o, NT), "mem": q}, device_id_type=MESH
        )

    for o in range(1, NY):
        pl.semaphore_signal(
            barrier, inc=1, device_id={"tile": me, "mem": at_y(o)}, device_id_type=MESH
        )

    prior_copy.wait()
    for j in range(FLUX_DEV):
        part = jnp.sum(prior[:, j * B : (j + 1) * B].astype(F32), axis=0, keepdims=True)
        sums[0, j : j + 1, :] = part
    pl.semaphore_wait(barrier, NT - 1 + NY - 1)

    sum_sends = []
    for o in range(1, NY):
        cp = remote(sums.at[0], sums.at[o], s_sum.at[o], r_sum.at[o], mem=at_y(o))
        cp.start()
        sum_sends.append(cp)
    fp_copy.wait()

    def send_tiles(dz):
        first = 1 if dz == 0 else 0

        @pl.loop(first, 8)
        def _(o):
            t = at_z(dz) * 8 + lax.rem(me + o, 8)
            for s in range(CAP):
                staged[t, s] = quarter[source[t * CAP + s]]
            remote(staged.at[t], tiles.at[q, me], s_tile, r_tile.at[dz], tile=t).start()
            remote(coded.at[t], codes.at[me], s_code, r_code, tile=t).start()

        if dz == 0:
            for s in range(CAP):
                staged[me, s] = quarter[source[me * CAP + s]]
            pltpu.make_async_copy(staged.at[me], tiles.at[q, me], r_tile.at[0]).start()
            pltpu.make_async_copy(coded.at[me], codes.at[me], r_code).start()

    def group(quarter_index, dz, first=0, size=8):
        zs = at_z(-dz)
        return tiles.at[quarter_index, pl.ds(zs * 8 + first, size)]

    pending = []

    def go(cp):
        cp.start()
        pending.append(cp)

    def y_first(dz):
        wait_for(group(q, dz), r_tile.at[dz])
        go(remote(group(q, dz), group(q, dz), s_y.at[0, dz], r_y.at[0, dz], mem=at_y(1)))
        go(remote(group(q, dz), group(q, dz), s_y.at[1, dz], r_y.at[1, dz], mem=at_y(-1)))

    def y_second(dz):
        back = group(at_y(-1), dz)
        wait_for(back, r_y.at[0, dz])
        part = group(at_y(-1), dz, 0, 4)
        go(remote(part, part, s_y.at[2, dz], r_y2.at[0, dz], mem=at_y(1)))
        fore = group(at_y(1), dz)
        wait_for(fore, r_y.at[1, dz])
        part = group(at_y(1), dz, 4, 4)
        go(remote(part, part, s_y.at[3, dz], r_y2.at[1, dz], mem=at_y(-1)))

    def y_last(dz):
        wait_for(group(at_y(2), dz, 0, 4), r_y2.at[0, dz])
        wait_for(group(at_y(2), dz, 4, 4), r_y2.at[1, dz])

    def block(oz, ox, own_core=True):
        return anoms.at[index(at_z(oz), at_x(ox), core if own_core else 1 - core)]

    def to_sibling(oz, ox):
        go(
            remote(
                block(oz, ox), block(oz, ox), s_sib.at[ox % NX, oz % NZ], r_sib.at[ox % NX, oz % NZ],
                tile=index(z, x, 1 - core),
            )
        )

    def x_first(oz, src=None):
        b = block(oz, 0)
        src = b if src is None else src
        k = oz % NZ
        go(remote(src, b, s_x.at[0, k], r_x.at[0, k], tile=index(z, at_x(1), core)))
        go(remote(src, b, s_x.at[1, k], r_x.at[1, k], tile=index(z, at_x(-1), core)))
        go(remote(src, b, s_sib.at[0, k], r_sib.at[0, k], tile=index(z, x, 1 - core)))

    def x_second(oz):
        k = oz % NZ
        b = block(oz, -1)
        wait_for(b, r_x.at[0, k])
        h = b.at[pl.ds(0, 4)]
        go(remote(h, h, s_x.at[2, k], r_x2.at[0, k], tile=index(z, at_x(1), core)))
        to_sibling(oz, -1)
        b = block(oz, 1)
        wait_for(b, r_x.at[1, k])
        h = b.at[pl.ds(4, 4)]
        go(remote(h, h, s_x.at[3, k], r_x2.at[1, k], tile=index(z, at_x(-1), core)))
        to_sibling(oz, 1)

    def x_last(oz):
        k = oz % NZ
        b = block(oz, 2)
        wait_for(b.at[pl.ds(0, 4)], r_x2.at[0, k])
        wait_for(b.at[pl.ds(4, 4)], r_x2.at[1, k])
        to_sibling(oz, 2)

    def z_step(k):
        up, down = index(at_z(1), x, core), index(at_z(-1), x, core)
        if k < 4:
            b = block(-k, 0)
            wait_for(b, r_z.at[0, k])
            h = b if k < 3 else b.at[pl.ds(0, 4)]
            go(remote(h, h, s_z.at[0, k + 1], r_z.at[0, k + 1], tile=up))
            x_first(-k)
            b = block(k, 0)
            wait_for(b, r_z.at[1, k])
            h = b if k < 3 else b.at[pl.ds(4, 4)]
            go(remote(h, h, s_z.at[1, k + 1], r_z.at[1, k + 1], tile=down))
            x_first(k)
        else:
            b = block(4, 0)
            wait_for(b.at[pl.ds(0, 4)], r_z.at[0, 4])
            wait_for(b.at[pl.ds(4, 4)], r_z.at[1, 4])
            x_first(4)

    send_tiles(0)

    for cp in sum_sends:
        cp.wait()
    mean = (sums[0] + sums[1] + sums[2] + sums[3]) / MEMBERS
    for j in range(FLUX_DEV):
        shard[j] = (prior[:, j * B : (j + 1) * B].astype(F32) - mean[j : j + 1, :]).astype(BF16)
    own_copy = pltpu.make_async_copy(shard, anoms.at[me], s_local)
    own_copy.start()
    go(remote(shard, anoms.at[me], s_z.at[0, 1], r_z.at[0, 1], tile=index(at_z(1), x, core)))
    go(remote(shard, anoms.at[me], s_z.at[1, 1], r_z.at[1, 1], tile=index(at_z(-1), x, core)))
    x_first(0, shard)

    send_tiles(1)
    send_tiles(7)
    y_first(0)
    z_step(1)
    send_tiles(2)
    send_tiles(6)
    x_second(0)
    y_first(1)
    y_first(7)
    z_step(2)
    send_tiles(3)
    send_tiles(5)
    y_second(0)
    x_second(-1)
    x_second(1)
    z_step(3)
    send_tiles(4)
    y_second(1)
    y_second(7)
    y_first(2)
    y_first(6)
    x_last(0)
    x_second(-2)
    x_second(2)
    z_step(4)
    y_first(3)
    y_first(5)
    y_second(2)
    y_second(6)
    x_last(-1)
    x_last(1)
    x_second(-3)
    x_second(3)
    y_first(4)
    y_second(3)
    y_second(5)
    x_last(-2)
    x_last(2)
    x_second(4)
    y_second(4)
    x_last(-3)
    x_last(3)
    x_last(4)
    for dz in (0, 1, 7, 2, 6, 3, 5, 4):
        y_last(dz)
    for oz in (0, 1, 7, 2, 6, 3, 5, 4):
        for ox in range(NX):
            wait_for(block(oz, ox, False), r_sib.at[ox, oz])
    wait_for(codes, r_code)
    own_copy.wait()
    for cp in pending:
        cp.wait_send()
    wait_for(staged.at[pl.ds(0, NT - 1)], s_tile)
    wait_for(codes.at[pl.ds(0, NT - 1)], s_code)


def spread(source, coded, footprints, prior):
    hbm = pl.BlockSpec(memory_space=pltpu.HBM)
    vmem = pl.BlockSpec(memory_space=pltpu.VMEM)
    dma = pltpu.SemaphoreType.DMA
    return pl.pallas_call(
        spread_kernel,
        out_shape=(
            jax.ShapeDtypeStruct((NY, NT, CAP, 32, B), BF16),
            jax.ShapeDtypeStruct((NT, FLUX_DEV, LM, B), BF16),
            jax.ShapeDtypeStruct((NT, 1, B), jnp.int32),
        ),
        in_specs=[pl.BlockSpec(memory_space=pltpu.SMEM), vmem, hbm, hbm],
        out_specs=(vmem, vmem, vmem),
        scratch_shapes=[
            pltpu.VMEM((LM, FLUX_DEV * B), BF16),
            pltpu.VMEM((B, 32, B), BF16),
            pltpu.VMEM((NT, CAP, 32, B), BF16),
            pltpu.VMEM((NY, FLUX_DEV, B), F32),
            pltpu.VMEM((FLUX_DEV, LM, B), BF16),
            dma, dma, dma((NY,)), dma((NY,)), dma, dma((NZ,)), dma, dma,
            dma((4, NZ)), dma((2, NZ)), dma((2, NZ)),
            dma, dma((2, 5)), dma((2, 5)), dma((4, NZ)), dma((2, NZ)), dma((2, NZ)),
            dma((NX, NZ)), dma((NX, NZ)),
        ],
        compiler_params=pltpu.CompilerParams(
            collective_id=0, has_side_effects=True, vmem_limit_bytes=16 * 2**20
        ),
        name="spread",
    )(source, coded, footprints, prior)


def local_kernel(
    codes, tiles, anoms, observed_h, weight_h, out,
    observed, weight, modelled, weighted, total, s_obs, s_weight,
):
    observed_in = pltpu.make_async_copy(observed_h, observed, s_obs)
    observed_in.start()
    weight_in = pltpu.make_async_copy(weight_h, weight, s_weight)
    weight_in.start()
    modelled[...] = jnp.zeros_like(modelled)
    step = 2

    def fetch(i, o, s):
        src = i * step + o
        code = codes[src, 0, s]
        return tiles[:, src, s].reshape(B, B), code // 512, lax.rem(code, 512)

    @pl.loop(0, NT // step)
    def _(i):
        terms = []
        for o in range(step):
            for s in range(CAP):
                tile, row, col = fetch(i, o, s)
                term = lax.dot_general(
                    anoms[col], tile, (((1,), (1,)), ((), ())), preferred_element_type=F32
                )
                terms.append((row, term))
        total[pl.ds(i * 16, 16)] = jnp.zeros((16, LM, B), F32)
        for row, term in terms:
            modelled[row] += term

    observed_in.wait()
    weight_in.wait()
    for r in range(SOUND_DEV):
        factor = weight[r].astype(F32) / 8.0
        gap = modelled[r] - observed[:, r * B : (r + 1) * B]
        weighted[r] = (factor * gap).astype(BF16)
    weighted[SOUND_DEV] = jnp.zeros((LM, B), BF16)

    @pl.loop(0, NT // step)
    def _(i):
        terms = []
        for o in range(step):
            for s in range(CAP):
                tile, row, col = fetch(i, o, s)
                term = lax.dot_general(
                    weighted[row], tile, (((1,), (0,)), ((), ())), preferred_element_type=F32
                )
                terms.append((col, term))
        for col, term in terms:
            total[col] += term

    @pl.loop(0, NT)
    def _(i):
        out[pl.ds(i * 8, 8)] = total[pl.ds(i * 8, 8)].astype(BF16)


def local(codes, tiles, anoms, observed, weight):
    hbm = pl.BlockSpec(memory_space=pltpu.HBM)
    vmem = pl.BlockSpec(memory_space=pltpu.VMEM)
    dma = pltpu.SemaphoreType.DMA
    return pl.pallas_call(
        local_kernel,
        out_shape=jax.ShapeDtypeStruct((NT * FLUX_DEV, LM, B), BF16),
        in_specs=[pl.BlockSpec(memory_space=pltpu.SMEM), vmem, vmem, hbm, hbm],
        out_specs=vmem,
        scratch_shapes=[
            pltpu.VMEM((LM, SOUND_DEV * B), F32),
            pltpu.VMEM((SOUND_DEV, 1, B), jnp.int32),
            pltpu.VMEM((SOUND_DEV + 1, LM, B), F32),
            pltpu.VMEM((SOUND_DEV + 1, LM, B), BF16),
            pltpu.VMEM((NT * FLUX_DEV, LM, B), F32),
            dma, dma,
        ],
        compiler_params=pltpu.CompilerParams(vmem_limit_bytes=22 * 2**20),
        name="local",
    )(codes, tiles, anoms.reshape(NT * FLUX_DEV, LM, B), observed, weight)


def gather_kernel(
    part, out,
    pa, pb, ra, rb, xa1, xa2, zb1, zb2, za1, za2, xb1, xb2,
    s_sib_a, r_sib_a, s_sib_b, r_sib_b,
    s_xa, r_xa, s_zb, r_zb, s_za, r_za, s_xb, r_xb,
):
    me = lax.axis_index("tile")
    q = lax.axis_index("mem")
    core = lax.rem(me, 2)
    x = lax.rem(me // 2, NX)
    z = me // 8

    def at_z(o):
        return lax.rem(z + o + NZ, NZ)

    def at_x(o):
        return lax.rem(x + o + NX, NX)

    def index(zz, xx, cc):
        return zz * 8 + xx * 2 + cc

    sibling = index(z, x, 1 - core)
    x_next = (index(z, at_x(1), core), index(z, at_x(-1), core))
    z_next = (index(at_z(1), x, core), index(at_z(-1), x, core))

    pending = []

    def send(src, dst, ssem, rsem, tile):
        cp = pltpu.make_async_remote_copy(
            src_ref=src, dst_ref=dst, send_sem=ssem, recv_sem=rsem,
            device_id={"tile": tile, "mem": q}, device_id_type=MESH,
        )
        cp.start()
        pending.append(cp)

    def wait_for(ref, sem):
        pltpu.make_async_copy(ref, ref, sem).wait()

    order = [("a", 2), ("b", 4), ("b", 3), ("b", 5), ("a", 1), ("a", 3),
             ("b", 2), ("b", 6), ("b", 1), ("b", 7), ("b", 0), ("a", 0)]
    barrier = pltpu.get_barrier_semaphore()
    for t in (sibling, *x_next, *z_next):
        pl.semaphore_signal(barrier, inc=1, device_id={"tile": t, "mem": q}, device_id_type=MESH)
    pl.semaphore_wait(barrier, 5)

    for kind, d in order:
        if kind == "a":
            send(part.at[:, at_x(d), 1 - core, pl.ds(0, 4)], ra.at[d], s_sib_a.at[d], r_sib_a.at[d], sibling)
        else:
            send(part.at[at_z(d), :, 1 - core, pl.ds(4, 4)], rb.at[d], s_sib_b.at[d], r_sib_b.at[d], sibling)

    def total(first, *rest):
        value = first.astype(F32)
        for r in rest:
            value = value + r.astype(F32)
        return value.astype(BF16)

    def add(dst, src):
        @pl.loop(0, dst.shape[0])
        def _(i):
            for b in range(dst.shape[1]):
                dst[i, b] = total(dst[i, b], src[i, b])

    def pair(kind, d, *more):
        if kind == "a":
            wait_for(ra.at[d], r_sib_a.at[d])

            @pl.loop(0, NZ)
            def _(i):
                for b in range(4):
                    pa[d, i, b] = total(part[i, at_x(d), core, b], ra[d, i, b], *(m[i, b] for m in more))
        else:
            wait_for(rb.at[d], r_sib_b.at[d])

            @pl.loop(0, NX)
            def _(i):
                for b in range(4):
                    pb[d, i, b] = total(part[at_z(d), i, core, 4 + b], rb[d, i, b], *(m[i, b] for m in more))

    pair("a", 2)
    for i in range(2):
        send(pa.at[2, pl.ds(4 * i, 4)], xa1.at[i], s_xa.at[i, 0], r_xa.at[i, 0], x_next[i])
    pair("b", 4)
    for i in range(2):
        send(pb.at[4, pl.ds(2 * i, 2)], zb1.at[i], s_zb.at[i, 0], r_zb.at[i, 0], z_next[i])
    pair("b", 3)
    pair("b", 5)
    for i, d in enumerate((3, 5)):
        wait_for(zb1.at[i], r_zb.at[i, 0])
        add(pb.at[d, pl.ds(2 * i, 2)], zb1.at[i])
        send(pb.at[d], zb2.at[i, 0], s_zb.at[i, 1], r_zb.at[i, 1], z_next[i])
    pair("a", 1)
    pair("a", 3)
    for i, d in enumerate((1, 3)):
        wait_for(xa1.at[i], r_xa.at[i, 0])
        add(pa.at[d, pl.ds(4 * i, 4)], xa1.at[i])
        send(pa.at[d], xa2.at[i], s_xa.at[i, 1], r_xa.at[i, 1], x_next[i])
    for step in (1, 2):
        pair("b", 3 - step)
        pair("b", 5 + step)
        for i, d in enumerate((3 - step, 5 + step)):
            wait_for(zb2.at[i, step - 1], r_zb.at[i, step])
            add(pb.at[d], zb2.at[i, step - 1])
            send(pb.at[d], zb2.at[i, step], s_zb.at[i, step + 1], r_zb.at[i, step + 1], z_next[i])

    for i in range(2):
        wait_for(xa2.at[i], r_xa.at[i, 1])
    pair("a", 0, xa2.at[0], xa2.at[1])
    for i in range(2):
        send(pa.at[0, at_z(4), pl.ds(2 * i, 2)], za1.at[i], s_za.at[i, 0], r_za.at[i, 0], z_next[i])

    def add3(dst, src):
        for b in range(dst.shape[0]):
            dst[b] = (dst[b].astype(F32) + src[b].astype(F32)).astype(BF16)

    for i, d in enumerate((3, 5)):
        wait_for(za1.at[i], r_za.at[i, 0])
        add3(pa.at[0, at_z(d), pl.ds(2 * i, 2)], za1.at[i])
        send(pa.at[0, at_z(d)], za2.at[i, 0], s_za.at[i, 1], r_za.at[i, 1], z_next[i])

    for i in range(2):
        wait_for(zb2.at[i, 2], r_zb.at[i, 3])
    pair("b", 0, zb2.at[0, 2], zb2.at[1, 2])
    for i in range(2):
        send(pb.at[0, at_x(2), pl.ds(2 * i, 2)], xb1.at[i], s_xb.at[i, 0], r_xb.at[i, 0], x_next[i])

    for i, d in enumerate((2, 6)):
        wait_for(za2.at[i, 0], r_za.at[i, 1])
        add3(pa.at[0, at_z(d)], za2.at[i, 0])
        send(pa.at[0, at_z(d)], za2.at[i, 1], s_za.at[i, 2], r_za.at[i, 2], z_next[i])
    for i, d in enumerate((1, 3)):
        wait_for(xb1.at[i], r_xb.at[i, 0])
        add3(pb.at[0, at_x(d), pl.ds(2 * i, 2)], xb1.at[i])
        send(pb.at[0, at_x(d)], xb2.at[i], s_xb.at[i, 1], r_xb.at[i, 1], x_next[i])
    for i, d in enumerate((1, 7)):
        wait_for(za2.at[i, 1], r_za.at[i, 2])
        add3(pa.at[0, at_z(d)], za2.at[i, 1])
        send(pa.at[0, at_z(d)], za2.at[i, 2], s_za.at[i, 3], r_za.at[i, 3], z_next[i])

    for i in range(2):
        wait_for(xb2.at[i], r_xb.at[i, 1])
    for b in range(4):
        out[:, (4 + b) * B : (5 + b) * B] = (
            pb[0, x, b].astype(F32) + xb2[0, b].astype(F32) + xb2[1, b].astype(F32)
        )
    for i in range(2):
        wait_for(za2.at[i, 2], r_za.at[i, 3])
    for b in range(4):
        out[:, b * B : (b + 1) * B] = (
            pa[0, z, b].astype(F32) + za2[0, 2, b].astype(F32) + za2[1, 2, b].astype(F32)
        )
    for cp in pending:
        cp.wait_send()


def gather(part):
    vmem = pl.BlockSpec(memory_space=pltpu.VMEM)
    dma = pltpu.SemaphoreType.DMA
    return pl.pallas_call(
        gather_kernel,
        out_shape=jax.ShapeDtypeStruct((LM, FLUX_DEV * B), F32),
        in_specs=[vmem],
        out_specs=vmem,
        scratch_shapes=[
            pltpu.VMEM((NX, NZ, 4, LM, B), BF16),
            pltpu.VMEM((NZ, NX, 4, LM, B), BF16),
            pltpu.VMEM((NX, NZ, 4, LM, B), BF16),
            pltpu.VMEM((NZ, NX, 4, LM, B), BF16),
            pltpu.VMEM((2, 4, 4, LM, B), BF16),
            pltpu.VMEM((2, NZ, 4, LM, B), BF16),
            pltpu.VMEM((2, 2, 4, LM, B), BF16),
            pltpu.VMEM((2, 3, NX, 4, LM, B), BF16),
            pltpu.VMEM((2, 2, LM, B), BF16),
            pltpu.VMEM((2, 3, 4, LM, B), BF16),
            pltpu.VMEM((2, 2, LM, B), BF16),
            pltpu.VMEM((2, 4, LM, B), BF16),
            dma((NX,)), dma((NX,)), dma((NZ,)), dma((NZ,)),
            dma((2, 2)), dma((2, 2)), dma((2, 4)), dma((2, 4)),
            dma((2, 4)), dma((2, 4)), dma((2, 2)), dma((2, 2)),
        ],
        compiler_params=pltpu.CompilerParams(
            collective_id=1, has_side_effects=True, vmem_limit_bytes=18 * 2**20
        ),
        name="gather",
    )(part.reshape(NZ, NX, 2, FLUX_DEV, LM, B))


def body(footprints, tile_row, tile_col, prior_flux, observed, precision_weight):
    pin = functools.partial(pltpu.with_memory_space_constraint, memory_space=pltpu.HBM)
    footprints, prior_flux, observed = pin(footprints), pin(prior_flux), pin(observed)
    source, coded = route(tile_row, tile_col)
    tiles, anoms, codes = spread(source, coded, footprints, prior_flux)
    weight = pin(precision_weight.reshape(SOUND_DEV, 1, B))
    part = local(codes, tiles, anoms, observed, weight)
    return gather(part)


def solution(mesh):
    in_specs = (
        P("tile", None, None),
        P("tile"),
        P("tile"),
        P("mem", "tile"),
        P("mem", "tile"),
        P("tile"),
    )
    out_specs = P("mem", "tile")
    return jax.shard_map(body, mesh=mesh, in_specs=in_specs, out_specs=out_specs, check_vma=False)
```

```python
import functools

import jax
import jax.numpy as jnp
from jax import lax
from jax.experimental import pallas as pl
from jax.experimental.pallas import tpu as pltpu
from jax.sharding import PartitionSpec as P

MEMBERS = 256
FLUX_DEV = 8
SOUND_DEV = 16
NZ, NX, NY, NT = 8, 4, 4, 64
CAP = 3
B = 128
LM = 64
MESH = pl.DeviceIdType.MESH
F32, BF16 = jnp.float32, jnp.bfloat16


def route(tile_row, tile_col):
    count = tile_row.shape[0]
    owner = tile_row // SOUND_DEV
    position = jnp.arange(count)
    earlier = (owner[:, None] == owner[None, :]) & (position[None, :] < position[:, None])
    slot = owner * CAP + jnp.sum(earlier.astype(jnp.int32), axis=1)
    match = slot[None, :] == jnp.arange(NT * CAP)[:, None]
    source = jnp.sum(jnp.where(match, position[None, :], 0), axis=1)
    blocks = (tile_row % SOUND_DEV) * 512 + tile_col
    coded = jnp.sum(jnp.where(match, blocks[None, :] + 1, 0), axis=1)
    coded = jnp.where(coded == 0, SOUND_DEV * 512, coded - 1)
    coded = jnp.pad(coded.reshape(NT, CAP), ((0, 0), (0, B - CAP))).reshape(NT, 1, B)
    return source, coded


def spread_kernel(
    source, coded, footprints, prior_h, tiles, anoms, codes,
    prior, quarter, staged, sums, shard,
    s_fp, s_prior, s_sum, r_sum, s_tile, r_tile, s_code, r_code, s_y, r_y, r_y2,
    s_local, s_z, r_z, s_x, r_x, r_x2, s_sib, r_sib,
):
    me = lax.axis_index("tile")
    q = lax.axis_index("mem")
    core = lax.rem(me, 2)
    x = lax.rem(me // 2, NX)
    z = me // 8

    def at_z(o):
        return lax.rem(z + o + NZ, NZ)

    def at_x(o):
        return lax.rem(x + o + NX, NX)

    def at_y(o):
        return lax.rem(q + o + NY, NY)

    def index(zz, xx, cc):
        return zz * 8 + xx * 2 + cc

    def remote(src, dst, ssem, rsem, tile=None, mem=None):
        return pltpu.make_async_remote_copy(
            src_ref=src, dst_ref=dst, send_sem=ssem, recv_sem=rsem,
            device_id={"tile": me if tile is None else tile, "mem": q if mem is None else mem},
            device_id_type=MESH,
        )

    def wait_for(ref, sem):
        pltpu.make_async_copy(ref, ref, sem).wait()

    prior_copy = pltpu.make_async_copy(prior_h, prior, s_prior)
    prior_copy.start()
    fp_copy = pltpu.make_async_copy(
        footprints.at[:, pl.ds(pl.multiple_of(q * 32, 32), 32), :], quarter, s_fp
    )
    fp_copy.start()

    barrier = pltpu.get_barrier_semaphore()

    @pl.loop(1, NT)
    def _(o):
        pl.semaphore_signal(
            barrier, inc=1, device_id={"tile": lax.rem(me + o, NT), "mem": q}, device_id_type=MESH
        )

    for o in range(1, NY):
        pl.semaphore_signal(
            barrier, inc=1, device_id={"tile": me, "mem": at_y(o)}, device_id_type=MESH
        )

    prior_copy.wait()
    for j in range(FLUX_DEV):
        part = jnp.sum(prior[:, j * B : (j + 1) * B].astype(F32), axis=0, keepdims=True)
        sums[0, j : j + 1, :] = part
    pl.semaphore_wait(barrier, NT - 1 + NY - 1)

    sum_sends = []
    for o in range(1, NY):
        cp = remote(sums.at[0], sums.at[o], s_sum.at[o], r_sum.at[o], mem=at_y(o))
        cp.start()
        sum_sends.append(cp)
    fp_copy.wait()

    def send_tiles(dz):
        first = 1 if dz == 0 else 0

        @pl.loop(first, 8)
        def _(o):
            t = at_z(dz) * 8 + lax.rem(me + o, 8)
            for s in range(CAP):
                staged[t, s] = quarter[source[t * CAP + s]]
            remote(staged.at[t], tiles.at[q, me], s_tile, r_tile.at[dz], tile=t).start()
            remote(coded.at[t], codes.at[me], s_code, r_code, tile=t).start()

        if dz == 0:
            for s in range(CAP):
                staged[me, s] = quarter[source[me * CAP + s]]
            pltpu.make_async_copy(staged.at[me], tiles.at[q, me], r_tile.at[0]).start()
            pltpu.make_async_copy(coded.at[me], codes.at[me], r_code).start()

    def group(quarter_index, dz, first=0, size=8):
        zs = at_z(-dz)
        return tiles.at[quarter_index, pl.ds(zs * 8 + first, size)]

    pending = []

    def go(cp):
        cp.start()
        pending.append(cp)

    def y_first(dz):
        wait_for(group(q, dz), r_tile.at[dz])
        go(remote(group(q, dz), group(q, dz), s_y.at[0, dz], r_y.at[0, dz], mem=at_y(1)))
        go(remote(group(q, dz), group(q, dz), s_y.at[1, dz], r_y.at[1, dz], mem=at_y(-1)))

    def y_second(dz):
        back = group(at_y(-1), dz)
        wait_for(back, r_y.at[0, dz])
        part = group(at_y(-1), dz, 0, 4)
        go(remote(part, part, s_y.at[2, dz], r_y2.at[0, dz], mem=at_y(1)))
        fore = group(at_y(1), dz)
        wait_for(fore, r_y.at[1, dz])
        part = group(at_y(1), dz, 4, 4)
        go(remote(part, part, s_y.at[3, dz], r_y2.at[1, dz], mem=at_y(-1)))

    def y_last(dz):
        wait_for(group(at_y(2), dz, 0, 4), r_y2.at[0, dz])
        wait_for(group(at_y(2), dz, 4, 4), r_y2.at[1, dz])

    def block(oz, ox, own_core=True):
        return anoms.at[index(at_z(oz), at_x(ox), core if own_core else 1 - core)]

    def to_sibling(oz, ox):
        go(
            remote(
                block(oz, ox), block(oz, ox), s_sib.at[ox % NX, oz % NZ], r_sib.at[ox % NX, oz % NZ],
                tile=index(z, x, 1 - core),
            )
        )

    def x_first(oz, src=None):
        b = block(oz, 0)
        src = b if src is None else src
        k = oz % NZ
        go(remote(src, b, s_x.at[0, k], r_x.at[0, k], tile=index(z, at_x(1), core)))
        go(remote(src, b, s_x.at[1, k], r_x.at[1, k], tile=index(z, at_x(-1), core)))
        go(remote(src, b, s_sib.at[0, k], r_sib.at[0, k], tile=index(z, x, 1 - core)))

    def x_second(oz):
        k = oz % NZ
        b = block(oz, -1)
        wait_for(b, r_x.at[0, k])
        h = b.at[pl.ds(0, 4)]
        go(remote(h, h, s_x.at[2, k], r_x2.at[0, k], tile=index(z, at_x(1), core)))
        to_sibling(oz, -1)
        b = block(oz, 1)
        wait_for(b, r_x.at[1, k])
        h = b.at[pl.ds(4, 4)]
        go(remote(h, h, s_x.at[3, k], r_x2.at[1, k], tile=index(z, at_x(-1), core)))
        to_sibling(oz, 1)

    def x_last(oz):
        k = oz % NZ
        b = block(oz, 2)
        wait_for(b.at[pl.ds(0, 4)], r_x2.at[0, k])
        wait_for(b.at[pl.ds(4, 4)], r_x2.at[1, k])
        to_sibling(oz, 2)

    def z_step(k):
        up, down = index(at_z(1), x, core), index(at_z(-1), x, core)
        if k < 4:
            b = block(-k, 0)
            wait_for(b, r_z.at[0, k])
            h = b if k < 3 else b.at[pl.ds(0, 4)]
            go(remote(h, h, s_z.at[0, k + 1], r_z.at[0, k + 1], tile=up))
            x_first(-k)
            b = block(k, 0)
            wait_for(b, r_z.at[1, k])
            h = b if k < 3 else b.at[pl.ds(4, 4)]
            go(remote(h, h, s_z.at[1, k + 1], r_z.at[1, k + 1], tile=down))
            x_first(k)
        else:
            b = block(4, 0)
            wait_for(b.at[pl.ds(0, 4)], r_z.at[0, 4])
            wait_for(b.at[pl.ds(4, 4)], r_z.at[1, 4])
            x_first(4)

    send_tiles(0)

    for cp in sum_sends:
        cp.wait()
    mean = (sums[0] + sums[1] + sums[2] + sums[3]) / MEMBERS
    for j in range(FLUX_DEV):
        shard[j] = (prior[:, j * B : (j + 1) * B].astype(F32) - mean[j : j + 1, :]).astype(BF16)
    own_copy = pltpu.make_async_copy(shard, anoms.at[me], s_local)
    own_copy.start()
    go(remote(shard, anoms.at[me], s_z.at[0, 1], r_z.at[0, 1], tile=index(at_z(1), x, core)))
    go(remote(shard, anoms.at[me], s_z.at[1, 1], r_z.at[1, 1], tile=index(at_z(-1), x, core)))
    x_first(0, shard)

    send_tiles(1)
    send_tiles(7)
    y_first(0)
    z_step(1)
    send_tiles(2)
    send_tiles(6)
    x_second(0)
    y_first(1)
    y_first(7)
    z_step(2)
    send_tiles(3)
    send_tiles(5)
    y_second(0)
    x_second(-1)
    x_second(1)
    z_step(3)
    send_tiles(4)
    y_second(1)
    y_second(7)
    y_first(2)
    y_first(6)
    x_last(0)
    x_second(-2)
    x_second(2)
    z_step(4)
    y_first(3)
    y_first(5)
    y_second(2)
    y_second(6)
    x_last(-1)
    x_last(1)
    x_second(-3)
    x_second(3)
    y_first(4)
    y_second(3)
    y_second(5)
    x_last(-2)
    x_last(2)
    x_second(4)
    y_second(4)
    x_last(-3)
    x_last(3)
    x_last(4)
    for dz in (0, 1, 7, 2, 6, 3, 5, 4):
        y_last(dz)
    for oz in (0, 1, 7, 2, 6, 3, 5, 4):
        for ox in range(NX):
            wait_for(block(oz, ox, False), r_sib.at[ox, oz])
    wait_for(codes, r_code)
    own_copy.wait()
    for cp in pending:
        cp.wait_send()
    wait_for(staged.at[pl.ds(0, NT - 1)], s_tile)
    wait_for(codes.at[pl.ds(0, NT - 1)], s_code)


def spread(source, coded, footprints, prior):
    hbm = pl.BlockSpec(memory_space=pltpu.HBM)
    vmem = pl.BlockSpec(memory_space=pltpu.VMEM)
    dma = pltpu.SemaphoreType.DMA
    return pl.pallas_call(
        spread_kernel,
        out_shape=(
            jax.ShapeDtypeStruct((NY, NT, CAP, 32, B), BF16),
            jax.ShapeDtypeStruct((NT, FLUX_DEV, LM, B), BF16),
            jax.ShapeDtypeStruct((NT, 1, B), jnp.int32),
        ),
        in_specs=[pl.BlockSpec(memory_space=pltpu.SMEM), vmem, hbm, hbm],
        out_specs=(vmem, vmem, vmem),
        scratch_shapes=[
            pltpu.VMEM((LM, FLUX_DEV * B), BF16),
            pltpu.VMEM((B, 32, B), BF16),
            pltpu.VMEM((NT, CAP, 32, B), BF16),
            pltpu.VMEM((NY, FLUX_DEV, B), F32),
            pltpu.VMEM((FLUX_DEV, LM, B), BF16),
            dma, dma, dma((NY,)), dma((NY,)), dma, dma((NZ,)), dma, dma,
            dma((4, NZ)), dma((2, NZ)), dma((2, NZ)),
            dma, dma((2, 5)), dma((2, 5)), dma((4, NZ)), dma((2, NZ)), dma((2, NZ)),
            dma((NX, NZ)), dma((NX, NZ)),
        ],
        compiler_params=pltpu.CompilerParams(
            collective_id=0, has_side_effects=True, vmem_limit_bytes=16 * 2**20
        ),
        name="spread",
    )(source, coded, footprints, prior)


def local_kernel(
    codes, tiles, anoms, observed_h, weight_h, out,
    observed, weight, modelled, weighted, total, s_obs, s_weight,
):
    observed_in = pltpu.make_async_copy(observed_h, observed, s_obs)
    observed_in.start()
    weight_in = pltpu.make_async_copy(weight_h, weight, s_weight)
    weight_in.start()
    modelled[...] = jnp.zeros_like(modelled)
    step = 2

    def fetch(i, o, s):
        src = i * step + o
        code = codes[src, 0, s]
        return tiles[:, src, s].reshape(B, B), code // 512, lax.rem(code, 512)

    @pl.loop(0, NT // step)
    def _(i):
        terms = []
        for o in range(step):
            for s in range(CAP):
                tile, row, col = fetch(i, o, s)
                term = lax.dot_general(
                    anoms[col], tile, (((1,), (1,)), ((), ())), preferred_element_type=F32
                )
                terms.append((row, term))
        total[pl.ds(i * 16, 16)] = jnp.zeros((16, LM, B), F32)
        for row, term in terms:
            modelled[row] += term

    observed_in.wait()
    weight_in.wait()
    for r in range(SOUND_DEV):
        factor = weight[r].astype(F32) / 8.0
        gap = modelled[r] - observed[:, r * B : (r + 1) * B]
        weighted[r] = (factor * gap).astype(BF16)
    weighted[SOUND_DEV] = jnp.zeros((LM, B), BF16)

    @pl.loop(0, NT // step)
    def _(i):
        terms = []
        for o in range(step):
            for s in range(CAP):
                tile, row, col = fetch(i, o, s)
                term = lax.dot_general(
                    weighted[row], tile, (((1,), (0,)), ((), ())), preferred_element_type=F32
                )
                terms.append((col, term))
        for col, term in terms:
            total[col] += term

    @pl.loop(0, NT)
    def _(i):
        out[pl.ds(i * 8, 8)] = total[pl.ds(i * 8, 8)].astype(BF16)


def local(codes, tiles, anoms, observed, weight):
    hbm = pl.BlockSpec(memory_space=pltpu.HBM)
    vmem = pl.BlockSpec(memory_space=pltpu.VMEM)
    dma = pltpu.SemaphoreType.DMA
    return pl.pallas_call(
        local_kernel,
        out_shape=jax.ShapeDtypeStruct((NT * FLUX_DEV, LM, B), BF16),
        in_specs=[pl.BlockSpec(memory_space=pltpu.SMEM), vmem, vmem, hbm, hbm],
        out_specs=vmem,
        scratch_shapes=[
            pltpu.VMEM((LM, SOUND_DEV * B), F32),
            pltpu.VMEM((SOUND_DEV, 1, B), jnp.int32),
            pltpu.VMEM((SOUND_DEV + 1, LM, B), F32),
            pltpu.VMEM((SOUND_DEV + 1, LM, B), BF16),
            pltpu.VMEM((NT * FLUX_DEV, LM, B), F32),
            dma, dma,
        ],
        compiler_params=pltpu.CompilerParams(vmem_limit_bytes=22 * 2**20),
        name="local",
    )(codes, tiles, anoms.reshape(NT * FLUX_DEV, LM, B), observed, weight)


NA = 5
NB = FLUX_DEV - NA
FAR_X = ((4, 3, 2, 1), (5, 6, 7, 0))
NEAR_X = (4, 5, 3, 6, 2, 7, 1, 0)
FAR_Z = ((2, 1), (3, 0))
NEAR_Z = (2, 1, 3, 0)


def gather_kernel(
    part, out,
    pa, pb, ra, rb, xa1, xa2, zb1, zb2, za1, za2, xb1, xb2,
    s_sib_a, r_sib_a, s_sib_b, r_sib_b,
    s_xa1, r_xa1, s_xa2, r_xa2, s_zb1, r_zb1, s_zb2, r_zb2, s_za, r_za, s_xb, r_xb,
):
    me = lax.axis_index("tile")
    q = lax.axis_index("mem")
    core = lax.rem(me, 2)
    x = lax.rem(me // 2, NX)
    z = me // 8

    def at_z(o):
        return lax.rem(z + o + NZ, NZ)

    def at_x(o):
        return lax.rem(x + o + NX, NX)

    def index(zz, xx, cc):
        return zz * 8 + xx * 2 + cc

    sibling = index(z, x, 1 - core)
    x_next = (index(z, at_x(1), core), index(z, at_x(-1), core))
    z_next = (index(at_z(1), x, core), index(at_z(-1), x, core))

    pending = []

    def send(src, dst, ssem, rsem, tile):
        cp = pltpu.make_async_remote_copy(
            src_ref=src, dst_ref=dst, send_sem=ssem, recv_sem=rsem,
            device_id={"tile": tile, "mem": q}, device_id_type=MESH,
        )
        cp.start()
        pending.append(cp)

    def wait_for(ref, sem):
        pltpu.make_async_copy(ref, ref, sem).wait()

    barrier = pltpu.get_barrier_semaphore()
    for t in (sibling, *x_next, *z_next):
        pl.semaphore_signal(barrier, inc=1, device_id={"tile": t, "mem": q}, device_id_type=MESH)
    pl.semaphore_wait(barrier, 5)

    for kind, d in (("b", 4), ("a", 2), ("b", 3), ("b", 5), ("a", 1), ("a", 3),
                    ("b", 2), ("b", 6), ("b", 1), ("b", 7), ("a", 0), ("b", 0)):
        if kind == "a":
            send(part.at[:, at_x(d), 1 - core, pl.ds(0, NA)], ra.at[d], s_sib_a.at[d], r_sib_a.at[d], sibling)
        else:
            send(part.at[at_z(d), :, 1 - core, pl.ds(NA, NB)], rb.at[d], s_sib_b.at[d], r_sib_b.at[d], sibling)

    settled = set()

    def from_a(d, zz):
        if ("a", d) not in settled:
            settled.add(("a", d))
            wait_for(ra.at[d], r_sib_a.at[d])
        return [part.at[zz, at_x(d), core], ra.at[d, zz]]

    def from_b(d, xx):
        if ("b", d) not in settled:
            settled.add(("b", d))
            wait_for(rb.at[d], r_sib_b.at[d])
        return [part.at[at_z(d), xx, core, pl.ds(NA, NB)], rb.at[d, xx]]

    def total(dst, sources, first, last):
        @pl.loop(first, last)
        def _(b):
            value = None
            for s in sources:
                ref, start = s if isinstance(s, tuple) else (s, 0)
                v = ref[b - start].astype(F32)
                value = v if value is None else value + v
            dst[b] = value.astype(BF16)

    def result(base, sources, count):
        for b in range(count):
            value = None
            for s in sources:
                v = s[b].astype(F32)
                value = v if value is None else value + v
            out[:, (base + b) * B : (base + b + 1) * B] = value

    def a_far(k):
        for i in range(2):
            zz = at_z(FAR_X[i][k])
            total(pa.at[2, zz], from_a(2, zz), 0, NA)
            send(pa.at[2, zz], xa1.at[i, k], s_xa1.at[i, k], r_xa1.at[i, k], x_next[i])

    def a_near(j):
        oz = NEAR_X[j]
        zz = at_z(oz)
        for i, d in enumerate((1, 3)):
            sources = from_a(d, zz)
            if oz in FAR_X[i]:
                k = FAR_X[i].index(oz)
                wait_for(xa1.at[i, k], r_xa1.at[i, k])
                sources.append(xa1.at[i, k])
            total(pa.at[d, zz], sources, 0, NA)
            send(pa.at[d, zz], xa2.at[i, j], s_xa2.at[i, j], r_xa2.at[i, j], x_next[i])

    half_a, half_b = (NA + 1) // 2, (NB + 1) // 2

    def a_own(oz):
        j = NEAR_X.index(oz)
        zz = at_z(oz)
        for i in range(2):
            wait_for(xa2.at[i, j], r_xa2.at[i, j])
        sources = [*from_a(0, zz), xa2.at[0, j], xa2.at[1, j]]
        mine = pa.at[0, zz]
        if oz == 4:
            total(mine, sources, 0, NA)
            for i, (first, size) in enumerate(((0, half_a), (half_a, NA - half_a))):
                piece = za1.at[pl.ds(first, size)]
                send(mine.at[pl.ds(first, size)], piece, s_za.at[i, 0], r_za.at[i, 0], z_next[i])
        elif oz in (3, 5):
            i = (3, 5).index(oz)
            first, size = ((0, half_a), (half_a, NA - half_a))[i]
            wait_for(za1.at[pl.ds(first, size)], r_za.at[i, 0])
            total(mine, [*sources, za1], first, first + size)
            total(mine, sources, *((half_a, NA), (0, half_a))[i])
            send(mine, za2.at[i, 0], s_za.at[i, 1], r_za.at[i, 1], z_next[i])
        elif oz != 0:
            i = 0 if oz < 4 else 1
            step = 4 - oz if i == 0 else oz - 4
            wait_for(za2.at[i, step - 2], r_za.at[i, step - 1])
            total(mine, [*sources, za2.at[i, step - 2]], 0, NA)
            send(mine, za2.at[i, step - 1], s_za.at[i, step], r_za.at[i, step], z_next[i])
        else:
            for i in range(2):
                wait_for(za2.at[i, 2], r_za.at[i, 3])
            result(0, [*sources, za2.at[0, 2], za2.at[1, 2]], NA)

    def b_far(k):
        for i in range(2):
            xx = at_x(FAR_Z[i][k])
            total(pb.at[4, xx], from_b(4, xx), 0, NB)
            send(pb.at[4, xx], zb1.at[i, k], s_zb1.at[i, k], r_zb1.at[i, k], z_next[i])

    def b_near(step, j):
        ox = NEAR_Z[j]
        xx = at_x(ox)
        for i, d in enumerate((4 - step, 4 + step)):
            sources = from_b(d, xx)
            if step > 1:
                wait_for(zb2.at[i, step - 2, j], r_zb2.at[i, step - 2, j])
                sources.append(zb2.at[i, step - 2, j])
            elif ox in FAR_Z[i]:
                k = FAR_Z[i].index(ox)
                wait_for(zb1.at[i, k], r_zb1.at[i, k])
                sources.append(zb1.at[i, k])
            total(pb.at[d, xx], sources, 0, NB)
            send(
                pb.at[d, xx], zb2.at[i, step - 1, j], s_zb2.at[i, step - 1, j], r_zb2.at[i, step - 1, j], z_next[i]
            )

    def b_own(ox):
        j = NEAR_Z.index(ox)
        xx = at_x(ox)
        for i in range(2):
            wait_for(zb2.at[i, 2, j], r_zb2.at[i, 2, j])
        sources = [*from_b(0, xx), zb2.at[0, 2, j], zb2.at[1, 2, j]]
        mine = pb.at[0, xx]
        halves = ((0, half_b), (half_b, NB - half_b))
        if ox == 2:
            total(mine, sources, 0, NB)
            for i, (first, size) in enumerate(halves):
                piece = xb1.at[pl.ds(first, size)]
                send(mine.at[pl.ds(first, size)], piece, s_xb.at[i, 0], r_xb.at[i, 0], x_next[i])
        elif ox != 0:
            i = (1, 3).index(ox)
            first, size = halves[i]
            wait_for(xb1.at[pl.ds(first, size)], r_xb.at[i, 0])
            total(mine, [*sources, xb1], first, first + size)
            total(mine, sources, *((half_b, NB), (0, half_b))[i])
            send(mine, xb2.at[i], s_xb.at[i, 1], r_xb.at[i, 1], x_next[i])
        else:
            for i in range(2):
                wait_for(xb2.at[i], r_xb.at[i, 1])
            result(NA, [*sources, xb2.at[0], xb2.at[1]], NB)

    events = []
    for k in range(2):
        events.append((1.9 + 0.3 * k, b_far, (k,)))
    for k in range(4):
        events.append((2.0 + 0.3 * k, a_far, (k,)))
    for j in range(8):
        events.append((4.0 + 1.7 * (j // 2 + 1), a_near, (j,)))
        events.append((11.2 + 1.65 * (j + 1), a_own, (NEAR_X[j],)))
    for j in range(4):
        for step in (1, 2, 3):
            events.append((4.0 * step + min(j + 1, 2 if step == 1 else 4), b_near, (step, j)))
    for ox, when in ((2, 17.0), (1, 19.5), (3, 19.6), (0, 22.5)):
        events.append((when, b_own, (ox,)))
    for _, act, args in sorted(events, key=lambda e: e[0]):
        act(*args)
    for cp in pending:
        cp.wait_send()


def gather(part):
    vmem = pl.BlockSpec(memory_space=pltpu.VMEM)
    dma = pltpu.SemaphoreType.DMA
    return pl.pallas_call(
        gather_kernel,
        out_shape=jax.ShapeDtypeStruct((LM, FLUX_DEV * B), F32),
        in_specs=[vmem],
        out_specs=vmem,
        scratch_shapes=[
            pltpu.VMEM((NX, NZ, NA, LM, B), BF16),
            pltpu.VMEM((NZ, NX, NB, LM, B), BF16),
            pltpu.VMEM((NX, NZ, NA, LM, B), BF16),
            pltpu.VMEM((NZ, NX, NB, LM, B), BF16),
            pltpu.VMEM((2, 4, NA, LM, B), BF16),
            pltpu.VMEM((2, NZ, NA, LM, B), BF16),
            pltpu.VMEM((2, 2, NB, LM, B), BF16),
            pltpu.VMEM((2, 3, NX, NB, LM, B), BF16),
            pltpu.VMEM((NA, LM, B), BF16),
            pltpu.VMEM((2, 3, NA, LM, B), BF16),
            pltpu.VMEM((NB, LM, B), BF16),
            pltpu.VMEM((2, NB, LM, B), BF16),
            dma((NX,)), dma((NX,)), dma((NZ,)), dma((NZ,)),
            dma((2, 4)), dma((2, 4)), dma((2, NZ)), dma((2, NZ)),
            dma((2, 2)), dma((2, 2)), dma((2, 3, NX)), dma((2, 3, NX)),
            dma((2, 4)), dma((2, 4)), dma((2, 2)), dma((2, 2)),
        ],
        compiler_params=pltpu.CompilerParams(
            collective_id=1, has_side_effects=True, vmem_limit_bytes=18 * 2**20
        ),
        name="gather",
    )(part.reshape(NZ, NX, 2, FLUX_DEV, LM, B))


def body(footprints, tile_row, tile_col, prior_flux, observed, precision_weight):
    pin = functools.partial(pltpu.with_memory_space_constraint, memory_space=pltpu.HBM)
    footprints, prior_flux, observed = pin(footprints), pin(prior_flux), pin(observed)
    source, coded = route(tile_row, tile_col)
    tiles, anoms, codes = spread(source, coded, footprints, prior_flux)
    weight = pin(precision_weight.reshape(SOUND_DEV, 1, B))
    part = local(codes, tiles, anoms, observed, weight)
    return gather(part)


def solution(mesh):
    in_specs = (
        P("tile", None, None),
        P("tile"),
        P("tile"),
        P("mem", "tile"),
        P("mem", "tile"),
        P("tile"),
    )
    out_specs = P("mem", "tile")
    return jax.shard_map(body, mesh=mesh, in_specs=in_specs, out_specs=out_specs, check_vma=False)
```

```python
import functools

import jax
import jax.numpy as jnp
from jax import lax
from jax.experimental import pallas as pl
from jax.experimental.pallas import tpu as pltpu
from jax.sharding import PartitionSpec as P

MEMBERS = 256
FLUX_DEV = 8
SOUND_DEV = 16
NZ, NX, NY, NT = 8, 4, 4, 64
CAP = 3
B = 128
LM = 64
MESH = pl.DeviceIdType.MESH
F32, BF16 = jnp.float32, jnp.bfloat16


def route(tile_row, tile_col):
    count = tile_row.shape[0]
    owner = tile_row // SOUND_DEV
    position = jnp.arange(count)
    earlier = (owner[:, None] == owner[None, :]) & (position[None, :] < position[:, None])
    slot = owner * CAP + jnp.sum(earlier.astype(jnp.int32), axis=1)
    match = slot[None, :] == jnp.arange(NT * CAP)[:, None]
    source = jnp.sum(jnp.where(match, position[None, :], 0), axis=1)
    blocks = (tile_row % SOUND_DEV) * 512 + tile_col
    coded = jnp.sum(jnp.where(match, blocks[None, :] + 1, 0), axis=1)
    coded = jnp.where(coded == 0, SOUND_DEV * 512, coded - 1)
    coded = jnp.pad(coded.reshape(NT, CAP), ((0, 0), (0, B - CAP))).reshape(NT, 1, B)
    return source, coded


SPREAD_ORDER = (
    ("T", 0), ("T", 1), ("T", 7), ("A0",), ("T", 2), ("T", 6), ("Y1", 0), ("Y1", 1), ("Y1", 7), ("Z", 0, 1),
    ("Z", 1, 1), ("X", 0, 0), ("X", 1, 0), ("Y2", 0, 0), ("Y2", 1, 0), ("T", 3), ("T", 5), ("Y2", 0, 1),
    ("Y2", 1, 1), ("X", 0, 7), ("X", 1, 7), ("Y1", 2), ("Y1", 6), ("Y2", 0, 7), ("Y2", 1, 7), ("X", 0, 1),
    ("Z", 0, 2), ("X", 1, 1), ("Z", 1, 2), ("XL", 0), ("T", 4), ("XL", 7), ("Y2", 0, 2), ("Y2", 1, 2),
    ("X", 1, 6), ("X", 0, 6), ("XL", 1), ("Y2", 0, 6), ("Y2", 1, 6), ("Y1", 3), ("X", 0, 2), ("X", 1, 2),
    ("Y1", 5), ("Z", 0, 3), ("Z", 1, 3), ("XL", 6), ("XL", 2), ("X", 0, 5), ("X", 1, 5), ("Y2", 0, 3),
    ("Y2", 1, 3), ("X", 0, 3), ("X", 1, 3), ("XL", 5), ("Y1", 4), ("Z", 0, 4), ("Y2", 0, 5), ("Y2", 1, 5),
    ("XL", 3), ("X", 0, 4), ("X", 1, 4), ("Y2", 0, 4), ("Y2", 1, 4), ("XL", 4),
)


def spread_kernel(
    source, coded, footprints, prior_h, tiles, anoms, codes,
    prior, quarter, staged, sums, shard,
    s_fp, s_prior, s_sum, r_sum, s_tile, r_tile, s_code, r_code, s_y, r_y, r_y2,
    s_local, s_z, r_z, s_x, r_x, r_x2, s_sib, r_sib,
):
    me = lax.axis_index("tile")
    q = lax.axis_index("mem")
    core = lax.rem(me, 2)
    x = lax.rem(me // 2, NX)
    z = me // 8

    def at_z(o):
        return lax.rem(z + o + NZ, NZ)

    def at_x(o):
        return lax.rem(x + o + NX, NX)

    def at_y(o):
        return lax.rem(q + o + NY, NY)

    def index(zz, xx, cc):
        return zz * 8 + xx * 2 + cc

    def remote(src, dst, ssem, rsem, tile=None, mem=None):
        return pltpu.make_async_remote_copy(
            src_ref=src, dst_ref=dst, send_sem=ssem, recv_sem=rsem,
            device_id={"tile": me if tile is None else tile, "mem": q if mem is None else mem},
            device_id_type=MESH,
        )

    def wait_for(ref, sem):
        pltpu.make_async_copy(ref, ref, sem).wait()

    prior_copy = pltpu.make_async_copy(prior_h, prior, s_prior)
    prior_copy.start()
    fp_copy = pltpu.make_async_copy(
        footprints.at[:, pl.ds(pl.multiple_of(q * 32, 32), 32), :], quarter, s_fp
    )
    fp_copy.start()

    barrier = pltpu.get_barrier_semaphore()

    @pl.loop(1, NT)
    def _(o):
        pl.semaphore_signal(
            barrier, inc=1, device_id={"tile": lax.rem(me + o, NT), "mem": q}, device_id_type=MESH
        )

    for o in range(1, NY):
        pl.semaphore_signal(
            barrier, inc=1, device_id={"tile": me, "mem": at_y(o)}, device_id_type=MESH
        )

    prior_copy.wait()
    for j in range(FLUX_DEV):
        part = jnp.sum(prior[:, j * B : (j + 1) * B].astype(F32), axis=0, keepdims=True)
        sums[0, j : j + 1, :] = part
    pl.semaphore_wait(barrier, NT - 1 + NY - 1)

    sum_sends = []
    for o in range(1, NY):
        cp = remote(sums.at[0], sums.at[o], s_sum.at[o], r_sum.at[o], mem=at_y(o))
        cp.start()
        sum_sends.append(cp)
    fp_copy.wait()

    def send_tiles(dz):
        first = 1 if dz == 0 else 0

        @pl.loop(first, 8)
        def _(o):
            t = at_z(dz) * 8 + lax.rem(me + o, 8)
            for s in range(CAP):
                staged[t, s] = quarter[source[t * CAP + s]]
            remote(staged.at[t], tiles.at[q, me], s_tile, r_tile.at[dz], tile=t).start()
            remote(coded.at[t], codes.at[me], s_code, r_code, tile=t).start()

        if dz == 0:
            for s in range(CAP):
                staged[me, s] = quarter[source[me * CAP + s]]
            pltpu.make_async_copy(staged.at[me], tiles.at[q, me], r_tile.at[0]).start()
            pltpu.make_async_copy(coded.at[me], codes.at[me], r_code).start()

    def group(quarter_index, dz, first=0, size=8):
        zs = at_z(-dz)
        return tiles.at[quarter_index, pl.ds(zs * 8 + first, size)]

    pending = []

    def go(cp):
        cp.start()
        pending.append(cp)

    def y_first(dz):
        wait_for(group(q, dz), r_tile.at[dz])
        go(remote(group(q, dz), group(q, dz), s_y.at[0, dz], r_y.at[0, dz], mem=at_y(1)))
        go(remote(group(q, dz), group(q, dz), s_y.at[1, dz], r_y.at[1, dz], mem=at_y(-1)))

    def y_second(i, dz):
        from_, to = ((-1, 1), (1, -1))[i]
        wait_for(group(at_y(from_), dz), r_y.at[i, dz])
        half = group(at_y(from_), dz, 4 * i, 4)
        go(remote(half, half, s_y.at[2 + i, dz], r_y2.at[i, dz], mem=at_y(to)))

    def y_last(dz):
        wait_for(group(at_y(2), dz, 0, 4), r_y2.at[0, dz])
        wait_for(group(at_y(2), dz, 4, 4), r_y2.at[1, dz])

    def block(oz, ox, own_core=True):
        return anoms.at[index(at_z(oz), at_x(ox), core if own_core else 1 - core)]

    def to_sibling(oz, ox):
        go(
            remote(
                block(oz, ox), block(oz, ox), s_sib.at[ox % NX, oz % NZ], r_sib.at[ox % NX, oz % NZ],
                tile=index(z, x, 1 - core),
            )
        )

    def x_first(oz, src=None):
        b = block(oz, 0)
        src = b if src is None else src
        k = oz % NZ
        go(remote(src, b, s_x.at[0, k], r_x.at[0, k], tile=index(z, at_x(1), core)))
        go(remote(src, b, s_x.at[1, k], r_x.at[1, k], tile=index(z, at_x(-1), core)))
        go(remote(src, b, s_sib.at[0, k], r_sib.at[0, k], tile=index(z, x, 1 - core)))

    def x_second(i, oz):
        k = oz % NZ
        from_, to = ((-1, 1), (1, -1))[i]
        b = block(oz, from_)
        wait_for(b, r_x.at[i, k])
        h = b.at[pl.ds(4 * i, 4)]
        go(remote(h, h, s_x.at[2 + i, k], r_x2.at[i, k], tile=index(z, at_x(to), core)))
        to_sibling(oz, from_)

    def x_last(oz):
        k = oz % NZ
        b = block(oz, 2)
        wait_for(b.at[pl.ds(0, 4)], r_x2.at[0, k])
        wait_for(b.at[pl.ds(4, 4)], r_x2.at[1, k])
        to_sibling(oz, 2)

    def z_step(i, k):
        if k < 4:
            b = block((-k, k)[i], 0)
            wait_for(b, r_z.at[i, k])
            h = b if k < 3 else b.at[pl.ds(4 * i, 4)]
            go(remote(h, h, s_z.at[i, k + 1], r_z.at[i, k + 1], tile=index(at_z((1, -1)[i]), x, core)))
            x_first((-k, k)[i])
        else:
            b = block(4, 0)
            wait_for(b.at[pl.ds(0, 4)], r_z.at[0, 4])
            wait_for(b.at[pl.ds(4, 4)], r_z.at[1, 4])
            x_first(4)

    own_copy = pltpu.make_async_copy(shard, anoms.at[me], s_local)

    def send_shard():
        for cp in sum_sends:
            cp.wait()
        mean = (sums[0] + sums[1] + sums[2] + sums[3]) / MEMBERS
        for j in range(FLUX_DEV):
            shard[j] = (prior[:, j * B : (j + 1) * B].astype(F32) - mean[j : j + 1, :]).astype(BF16)
        own_copy.start()
        go(remote(shard, anoms.at[me], s_z.at[0, 1], r_z.at[0, 1], tile=index(at_z(1), x, core)))
        go(remote(shard, anoms.at[me], s_z.at[1, 1], r_z.at[1, 1], tile=index(at_z(-1), x, core)))
        x_first(0, shard)

    acts = {
        "T": send_tiles, "A0": send_shard, "Z": z_step, "X": x_second, "XL": x_last, "Y1": y_first, "Y2": y_second
    }
    for name, *numbers in SPREAD_ORDER:
        acts[name](*numbers)
    for dz in (0, 1, 7, 2, 6, 3, 5, 4):
        y_last(dz)
    for oz in (0, 1, 7, 2, 6, 3, 5, 4):
        for ox in range(NX):
            wait_for(block(oz, ox, False), r_sib.at[ox, oz])
    wait_for(codes, r_code)
    own_copy.wait()
    for cp in pending:
        cp.wait_send()
    wait_for(staged.at[pl.ds(0, NT - 1)], s_tile)
    wait_for(codes.at[pl.ds(0, NT - 1)], s_code)


def spread(source, coded, footprints, prior):
    hbm = pl.BlockSpec(memory_space=pltpu.HBM)
    vmem = pl.BlockSpec(memory_space=pltpu.VMEM)
    dma = pltpu.SemaphoreType.DMA
    return pl.pallas_call(
        spread_kernel,
        out_shape=(
            jax.ShapeDtypeStruct((NY, NT, CAP, 32, B), BF16),
            jax.ShapeDtypeStruct((NT, FLUX_DEV, LM, B), BF16),
            jax.ShapeDtypeStruct((NT, 1, B), jnp.int32),
        ),
        in_specs=[pl.BlockSpec(memory_space=pltpu.SMEM), vmem, hbm, hbm],
        out_specs=(vmem, vmem, vmem),
        scratch_shapes=[
            pltpu.VMEM((LM, FLUX_DEV * B), BF16),
            pltpu.VMEM((B, 32, B), BF16),
            pltpu.VMEM((NT, CAP, 32, B), BF16),
            pltpu.VMEM((NY, FLUX_DEV, B), F32),
            pltpu.VMEM((FLUX_DEV, LM, B), BF16),
            dma, dma, dma((NY,)), dma((NY,)), dma, dma((NZ,)), dma, dma,
            dma((4, NZ)), dma((2, NZ)), dma((2, NZ)),
            dma, dma((2, 5)), dma((2, 5)), dma((4, NZ)), dma((2, NZ)), dma((2, NZ)),
            dma((NX, NZ)), dma((NX, NZ)),
        ],
        compiler_params=pltpu.CompilerParams(
            collective_id=0, has_side_effects=True, vmem_limit_bytes=16 * 2**20
        ),
        name="spread",
    )(source, coded, footprints, prior)


def local_kernel(
    codes, tiles, anoms, observed_h, weight_h, out,
    observed, weight, modelled, weighted, total, s_obs, s_weight,
):
    observed_in = pltpu.make_async_copy(observed_h, observed, s_obs)
    observed_in.start()
    weight_in = pltpu.make_async_copy(weight_h, weight, s_weight)
    weight_in.start()
    modelled[...] = jnp.zeros_like(modelled)
    step = 16

    def fetch(i, o, s):
        src = i * step + o
        code = codes[src, 0, s]
        return tiles[:, src, s].reshape(B, B), code // 512, lax.rem(code, 512)

    @pl.loop(0, NT // step)
    def _(i):
        terms = []
        for o in range(step):
            for s in range(CAP):
                tile, row, col = fetch(i, o, s)
                term = lax.dot_general(
                    anoms[col], tile, (((1,), (1,)), ((), ())), preferred_element_type=F32
                )
                terms.append((row, term))
        total[pl.ds(i * 128, 128)] = jnp.zeros((128, LM, B), F32)
        for row, term in terms:
            modelled[row] += term

    observed_in.wait()
    weight_in.wait()
    for r in range(SOUND_DEV):
        factor = weight[r].astype(F32) / 8.0
        gap = modelled[r] - observed[:, r * B : (r + 1) * B]
        weighted[r] = (factor * gap).astype(BF16)
    weighted[SOUND_DEV] = jnp.zeros((LM, B), BF16)

    @pl.loop(0, NT // step)
    def _(i):
        terms = []
        for o in range(step):
            for s in range(CAP):
                tile, row, col = fetch(i, o, s)
                term = lax.dot_general(
                    weighted[row], tile, (((1,), (0,)), ((), ())), preferred_element_type=F32
                )
                terms.append((col, term))
        for col, term in terms:
            total[col] += term

    @pl.loop(0, NT)
    def _(i):
        out[pl.ds(i * 8, 8)] = total[pl.ds(i * 8, 8)].astype(BF16)


def local(codes, tiles, anoms, observed, weight):
    hbm = pl.BlockSpec(memory_space=pltpu.HBM)
    vmem = pl.BlockSpec(memory_space=pltpu.VMEM)
    dma = pltpu.SemaphoreType.DMA
    return pl.pallas_call(
        local_kernel,
        out_shape=jax.ShapeDtypeStruct((NT * FLUX_DEV, LM, B), BF16),
        in_specs=[pl.BlockSpec(memory_space=pltpu.SMEM), vmem, vmem, hbm, hbm],
        out_specs=vmem,
        scratch_shapes=[
            pltpu.VMEM((LM, SOUND_DEV * B), F32),
            pltpu.VMEM((SOUND_DEV, 1, B), jnp.int32),
            pltpu.VMEM((SOUND_DEV + 1, LM, B), F32),
            pltpu.VMEM((SOUND_DEV + 1, LM, B), BF16),
            pltpu.VMEM((NT * FLUX_DEV, LM, B), F32),
            dma, dma,
        ],
        compiler_params=pltpu.CompilerParams(vmem_limit_bytes=22 * 2**20),
        name="local",
    )(codes, tiles, anoms.reshape(NT * FLUX_DEV, LM, B), observed, weight)


NA = 5
NB = FLUX_DEV - NA
FAR_X = ((4, 3, 2, 1), (5, 6, 7, 0))
NEAR_X = (4, 5, 3, 6, 2, 7, 1, 0)
FAR_Z = ((2, 1), (3, 0))
NEAR_Z = (2, 1, 3, 0)


def gather_kernel(
    part, out,
    pa, pb, ra, rb, xa1, xa2, zb1, zb2, za1, za2, xb1, xb2,
    s_sib_a, r_sib_a, s_sib_b, r_sib_b,
    s_xa1, r_xa1, s_xa2, r_xa2, s_zb1, r_zb1, s_zb2, r_zb2, s_za, r_za, s_xb, r_xb,
):
    me = lax.axis_index("tile")
    q = lax.axis_index("mem")
    core = lax.rem(me, 2)
    x = lax.rem(me // 2, NX)
    z = me // 8

    def at_z(o):
        return lax.rem(z + o + NZ, NZ)

    def at_x(o):
        return lax.rem(x + o + NX, NX)

    def index(zz, xx, cc):
        return zz * 8 + xx * 2 + cc

    sibling = index(z, x, 1 - core)
    x_next = (index(z, at_x(1), core), index(z, at_x(-1), core))
    z_next = (index(at_z(1), x, core), index(at_z(-1), x, core))

    pending = []

    def send(src, dst, ssem, rsem, tile):
        cp = pltpu.make_async_remote_copy(
            src_ref=src, dst_ref=dst, send_sem=ssem, recv_sem=rsem,
            device_id={"tile": tile, "mem": q}, device_id_type=MESH,
        )
        cp.start()
        pending.append(cp)

    def wait_for(ref, sem):
        pltpu.make_async_copy(ref, ref, sem).wait()

    barrier = pltpu.get_barrier_semaphore()
    for t in (sibling, *x_next, *z_next):
        pl.semaphore_signal(barrier, inc=1, device_id={"tile": t, "mem": q}, device_id_type=MESH)
    pl.semaphore_wait(barrier, 5)

    for kind, d in (("b", 4), ("a", 2), ("b", 3), ("b", 5), ("a", 1), ("a", 3),
                    ("b", 2), ("b", 6), ("b", 1), ("b", 7), ("a", 0), ("b", 0)):
        if kind == "a":
            send(part.at[:, at_x(d), 1 - core, pl.ds(0, NA)], ra.at[d], s_sib_a.at[d], r_sib_a.at[d], sibling)
        else:
            send(part.at[at_z(d), :, 1 - core, pl.ds(NA, NB)], rb.at[d], s_sib_b.at[d], r_sib_b.at[d], sibling)

    settled = set()

    def from_a(d, zz):
        if ("a", d) not in settled:
            settled.add(("a", d))
            wait_for(ra.at[d], r_sib_a.at[d])
        return [part.at[zz, at_x(d), core], ra.at[d, zz]]

    def from_b(d, xx):
        if ("b", d) not in settled:
            settled.add(("b", d))
            wait_for(rb.at[d], r_sib_b.at[d])
        return [part.at[at_z(d), xx, core, pl.ds(NA, NB)], rb.at[d, xx]]

    def total(dst, sources, first, last):
        @pl.loop(first, last)
        def _(b):
            value = None
            for s in sources:
                ref, start = s if isinstance(s, tuple) else (s, 0)
                v = ref[b - start].astype(F32)
                value = v if value is None else value + v
            dst[b] = value.astype(BF16)

    def result(base, sources, count):
        for b in range(count):
            value = None
            for s in sources:
                v = s[b].astype(F32)
                value = v if value is None else value + v
            out[:, (base + b) * B : (base + b + 1) * B] = value

    def a_far(k):
        for i in range(2):
            zz = at_z(FAR_X[i][k])
            total(pa.at[2, zz], from_a(2, zz), 0, NA)
            send(pa.at[2, zz], xa1.at[i, k], s_xa1.at[i, k], r_xa1.at[i, k], x_next[i])

    def a_near(j):
        oz = NEAR_X[j]
        zz = at_z(oz)
        for i, d in enumerate((1, 3)):
            sources = from_a(d, zz)
            if oz in FAR_X[i]:
                k = FAR_X[i].index(oz)
                wait_for(xa1.at[i, k], r_xa1.at[i, k])
                sources.append(xa1.at[i, k])
            total(pa.at[d, zz], sources, 0, NA)
            send(pa.at[d, zz], xa2.at[i, j], s_xa2.at[i, j], r_xa2.at[i, j], x_next[i])

    half_a, half_b = (NA + 1) // 2, (NB + 1) // 2

    def a_own(oz):
        j = NEAR_X.index(oz)
        zz = at_z(oz)
        for i in range(2):
            wait_for(xa2.at[i, j], r_xa2.at[i, j])
        sources = [*from_a(0, zz), xa2.at[0, j], xa2.at[1, j]]
        mine = pa.at[0, zz]
        if oz == 4:
            total(mine, sources, 0, NA)
            for i, (first, size) in enumerate(((0, half_a), (half_a, NA - half_a))):
                piece = za1.at[pl.ds(first, size)]
                send(mine.at[pl.ds(first, size)], piece, s_za.at[i, 0], r_za.at[i, 0], z_next[i])
        elif oz in (3, 5):
            i = (3, 5).index(oz)
            first, size = ((0, half_a), (half_a, NA - half_a))[i]
            wait_for(za1.at[pl.ds(first, size)], r_za.at[i, 0])
            total(mine, [*sources, za1], first, first + size)
            total(mine, sources, *((half_a, NA), (0, half_a))[i])
            send(mine, za2.at[i, 0], s_za.at[i, 1], r_za.at[i, 1], z_next[i])
        elif oz != 0:
            i = 0 if oz < 4 else 1
            step = 4 - oz if i == 0 else oz - 4
            wait_for(za2.at[i, step - 2], r_za.at[i, step - 1])
            total(mine, [*sources, za2.at[i, step - 2]], 0, NA)
            send(mine, za2.at[i, step - 1], s_za.at[i, step], r_za.at[i, step], z_next[i])
        else:
            for i in range(2):
                wait_for(za2.at[i, 2], r_za.at[i, 3])
            result(0, [*sources, za2.at[0, 2], za2.at[1, 2]], NA)

    def b_far(k):
        for i in range(2):
            xx = at_x(FAR_Z[i][k])
            total(pb.at[4, xx], from_b(4, xx), 0, NB)
            send(pb.at[4, xx], zb1.at[i, k], s_zb1.at[i, k], r_zb1.at[i, k], z_next[i])

    def b_near(step, j):
        ox = NEAR_Z[j]
        xx = at_x(ox)
        for i, d in enumerate((4 - step, 4 + step)):
            sources = from_b(d, xx)
            if step > 1:
                wait_for(zb2.at[i, step - 2, j], r_zb2.at[i, step - 2, j])
                sources.append(zb2.at[i, step - 2, j])
            elif ox in FAR_Z[i]:
                k = FAR_Z[i].index(ox)
                wait_for(zb1.at[i, k], r_zb1.at[i, k])
                sources.append(zb1.at[i, k])
            total(pb.at[d, xx], sources, 0, NB)
            send(
                pb.at[d, xx], zb2.at[i, step - 1, j], s_zb2.at[i, step - 1, j], r_zb2.at[i, step - 1, j], z_next[i]
            )

    def b_own(ox):
        j = NEAR_Z.index(ox)
        xx = at_x(ox)
        for i in range(2):
            wait_for(zb2.at[i, 2, j], r_zb2.at[i, 2, j])
        sources = [*from_b(0, xx), zb2.at[0, 2, j], zb2.at[1, 2, j]]
        mine = pb.at[0, xx]
        halves = ((0, half_b), (half_b, NB - half_b))
        if ox == 2:
            total(mine, sources, 0, NB)
            for i, (first, size) in enumerate(halves):
                piece = xb1.at[pl.ds(first, size)]
                send(mine.at[pl.ds(first, size)], piece, s_xb.at[i, 0], r_xb.at[i, 0], x_next[i])
        elif ox != 0:
            i = (1, 3).index(ox)
            first, size = halves[i]
            wait_for(xb1.at[pl.ds(first, size)], r_xb.at[i, 0])
            total(mine, [*sources, xb1], first, first + size)
            total(mine, sources, *((half_b, NB), (0, half_b))[i])
            send(mine, xb2.at[i], s_xb.at[i, 1], r_xb.at[i, 1], x_next[i])
        else:
            for i in range(2):
                wait_for(xb2.at[i], r_xb.at[i, 1])
            result(NA, [*sources, xb2.at[0], xb2.at[1]], NB)

    events = [(5.0, b_far, (k,)) for k in range(2)] + [(5.1, a_far, (k,)) for k in range(4)]
    for j in range(8):
        events.append((8.3 + 1.65 * (j // 2), a_near, (j,)))
    for oz, when in ((4, 14.9), (5, 18.2), (3, 18.2), (6, 21.5), (2, 21.6), (7, 24.9), (1, 24.9), (0, 28.2)):
        events.append((when, a_own, (oz,)))
    for j in range(4):
        for step, when in ((1, min(7.7 + j, 8.7)), (2, 10.4 + j), (3, 13.1 + j)):
            events.append((when, b_near, (step, j)))
    for ox, when in ((2, 18.6), (1, 23.0), (3, 23.1), (0, 28.5)):
        events.append((when, b_own, (ox,)))
    for _, act, args in sorted(events, key=lambda e: e[0]):
        act(*args)
    for cp in pending:
        cp.wait_send()


def gather(part):
    vmem = pl.BlockSpec(memory_space=pltpu.VMEM)
    dma = pltpu.SemaphoreType.DMA
    return pl.pallas_call(
        gather_kernel,
        out_shape=jax.ShapeDtypeStruct((LM, FLUX_DEV * B), F32),
        in_specs=[vmem],
        out_specs=vmem,
        scratch_shapes=[
            pltpu.VMEM((NX, NZ, NA, LM, B), BF16),
            pltpu.VMEM((NZ, NX, NB, LM, B), BF16),
            pltpu.VMEM((NX, NZ, NA, LM, B), BF16),
            pltpu.VMEM((NZ, NX, NB, LM, B), BF16),
            pltpu.VMEM((2, 4, NA, LM, B), BF16),
            pltpu.VMEM((2, NZ, NA, LM, B), BF16),
            pltpu.VMEM((2, 2, NB, LM, B), BF16),
            pltpu.VMEM((2, 3, NX, NB, LM, B), BF16),
            pltpu.VMEM((NA, LM, B), BF16),
            pltpu.VMEM((2, 3, NA, LM, B), BF16),
            pltpu.VMEM((NB, LM, B), BF16),
            pltpu.VMEM((2, NB, LM, B), BF16),
            dma((NX,)), dma((NX,)), dma((NZ,)), dma((NZ,)),
            dma((2, 4)), dma((2, 4)), dma((2, NZ)), dma((2, NZ)),
            dma((2, 2)), dma((2, 2)), dma((2, 3, NX)), dma((2, 3, NX)),
            dma((2, 4)), dma((2, 4)), dma((2, 2)), dma((2, 2)),
        ],
        compiler_params=pltpu.CompilerParams(
            collective_id=1, has_side_effects=True, vmem_limit_bytes=18 * 2**20
        ),
        name="gather",
    )(part.reshape(NZ, NX, 2, FLUX_DEV, LM, B))


def body(footprints, tile_row, tile_col, prior_flux, observed, precision_weight):
    pin = functools.partial(pltpu.with_memory_space_constraint, memory_space=pltpu.HBM)
    footprints, prior_flux, observed = pin(footprints), pin(prior_flux), pin(observed)
    source, coded = route(tile_row, tile_col)
    tiles, anoms, codes = spread(source, coded, footprints, prior_flux)
    weight = pin(precision_weight.reshape(SOUND_DEV, 1, B))
    part = local(codes, tiles, anoms, observed, weight)
    return gather(part)


def solution(mesh):
    in_specs = (
        P("tile", None, None),
        P("tile"),
        P("tile"),
        P("mem", "tile"),
        P("mem", "tile"),
        P("tile"),
    )
    out_specs = P("mem", "tile")
    return jax.shard_map(body, mesh=mesh, in_specs=in_specs, out_specs=out_specs, check_vma=False)
```

```python
import functools

import jax
import jax.numpy as jnp
from jax import lax
from jax.experimental import pallas as pl
from jax.experimental.pallas import tpu as pltpu
from jax.sharding import PartitionSpec as P

MEMBERS = 256
FLUX_DEV = 8
SOUND_DEV = 16
NZ, NX, NY, NT = 8, 4, 4, 64
CAP = 3
B = 128
LM = 64
MESH = pl.DeviceIdType.MESH
F32, BF16 = jnp.float32, jnp.bfloat16


def route(row, col):
    shape = (B, B)
    down, across = lax.broadcasted_iota(jnp.int32, shape, 0), lax.broadcasted_iota(jnp.int32, shape, 1)

    def column(v):
        return jnp.sum(jnp.where(down == across, v, 0), axis=1, keepdims=True)

    owner = row // SOUND_DEV
    earlier = (column(owner) == owner) & (down < across)
    place = jnp.sum(earlier.astype(jnp.int32), axis=0, keepdims=True)
    slot = column(owner * CAP + place)
    index = lax.broadcasted_iota(jnp.int32, (B, 2 * B), 0)
    at = lax.broadcasted_iota(jnp.int32, (B, 2 * B), 1)
    source = jnp.sum(jnp.where(slot == at, index, 0), axis=0, keepdims=True)
    blocks = (row - owner * SOUND_DEV) * 512 + col - SOUND_DEV * 512
    mine = lax.broadcasted_iota(jnp.int32, (NT, B), 0) == owner
    lane = lax.broadcasted_iota(jnp.int32, (NT, B), 1)
    coded = jnp.full((NT, B), SOUND_DEV * 512, jnp.int32)
    for k in range(CAP):
        found = jnp.sum(jnp.where(mine & (place == k), blocks, 0), axis=1, keepdims=True)
        coded = coded + jnp.where(lane == k, found, 0)
    return source, coded


SPREAD_ORDER = (
    ("T", 0), ("T", 1), ("T", 7), ("A0",), ("T", 2), ("T", 6), ("Y1", 0), ("Y1", 1), ("Y1", 7), ("Z", 0, 1),
    ("Z", 1, 1), ("X", 0, 0), ("X", 1, 0), ("Y2", 0, 0), ("Y2", 1, 0), ("T", 3), ("T", 5), ("Y2", 0, 1),
    ("Y2", 1, 1), ("X", 0, 7), ("X", 1, 7), ("Y1", 2), ("Y1", 6), ("Y2", 0, 7), ("Y2", 1, 7), ("X", 0, 1),
    ("Z", 0, 2), ("X", 1, 1), ("Z", 1, 2), ("XL", 0), ("T", 4), ("XL", 7), ("Y2", 0, 2), ("Y2", 1, 2),
    ("X", 1, 6), ("X", 0, 6), ("XL", 1), ("Y2", 0, 6), ("Y2", 1, 6), ("Y1", 3), ("X", 0, 2), ("X", 1, 2),
    ("Y1", 5), ("Z", 0, 3), ("Z", 1, 3), ("XL", 6), ("XL", 2), ("X", 0, 5), ("X", 1, 5), ("Y2", 0, 3),
    ("Y2", 1, 3), ("X", 0, 3), ("X", 1, 3), ("XL", 5), ("Y1", 4), ("Z", 0, 4), ("Y2", 0, 5), ("Y2", 1, 5),
    ("XL", 3), ("X", 0, 4), ("X", 1, 4), ("Y2", 0, 4), ("Y2", 1, 4), ("XL", 4),
)


def spread_kernel(
    row_h, col_h, footprints, prior_h, tiles, anoms, codes,
    row, col, source_v, source, coded, prior, quarter, staged, sums, shard,
    s_row, s_fp, s_prior, s_sum, r_sum, s_tile, r_tile, s_code, r_code, s_y, r_y, r_y2,
    s_local, s_z, r_z, s_x, r_x, r_x2, s_sib, r_sib, came,
):
    me = lax.axis_index("tile")
    q = lax.axis_index("mem")
    core = lax.rem(me, 2)
    x = lax.rem(me // 2, NX)
    z = me // 8

    def at_z(o):
        return lax.rem(z + o + NZ, NZ)

    def at_x(o):
        return lax.rem(x + o + NX, NX)

    def at_y(o):
        return lax.rem(q + o + NY, NY)

    def index(zz, xx, cc):
        return zz * 8 + xx * 2 + cc

    def remote(src, dst, ssem, rsem, tile=None, mem=None):
        return pltpu.make_async_remote_copy(
            src_ref=src, dst_ref=dst, send_sem=ssem, recv_sem=rsem,
            device_id={"tile": me if tile is None else tile, "mem": q if mem is None else mem},
            device_id_type=MESH,
        )

    def wait_for(ref, sem):
        pltpu.make_async_copy(ref, ref, sem).wait()

    row_copy = pltpu.make_async_copy(row_h, row, s_row.at[0])
    row_copy.start()
    col_copy = pltpu.make_async_copy(col_h, col, s_row.at[1])
    col_copy.start()
    prior_copy = pltpu.make_async_copy(prior_h, prior, s_prior)
    prior_copy.start()
    fp_copy = pltpu.make_async_copy(
        footprints.at[:, pl.ds(pl.multiple_of(q * 32, 32), 32), :], quarter, s_fp
    )
    fp_copy.start()

    barrier = pltpu.get_barrier_semaphore()
    for o in range(1, 8):
        pl.semaphore_signal(
            barrier, inc=1, device_id={"tile": z * 8 + lax.rem(me + o, 8), "mem": q}, device_id_type=MESH
        )
    for o in range(1, NY):
        pl.semaphore_signal(barrier, inc=1, device_id={"tile": me, "mem": at_y(o)}, device_id_type=MESH)
    for o in (1, -1):
        pl.semaphore_signal(
            barrier, inc=1, device_id={"tile": index(at_z(o), x, core), "mem": q}, device_id_type=MESH
        )

    def tell(stage):
        for i, o in enumerate((1, -1)):
            pl.semaphore_signal(
                came.at[i, stage], inc=1, device_id={"tile": index(at_z(o), x, core), "mem": q}, device_id_type=MESH
            )

    def hear(stage):
        for i in range(2):
            pl.semaphore_wait(came.at[i, stage], 1)

    row_copy.wait()
    col_copy.wait()
    source_row, coded_rows = route(row[...], col[...])
    source_v[...] = source_row
    source_copy = pltpu.make_async_copy(source_v, source, s_row.at[2])
    source_copy.start()
    for t in range(NT):
        coded[t] = coded_rows[t : t + 1]
    prior_copy.wait()
    for j in range(FLUX_DEV):
        part = jnp.sum(prior[:, j * B : (j + 1) * B].astype(F32), axis=0, keepdims=True)
        sums[0, j : j + 1, :] = part
    pl.semaphore_wait(barrier, 7 + NY - 1 + 2)
    tell(1)

    sum_sends = []
    for o in range(1, NY):
        cp = remote(sums.at[0], sums.at[o], s_sum.at[o], r_sum.at[o], mem=at_y(o))
        cp.start()
        sum_sends.append(cp)
    fp_copy.wait()
    source_copy.wait()

    def send_tiles(dz):
        first = 1 if dz == 0 else 0
        if 1 <= dz <= 4:
            hear(dz)
            if dz < 4:
                tell(dz + 1)

        @pl.loop(first, 8)
        def _(o):
            t = at_z(dz) * 8 + lax.rem(me + o, 8)
            for s in range(CAP):
                staged[t, s] = quarter[source[0, t * CAP + s]]
            remote(staged.at[t], tiles.at[q, me], s_tile, r_tile.at[dz], tile=t).start()
            remote(coded.at[t], codes.at[me], s_code, r_code, tile=t).start()

        if dz == 0:
            for s in range(CAP):
                staged[me, s] = quarter[source[0, me * CAP + s]]
            pltpu.make_async_copy(staged.at[me], tiles.at[q, me], r_tile.at[0]).start()
            pltpu.make_async_copy(coded.at[me], codes.at[me], r_code).start()

    def group(quarter_index, dz, first=0, size=8):
        zs = at_z(-dz)
        return tiles.at[quarter_index, pl.ds(zs * 8 + first, size)]

    pending = []

    def go(cp):
        cp.start()
        pending.append(cp)

    def y_first(dz):
        wait_for(group(q, dz), r_tile.at[dz])
        go(remote(group(q, dz), group(q, dz), s_y.at[0, dz], r_y.at[0, dz], mem=at_y(1)))
        go(remote(group(q, dz), group(q, dz), s_y.at[1, dz], r_y.at[1, dz], mem=at_y(-1)))

    def y_second(i, dz):
        from_, to = ((-1, 1), (1, -1))[i]
        wait_for(group(at_y(from_), dz), r_y.at[i, dz])
        half = group(at_y(from_), dz, 4 * i, 4)
        go(remote(half, half, s_y.at[2 + i, dz], r_y2.at[i, dz], mem=at_y(to)))

    def y_last(dz):
        wait_for(group(at_y(2), dz, 0, 4), r_y2.at[0, dz])
        wait_for(group(at_y(2), dz, 4, 4), r_y2.at[1, dz])

    def block(oz, ox, own_core=True):
        return anoms.at[index(at_z(oz), at_x(ox), core if own_core else 1 - core)]

    def to_sibling(oz, ox):
        go(
            remote(
                block(oz, ox), block(oz, ox), s_sib.at[ox % NX, oz % NZ], r_sib.at[ox % NX, oz % NZ],
                tile=index(z, x, 1 - core),
            )
        )

    def x_first(oz, src=None):
        b = block(oz, 0)
        src = b if src is None else src
        k = oz % NZ
        go(remote(src, b, s_x.at[0, k], r_x.at[0, k], tile=index(z, at_x(1), core)))
        go(remote(src, b, s_x.at[1, k], r_x.at[1, k], tile=index(z, at_x(-1), core)))
        go(remote(src, b, s_sib.at[0, k], r_sib.at[0, k], tile=index(z, x, 1 - core)))

    def x_second(i, oz):
        k = oz % NZ
        from_, to = ((-1, 1), (1, -1))[i]
        b = block(oz, from_)
        wait_for(b, r_x.at[i, k])
        h = b.at[pl.ds(4 * i, 4)]
        go(remote(h, h, s_x.at[2 + i, k], r_x2.at[i, k], tile=index(z, at_x(to), core)))
        to_sibling(oz, from_)

    def x_last(oz):
        k = oz % NZ
        b = block(oz, 2)
        wait_for(b.at[pl.ds(0, 4)], r_x2.at[0, k])
        wait_for(b.at[pl.ds(4, 4)], r_x2.at[1, k])
        to_sibling(oz, 2)

    def z_step(i, k):
        if k < 4:
            b = block((-k, k)[i], 0)
            wait_for(b, r_z.at[i, k])
            h = b if k < 3 else b.at[pl.ds(4 * i, 4)]
            go(remote(h, h, s_z.at[i, k + 1], r_z.at[i, k + 1], tile=index(at_z((1, -1)[i]), x, core)))
            x_first((-k, k)[i])
        else:
            b = block(4, 0)
            wait_for(b.at[pl.ds(0, 4)], r_z.at[0, 4])
            wait_for(b.at[pl.ds(4, 4)], r_z.at[1, 4])
            x_first(4)

    own_copy = pltpu.make_async_copy(shard, anoms.at[me], s_local)

    def send_shard():
        for cp in sum_sends:
            cp.wait()
        mean = (sums[0] + sums[1] + sums[2] + sums[3]) / MEMBERS
        for j in range(FLUX_DEV):
            shard[j] = (prior[:, j * B : (j + 1) * B].astype(F32) - mean[j : j + 1, :]).astype(BF16)
        own_copy.start()
        go(remote(shard, anoms.at[me], s_z.at[0, 1], r_z.at[0, 1], tile=index(at_z(1), x, core)))
        go(remote(shard, anoms.at[me], s_z.at[1, 1], r_z.at[1, 1], tile=index(at_z(-1), x, core)))
        x_first(0, shard)

    acts = {
        "T": send_tiles, "A0": send_shard, "Z": z_step, "X": x_second, "XL": x_last, "Y1": y_first, "Y2": y_second
    }
    for name, *numbers in SPREAD_ORDER:
        while len(pending) > 40:
            pending.pop(0).wait_send()
        acts[name](*numbers)
    for dz in (0, 1, 7, 2, 6, 3, 5, 4):
        y_last(dz)
    for oz in (0, 1, 7, 2, 6, 3, 5, 4):
        for ox in range(NX):
            wait_for(block(oz, ox, False), r_sib.at[ox, oz])
    wait_for(codes, r_code)
    own_copy.wait()
    for cp in pending:
        cp.wait_send()
    wait_for(staged.at[pl.ds(0, NT - 1)], s_tile)
    wait_for(codes.at[pl.ds(0, NT - 1)], s_code)


def spread(tile_row, tile_col, footprints, prior):
    hbm = pl.BlockSpec(memory_space=pltpu.HBM)
    vmem = pl.BlockSpec(memory_space=pltpu.VMEM)
    dma = pltpu.SemaphoreType.DMA
    return pl.pallas_call(
        spread_kernel,
        out_shape=(
            jax.ShapeDtypeStruct((NY, NT, CAP, 32, B), BF16),
            jax.ShapeDtypeStruct((NT, FLUX_DEV, LM, B), BF16),
            jax.ShapeDtypeStruct((NT, 1, B), jnp.int32),
        ),
        in_specs=[hbm, hbm, hbm, hbm],
        out_specs=(vmem, vmem, vmem),
        scratch_shapes=[
            pltpu.VMEM((1, B), jnp.int32),
            pltpu.VMEM((1, B), jnp.int32),
            pltpu.VMEM((1, 2 * B), jnp.int32),
            pltpu.SMEM((1, 2 * B), jnp.int32),
            pltpu.VMEM((NT, 1, B), jnp.int32),
            pltpu.VMEM((LM, FLUX_DEV * B), BF16),
            pltpu.VMEM((B, 32, B), BF16),
            pltpu.VMEM((NT, CAP, 32, B), BF16),
            pltpu.VMEM((NY, FLUX_DEV, B), F32),
            pltpu.VMEM((FLUX_DEV, LM, B), BF16),
            dma((3,)), dma, dma, dma((NY,)), dma((NY,)), dma, dma((NZ,)), dma, dma,
            dma((4, NZ)), dma((2, NZ)), dma((2, NZ)),
            dma, dma((2, 5)), dma((2, 5)), dma((4, NZ)), dma((2, NZ)), dma((2, NZ)),
            dma((NX, NZ)), dma((NX, NZ)), pltpu.SemaphoreType.REGULAR((2, 5)),
        ],
        compiler_params=pltpu.CompilerParams(
            collective_id=0, has_side_effects=True, vmem_limit_bytes=16 * 2**20
        ),
        name="spread",
    )(tile_row, tile_col, footprints, prior)


def local_kernel(
    codes, tiles, anoms, observed_h, weight_h, out,
    observed, weight, modelled, weighted, total, s_obs, s_weight,
):
    observed_in = pltpu.make_async_copy(observed_h, observed, s_obs)
    observed_in.start()
    weight_in = pltpu.make_async_copy(weight_h, weight, s_weight)
    weight_in.start()
    modelled[...] = jnp.zeros_like(modelled)
    step = 16

    def fetch(i, o, s):
        src = i * step + o
        code = codes[src, 0, s]
        return tiles[:, src, s].reshape(B, B), code // 512, lax.rem(code, 512)

    @pl.loop(0, NT // step)
    def _(i):
        terms = []
        for o in range(step):
            for s in range(CAP):
                tile, row, col = fetch(i, o, s)
                term = lax.dot_general(
                    anoms[col], tile, (((1,), (1,)), ((), ())), preferred_element_type=F32
                )
                terms.append((row, term))
        total[pl.ds(i * 128, 128)] = jnp.zeros((128, LM, B), F32)
        for row, term in terms:
            modelled[row] += term

    observed_in.wait()
    weight_in.wait()
    for r in range(SOUND_DEV):
        factor = weight[r].astype(F32) / 8.0
        gap = modelled[r] - observed[:, r * B : (r + 1) * B]
        weighted[r] = (factor * gap).astype(BF16)
    weighted[SOUND_DEV] = jnp.zeros((LM, B), BF16)

    @pl.loop(0, NT // step)
    def _(i):
        terms = []
        for o in range(step):
            for s in range(CAP):
                tile, row, col = fetch(i, o, s)
                term = lax.dot_general(
                    weighted[row], tile, (((1,), (0,)), ((), ())), preferred_element_type=F32
                )
                terms.append((col, term))
        for col, term in terms:
            total[col] += term

    @pl.loop(0, NT)
    def _(i):
        out[pl.ds(i * 8, 8)] = total[pl.ds(i * 8, 8)].astype(BF16)


def local(codes, tiles, anoms, observed, weight):
    hbm = pl.BlockSpec(memory_space=pltpu.HBM)
    vmem = pl.BlockSpec(memory_space=pltpu.VMEM)
    dma = pltpu.SemaphoreType.DMA
    return pl.pallas_call(
        local_kernel,
        out_shape=jax.ShapeDtypeStruct((NT * FLUX_DEV, LM, B), BF16),
        in_specs=[pl.BlockSpec(memory_space=pltpu.SMEM), vmem, vmem, hbm, hbm],
        out_specs=vmem,
        scratch_shapes=[
            pltpu.VMEM((LM, SOUND_DEV * B), F32),
            pltpu.VMEM((SOUND_DEV, 1, B), jnp.int32),
            pltpu.VMEM((SOUND_DEV + 1, LM, B), F32),
            pltpu.VMEM((SOUND_DEV + 1, LM, B), BF16),
            pltpu.VMEM((NT * FLUX_DEV, LM, B), F32),
            dma, dma,
        ],
        compiler_params=pltpu.CompilerParams(vmem_limit_bytes=22 * 2**20),
        name="local",
    )(codes, tiles, anoms.reshape(NT * FLUX_DEV, LM, B), observed, weight)


NA = 5
NB = FLUX_DEV - NA
FAR_X = ((4, 3, 2, 1), (5, 6, 7, 0))
NEAR_X = (4, 5, 3, 6, 2, 7, 1, 0)
FAR_Z = ((2, 1), (3, 0))
NEAR_Z = (2, 1, 3, 0)


def gather_kernel(
    part, out,
    pa, pb, ra, rb, xa1, xa2, zb1, zb2, za1, za2, xb1, xb2,
    s_sib_a, r_sib_a, s_sib_b, r_sib_b, s_a2, r_a2, s_b4, r_b4,
    s_xa1, r_xa1, s_xa2, r_xa2, s_zb1, r_zb1, s_zb2, r_zb2, s_za, r_za, s_xb, r_xb,
):
    me = lax.axis_index("tile")
    q = lax.axis_index("mem")
    core = lax.rem(me, 2)
    x = lax.rem(me // 2, NX)
    z = me // 8

    def at_z(o):
        return lax.rem(z + o + NZ, NZ)

    def at_x(o):
        return lax.rem(x + o + NX, NX)

    def index(zz, xx, cc):
        return zz * 8 + xx * 2 + cc

    sibling = index(z, x, 1 - core)
    x_next = (index(z, at_x(1), core), index(z, at_x(-1), core))
    z_next = (index(at_z(1), x, core), index(at_z(-1), x, core))

    pending = []

    def send(src, dst, ssem, rsem, tile):
        cp = pltpu.make_async_remote_copy(
            src_ref=src, dst_ref=dst, send_sem=ssem, recv_sem=rsem,
            device_id={"tile": tile, "mem": q}, device_id_type=MESH,
        )
        cp.start()
        pending.append(cp)

    def wait_for(ref, sem):
        pltpu.make_async_copy(ref, ref, sem).wait()

    barrier = pltpu.get_barrier_semaphore()
    for t in (sibling, *x_next, *z_next):
        pl.semaphore_signal(barrier, inc=1, device_id={"tile": t, "mem": q}, device_id_type=MESH)
    pl.semaphore_wait(barrier, 5)

    for ox in NEAR_Z:
        xx = at_x(ox)
        send(part.at[at_z(4), xx, 1 - core, pl.ds(NA, NB)], rb.at[4, xx], s_b4.at[ox], r_b4.at[ox], sibling)
    for oz in NEAR_X:
        zz = at_z(oz)
        send(part.at[zz, at_x(2), 1 - core, pl.ds(0, NA)], ra.at[2, zz], s_a2.at[oz], r_a2.at[oz], sibling)
    for kind, d in (("b", 3), ("b", 5), ("a", 1), ("a", 3), ("b", 2), ("b", 6), ("b", 1), ("b", 7), ("a", 0), ("b", 0)):
        if kind == "a":
            send(part.at[:, at_x(d), 1 - core, pl.ds(0, NA)], ra.at[d], s_sib_a.at[d], r_sib_a.at[d], sibling)
        else:
            send(part.at[at_z(d), :, 1 - core, pl.ds(NA, NB)], rb.at[d], s_sib_b.at[d], r_sib_b.at[d], sibling)

    settled = set()

    def from_a(d, zz):
        if ("a", d) not in settled:
            settled.add(("a", d))
            if d != 2:
                wait_for(ra.at[d], r_sib_a.at[d])
        return [part.at[zz, at_x(d), core], ra.at[d, zz]]

    def from_b(d, xx):
        if ("b", d) not in settled:
            settled.add(("b", d))
            if d != 4:
                wait_for(rb.at[d], r_sib_b.at[d])
        return [part.at[at_z(d), xx, core, pl.ds(NA, NB)], rb.at[d, xx]]

    def total(dst, sources, first, last):
        @pl.loop(first, last)
        def _(b):
            value = None
            for s in sources:
                ref, start = s if isinstance(s, tuple) else (s, 0)
                v = ref[b - start].astype(F32)
                value = v if value is None else value + v
            dst[b] = value.astype(BF16)

    def result(base, sources, count):
        for b in range(count):
            value = None
            for s in sources:
                v = s[b].astype(F32)
                value = v if value is None else value + v
            out[:, (base + b) * B : (base + b + 1) * B] = value

    def a_far(k):
        for i in range(2):
            zz = at_z(FAR_X[i][k])
            wait_for(ra.at[2, zz], r_a2.at[FAR_X[i][k]])
            total(pa.at[2, zz], from_a(2, zz), 0, NA)
            send(pa.at[2, zz], xa1.at[i, k], s_xa1.at[i, k], r_xa1.at[i, k], x_next[i])

    def a_near(j):
        oz = NEAR_X[j]
        zz = at_z(oz)
        for i, d in enumerate((1, 3)):
            sources = from_a(d, zz)
            if oz in FAR_X[i]:
                k = FAR_X[i].index(oz)
                wait_for(xa1.at[i, k], r_xa1.at[i, k])
                sources.append(xa1.at[i, k])
            total(pa.at[d, zz], sources, 0, NA)
            send(pa.at[d, zz], xa2.at[i, j], s_xa2.at[i, j], r_xa2.at[i, j], x_next[i])

    half_a, half_b = (NA + 1) // 2, (NB + 1) // 2

    def a_own(oz):
        j = NEAR_X.index(oz)
        zz = at_z(oz)
        for i in range(2):
            wait_for(xa2.at[i, j], r_xa2.at[i, j])
        sources = [*from_a(0, zz), xa2.at[0, j], xa2.at[1, j]]
        mine = pa.at[0, zz]
        if oz == 4:
            total(mine, sources, 0, NA)
            for i, (first, size) in enumerate(((0, half_a), (half_a, NA - half_a))):
                piece = za1.at[pl.ds(first, size)]
                send(mine.at[pl.ds(first, size)], piece, s_za.at[i, 0], r_za.at[i, 0], z_next[i])
        elif oz in (3, 5):
            i = (3, 5).index(oz)
            first, size = ((0, half_a), (half_a, NA - half_a))[i]
            wait_for(za1.at[pl.ds(first, size)], r_za.at[i, 0])
            total(mine, [*sources, za1], first, first + size)
            total(mine, sources, *((half_a, NA), (0, half_a))[i])
            send(mine, za2.at[i, 0], s_za.at[i, 1], r_za.at[i, 1], z_next[i])
        elif oz != 0:
            i = 0 if oz < 4 else 1
            step = 4 - oz if i == 0 else oz - 4
            wait_for(za2.at[i, step - 2], r_za.at[i, step - 1])
            total(mine, [*sources, za2.at[i, step - 2]], 0, NA)
            send(mine, za2.at[i, step - 1], s_za.at[i, step], r_za.at[i, step], z_next[i])
        else:
            for i in range(2):
                wait_for(za2.at[i, 2], r_za.at[i, 3])
            result(0, [*sources, za2.at[0, 2], za2.at[1, 2]], NA)

    def b_far(k):
        for i in range(2):
            xx = at_x(FAR_Z[i][k])
            wait_for(rb.at[4, xx], r_b4.at[FAR_Z[i][k]])
            total(pb.at[4, xx], from_b(4, xx), 0, NB)
            send(pb.at[4, xx], zb1.at[i, k], s_zb1.at[i, k], r_zb1.at[i, k], z_next[i])

    def b_near(step, j):
        ox = NEAR_Z[j]
        xx = at_x(ox)
        for i, d in enumerate((4 - step, 4 + step)):
            sources = from_b(d, xx)
            if step > 1:
                wait_for(zb2.at[i, step - 2, j], r_zb2.at[i, step - 2, j])
                sources.append(zb2.at[i, step - 2, j])
            elif ox in FAR_Z[i]:
                k = FAR_Z[i].index(ox)
                wait_for(zb1.at[i, k], r_zb1.at[i, k])
                sources.append(zb1.at[i, k])
            total(pb.at[d, xx], sources, 0, NB)
            send(
                pb.at[d, xx], zb2.at[i, step - 1, j], s_zb2.at[i, step - 1, j], r_zb2.at[i, step - 1, j], z_next[i]
            )

    def b_own(ox):
        j = NEAR_Z.index(ox)
        xx = at_x(ox)
        for i in range(2):
            wait_for(zb2.at[i, 2, j], r_zb2.at[i, 2, j])
        sources = [*from_b(0, xx), zb2.at[0, 2, j], zb2.at[1, 2, j]]
        mine = pb.at[0, xx]
        halves = ((0, half_b), (half_b, NB - half_b))
        if ox == 2:
            total(mine, sources, 0, NB)
            for i, (first, size) in enumerate(halves):
                piece = xb1.at[pl.ds(first, size)]
                send(mine.at[pl.ds(first, size)], piece, s_xb.at[i, 0], r_xb.at[i, 0], x_next[i])
        elif ox != 0:
            i = (1, 3).index(ox)
            first, size = halves[i]
            wait_for(xb1.at[pl.ds(first, size)], r_xb.at[i, 0])
            total(mine, [*sources, xb1], first, first + size)
            total(mine, sources, *((half_b, NB), (0, half_b))[i])
            send(mine, xb2.at[i], s_xb.at[i, 1], r_xb.at[i, 1], x_next[i])
        else:
            for i in range(2):
                wait_for(xb2.at[i], r_xb.at[i, 1])
            result(NA, [*sources, xb2.at[0], xb2.at[1]], NB)

    events = [(5.0, b_far, (k,)) for k in range(2)] + [(5.1, a_far, (k,)) for k in range(4)]
    for j in range(8):
        events.append((8.3 + 1.65 * (j // 2), a_near, (j,)))
    for oz, when in ((4, 14.9), (5, 18.2), (3, 18.2), (6, 21.5), (2, 21.6), (7, 24.9), (1, 24.9), (0, 28.2)):
        events.append((when, a_own, (oz,)))
    for j in range(4):
        for step, when in ((1, min(7.7 + j, 8.7)), (2, 10.4 + j), (3, 13.1 + j)):
            events.append((when, b_near, (step, j)))
    for ox, when in ((2, 18.6), (1, 23.0), (3, 23.1), (0, 28.5)):
        events.append((when, b_own, (ox,)))
    for _, act, args in sorted(events, key=lambda e: e[0]):
        while len(pending) > 30:
            pending.pop(0).wait_send()
        act(*args)
    for cp in pending:
        cp.wait_send()


def gather(part):
    vmem = pl.BlockSpec(memory_space=pltpu.VMEM)
    dma = pltpu.SemaphoreType.DMA
    return pl.pallas_call(
        gather_kernel,
        out_shape=jax.ShapeDtypeStruct((LM, FLUX_DEV * B), F32),
        in_specs=[vmem],
        out_specs=vmem,
        scratch_shapes=[
            pltpu.VMEM((NX, NZ, NA, LM, B), BF16),
            pltpu.VMEM((NZ, NX, NB, LM, B), BF16),
            pltpu.VMEM((NX, NZ, NA, LM, B), BF16),
            pltpu.VMEM((NZ, NX, NB, LM, B), BF16),
            pltpu.VMEM((2, 4, NA, LM, B), BF16),
            pltpu.VMEM((2, NZ, NA, LM, B), BF16),
            pltpu.VMEM((2, 2, NB, LM, B), BF16),
            pltpu.VMEM((2, 3, NX, NB, LM, B), BF16),
            pltpu.VMEM((NA, LM, B), BF16),
            pltpu.VMEM((2, 3, NA, LM, B), BF16),
            pltpu.VMEM((NB, LM, B), BF16),
            pltpu.VMEM((2, NB, LM, B), BF16),
            dma((NX,)), dma((NX,)), dma((NZ,)), dma((NZ,)), dma((NZ,)), dma((NZ,)), dma((NX,)), dma((NX,)),
            dma((2, 4)), dma((2, 4)), dma((2, NZ)), dma((2, NZ)),
            dma((2, 2)), dma((2, 2)), dma((2, 3, NX)), dma((2, 3, NX)),
            dma((2, 4)), dma((2, 4)), dma((2, 2)), dma((2, 2)),
        ],
        compiler_params=pltpu.CompilerParams(
            collective_id=1, has_side_effects=True, vmem_limit_bytes=18 * 2**20
        ),
        name="gather",
    )(part.reshape(NZ, NX, 2, FLUX_DEV, LM, B))


def body(footprints, tile_row, tile_col, prior_flux, observed, precision_weight):
    pin = functools.partial(pltpu.with_memory_space_constraint, memory_space=pltpu.HBM)
    footprints, prior_flux, observed = pin(footprints), pin(prior_flux), pin(observed)
    tile_row, tile_col = pin(tile_row.reshape(1, B)), pin(tile_col.reshape(1, B))
    tiles, anoms, codes = spread(tile_row, tile_col, footprints, prior_flux)
    weight = pin(precision_weight.reshape(SOUND_DEV, 1, B))
    part = local(codes, tiles, anoms, observed, weight)
    return gather(part)


def solution(mesh):
    in_specs = (
        P("tile", None, None),
        P("tile"),
        P("tile"),
        P("mem", "tile"),
        P("mem", "tile"),
        P("tile"),
    )
    out_specs = P("mem", "tile")
    return jax.shard_map(body, mesh=mesh, in_specs=in_specs, out_specs=out_specs, check_vma=False)
```

```python
import functools

import jax
import jax.numpy as jnp
from jax import lax
from jax.experimental import pallas as pl
from jax.experimental.pallas import tpu as pltpu
from jax.sharding import PartitionSpec as P

MEMBERS = 256
FLUX_DEV = 8
SOUND_DEV = 16
NZ, NX, NY, NT = 8, 4, 4, 64
CAP = 3
B = 128
LM = 64
MESH = pl.DeviceIdType.MESH
F32, BF16 = jnp.float32, jnp.bfloat16


def route(row, col):
    shape = (B, B)
    down, across = lax.broadcasted_iota(jnp.int32, shape, 0), lax.broadcasted_iota(jnp.int32, shape, 1)

    def column(v):
        return jnp.sum(jnp.where(down == across, v, 0), axis=1, keepdims=True)

    owner = row // SOUND_DEV
    earlier = (column(owner) == owner) & (down < across)
    place = jnp.sum(earlier.astype(jnp.int32), axis=0, keepdims=True)
    slot = column(owner * CAP + place)
    index = lax.broadcasted_iota(jnp.int32, (B, 2 * B), 0)
    at = lax.broadcasted_iota(jnp.int32, (B, 2 * B), 1)
    source = jnp.sum(jnp.where(slot == at, index, 0), axis=0, keepdims=True)
    blocks = (row - owner * SOUND_DEV) * 512 + col - SOUND_DEV * 512
    mine = lax.broadcasted_iota(jnp.int32, (NT, B), 0) == owner
    lane = lax.broadcasted_iota(jnp.int32, (NT, B), 1)
    coded = jnp.full((NT, B), SOUND_DEV * 512, jnp.int32)
    for k in range(CAP):
        found = jnp.sum(jnp.where(mine & (place == k), blocks, 0), axis=1, keepdims=True)
        coded = coded + jnp.where(lane == k, found, 0)
    return source, coded


SPREAD_ORDER = (
    ("T", 0), ("T", 1), ("T", 7), ("A0",), ("T", 2), ("T", 6), ("Y1", 0), ("Y1", 1), ("Y1", 7), ("Y2", 0, 0),
    ("Y2", 1, 0), ("Z", 0, 1), ("X", 0, 0), ("X", 1, 0), ("Z", 1, 1), ("Y2", 0, 1), ("Y2", 1, 1), ("T", 3),
    ("T", 5), ("X", 0, 7), ("X", 1, 7), ("Y2", 0, 7), ("Y2", 1, 7), ("Y1", 2), ("Y1", 6), ("XL", 0),
    ("Z", 0, 2), ("X", 0, 1), ("X", 1, 1), ("Z", 1, 2), ("T", 4), ("XL", 7), ("Y2", 0, 2), ("Y2", 1, 2),
    ("X", 0, 6), ("X", 1, 6), ("XL", 1), ("Y2", 0, 6), ("Y2", 1, 6), ("X", 0, 2), ("X", 1, 2), ("Y1", 3),
    ("Y1", 5), ("Z", 0, 3), ("Z", 1, 3), ("XL", 6), ("XL", 2), ("Y2", 0, 3), ("Y2", 1, 3), ("X", 0, 5),
    ("X", 1, 5), ("X", 0, 3), ("X", 1, 3), ("Y2", 0, 5), ("Y2", 1, 5), ("Y1", 4), ("Z", 0, 4), ("XL", 5),
    ("XL", 3), ("X", 0, 4), ("X", 1, 4), ("Y2", 0, 4), ("Y2", 1, 4), ("XL", 4),
)


def spread_kernel(
    row_h, col_h, footprints, prior_h, tiles, anoms, codes,
    row, col, source_v, source, coded, prior, quarter, staged, sums, shard,
    s_row, s_fp, s_prior, s_sum, r_sum, s_tile, r_tile, s_code, r_code, s_y, r_y, s_y2, r_y2,
    s_local, s_z, r_z, s_x, r_x, s_x2, r_x2, s_sib, r_sib, came,
):
    me = lax.axis_index("tile")
    q = lax.axis_index("mem")
    core = lax.rem(me, 2)
    x = lax.rem(me // 2, NX)
    z = me // 8

    def at_z(o):
        return lax.rem(z + o + NZ, NZ)

    def at_x(o):
        return lax.rem(x + o + NX, NX)

    def at_y(o):
        return lax.rem(q + o + NY, NY)

    def index(zz, xx, cc):
        return zz * 8 + xx * 2 + cc

    def remote(src, dst, ssem, rsem, tile=None, mem=None):
        return pltpu.make_async_remote_copy(
            src_ref=src, dst_ref=dst, send_sem=ssem, recv_sem=rsem,
            device_id={"tile": me if tile is None else tile, "mem": q if mem is None else mem},
            device_id_type=MESH,
        )

    def wait_for(ref, sem):
        pltpu.make_async_copy(ref, ref, sem).wait()

    row_copy = pltpu.make_async_copy(row_h, row, s_row.at[0])
    row_copy.start()
    col_copy = pltpu.make_async_copy(col_h, col, s_row.at[1])
    col_copy.start()
    prior_copy = pltpu.make_async_copy(prior_h, prior, s_prior)
    prior_copy.start()
    fp_copy = pltpu.make_async_copy(
        footprints.at[:, pl.ds(pl.multiple_of(q * 32, 32), 32), :], quarter, s_fp
    )
    fp_copy.start()

    barrier = pltpu.get_barrier_semaphore()
    for o in range(1, 8):
        pl.semaphore_signal(
            barrier, inc=1, device_id={"tile": z * 8 + lax.rem(me + o, 8), "mem": q}, device_id_type=MESH
        )
    for o in range(1, NY):
        pl.semaphore_signal(barrier, inc=1, device_id={"tile": me, "mem": at_y(o)}, device_id_type=MESH)
    for o in (1, -1):
        pl.semaphore_signal(
            barrier, inc=1, device_id={"tile": index(at_z(o), x, core), "mem": q}, device_id_type=MESH
        )

    def tell(stage):
        for i, o in enumerate((1, -1)):
            pl.semaphore_signal(
                came.at[i, stage], inc=1, device_id={"tile": index(at_z(o), x, core), "mem": q}, device_id_type=MESH
            )

    def hear(stage):
        for i in range(2):
            pl.semaphore_wait(came.at[i, stage], 1)

    row_copy.wait()
    col_copy.wait()
    source_row, coded_rows = route(row[...], col[...])
    source_v[...] = source_row
    source_copy = pltpu.make_async_copy(source_v, source, s_row.at[2])
    source_copy.start()
    for t in range(NT):
        coded[t] = coded_rows[t : t + 1]
    prior_copy.wait()
    for j in range(FLUX_DEV):
        part = jnp.sum(prior[:, j * B : (j + 1) * B].astype(F32), axis=0, keepdims=True)
        sums[0, j : j + 1, :] = part
    pl.semaphore_wait(barrier, 7 + NY - 1 + 2)
    tell(1)

    sum_sends = []
    for o in range(1, NY):
        cp = remote(sums.at[0], sums.at[o], s_sum.at[o], r_sum.at[o], mem=at_y(o))
        cp.start()
        sum_sends.append(cp)
    fp_copy.wait()
    source_copy.wait()

    def send_tiles(dz):
        first = 1 if dz == 0 else 0
        if 1 <= dz <= 4:
            hear(dz)
            if dz < 4:
                tell(dz + 1)

        @pl.loop(first, 8)
        def _(o):
            t = at_z(dz) * 8 + lax.rem(me + o, 8)
            for s in range(CAP):
                staged[t, s] = quarter[source[0, t * CAP + s]]
            remote(staged.at[t], tiles.at[q, me], s_tile, r_tile.at[dz], tile=t).start()
            remote(coded.at[t], codes.at[me], s_code, r_code, tile=t).start()

        if dz == 0:
            for s in range(CAP):
                staged[me, s] = quarter[source[0, me * CAP + s]]
            pltpu.make_async_copy(staged.at[me], tiles.at[q, me], r_tile.at[0]).start()
            pltpu.make_async_copy(coded.at[me], codes.at[me], r_code).start()

    def group(quarter_index, dz, first=0, size=8):
        zs = at_z(-dz)
        return tiles.at[quarter_index, pl.ds(zs * 8 + first, size)]

    pending = []

    def go(cp):
        cp.start()
        pending.append(cp)

    def y_first(dz):
        wait_for(group(q, dz), r_tile.at[dz])
        for late in range(2):
            for i, to in enumerate((1, -1)):
                h = (i + late) % 2
                half = group(q, dz, 4 * h, 4)
                go(remote(half, half, s_y.at[i, h, dz], r_y.at[i, h, dz], mem=at_y(to)))

    def y_second(i, dz):
        from_, to = ((-1, 1), (1, -1))[i]
        half = group(at_y(from_), dz, 4 * i, 4)
        wait_for(half, r_y.at[i, i, dz])
        go(remote(half, half, s_y2.at[i, dz], r_y2.at[i, dz], mem=at_y(to)))

    def y_last(dz):
        for i in range(2):
            wait_for(group(at_y((-1, 1)[i]), dz, 4 - 4 * i, 4), r_y.at[i, 1 - i, dz])
            wait_for(group(at_y(2), dz, 4 * i, 4), r_y2.at[i, dz])

    def block(oz, ox, own_core=True):
        return anoms.at[index(at_z(oz), at_x(ox), core if own_core else 1 - core)]

    def to_sibling(oz, ox):
        go(
            remote(
                block(oz, ox), block(oz, ox), s_sib.at[ox % NX, oz % NZ], r_sib.at[ox % NX, oz % NZ],
                tile=index(z, x, 1 - core),
            )
        )

    def x_first(oz, src=None):
        b = block(oz, 0)
        src = b if src is None else src
        k = oz % NZ
        for late in range(2):
            for i, to in enumerate((1, -1)):
                h = (i + late) % 2
                part = pl.ds(4 * h, 4)
                go(remote(src.at[part], b.at[part], s_x.at[i, h, k], r_x.at[i, h, k], tile=index(z, at_x(to), core)))
        go(remote(src, b, s_sib.at[0, k], r_sib.at[0, k], tile=index(z, x, 1 - core)))

    def x_second(i, oz):
        k = oz % NZ
        from_, to = ((-1, 1), (1, -1))[i]
        half = block(oz, from_).at[pl.ds(4 * i, 4)]
        wait_for(half, r_x.at[i, i, k])
        go(remote(half, half, s_x2.at[i, k], r_x2.at[i, k], tile=index(z, at_x(to), core)))

    def x_last(oz):
        k = oz % NZ
        for i, from_ in enumerate((-1, 1)):
            wait_for(block(oz, from_).at[pl.ds(4 - 4 * i, 4)], r_x.at[i, 1 - i, k])
            to_sibling(oz, from_)
        for i in range(2):
            wait_for(block(oz, 2).at[pl.ds(4 * i, 4)], r_x2.at[i, k])
        to_sibling(oz, 2)

    def z_step(i, k):
        if k < 4:
            b = block((-k, k)[i], 0)
            wait_for(b, r_z.at[i, k])
            h = b if k < 3 else b.at[pl.ds(4 * i, 4)]
            go(remote(h, h, s_z.at[i, k + 1], r_z.at[i, k + 1], tile=index(at_z((1, -1)[i]), x, core)))
            x_first((-k, k)[i])
        else:
            b = block(4, 0)
            wait_for(b.at[pl.ds(0, 4)], r_z.at[0, 4])
            wait_for(b.at[pl.ds(4, 4)], r_z.at[1, 4])
            x_first(4)

    own_copy = pltpu.make_async_copy(shard, anoms.at[me], s_local)

    def send_shard():
        for cp in sum_sends:
            cp.wait()
        mean = (sums[0] + sums[1] + sums[2] + sums[3]) / MEMBERS
        for j in range(FLUX_DEV):
            shard[j] = (prior[:, j * B : (j + 1) * B].astype(F32) - mean[j : j + 1, :]).astype(BF16)
        own_copy.start()
        go(remote(shard, anoms.at[me], s_z.at[0, 1], r_z.at[0, 1], tile=index(at_z(1), x, core)))
        go(remote(shard, anoms.at[me], s_z.at[1, 1], r_z.at[1, 1], tile=index(at_z(-1), x, core)))
        x_first(0, shard)

    acts = {
        "T": send_tiles, "A0": send_shard, "Z": z_step, "X": x_second, "XL": x_last, "Y1": y_first, "Y2": y_second
    }
    for name, *numbers in SPREAD_ORDER:
        while len(pending) > 40:
            pending.pop(0).wait_send()
        acts[name](*numbers)
    for dz in (0, 1, 7, 2, 6, 3, 5, 4):
        y_last(dz)
    for oz in (0, 1, 7, 2, 6, 3, 5, 4):
        for ox in range(NX):
            wait_for(block(oz, ox, False), r_sib.at[ox, oz])
    wait_for(codes, r_code)
    own_copy.wait()
    for cp in pending:
        cp.wait_send()
    wait_for(staged.at[pl.ds(0, NT - 1)], s_tile)
    wait_for(codes.at[pl.ds(0, NT - 1)], s_code)


def spread(tile_row, tile_col, footprints, prior):
    hbm = pl.BlockSpec(memory_space=pltpu.HBM)
    vmem = pl.BlockSpec(memory_space=pltpu.VMEM)
    dma = pltpu.SemaphoreType.DMA
    return pl.pallas_call(
        spread_kernel,
        out_shape=(
            jax.ShapeDtypeStruct((NY, NT, CAP, 32, B), BF16),
            jax.ShapeDtypeStruct((NT, FLUX_DEV, LM, B), BF16),
            jax.ShapeDtypeStruct((NT, 1, B), jnp.int32),
        ),
        in_specs=[hbm, hbm, hbm, hbm],
        out_specs=(vmem, vmem, vmem),
        scratch_shapes=[
            pltpu.VMEM((1, B), jnp.int32),
            pltpu.VMEM((1, B), jnp.int32),
            pltpu.VMEM((1, 2 * B), jnp.int32),
            pltpu.SMEM((1, 2 * B), jnp.int32),
            pltpu.VMEM((NT, 1, B), jnp.int32),
            pltpu.VMEM((LM, FLUX_DEV * B), BF16),
            pltpu.VMEM((B, 32, B), BF16),
            pltpu.VMEM((NT, CAP, 32, B), BF16),
            pltpu.VMEM((NY, FLUX_DEV, B), F32),
            pltpu.VMEM((FLUX_DEV, LM, B), BF16),
            dma((3,)), dma, dma, dma((NY,)), dma((NY,)), dma, dma((NZ,)), dma, dma,
            dma((2, 2, NZ)), dma((2, 2, NZ)), dma((2, NZ)), dma((2, NZ)),
            dma, dma((2, 5)), dma((2, 5)), dma((2, 2, NZ)), dma((2, 2, NZ)), dma((2, NZ)), dma((2, NZ)),
            dma((NX, NZ)), dma((NX, NZ)), pltpu.SemaphoreType.REGULAR((2, 5)),
        ],
        compiler_params=pltpu.CompilerParams(
            collective_id=0, has_side_effects=True, vmem_limit_bytes=16 * 2**20
        ),
        name="spread",
    )(tile_row, tile_col, footprints, prior)


def local_kernel(
    codes, tiles, anoms, observed_h, weight_h, out,
    observed, weight, modelled, weighted, total, s_obs, s_weight,
):
    observed_in = pltpu.make_async_copy(observed_h, observed, s_obs)
    observed_in.start()
    weight_in = pltpu.make_async_copy(weight_h, weight, s_weight)
    weight_in.start()
    modelled[...] = jnp.zeros_like(modelled)
    step = 16

    def fetch(i, o, s):
        src = i * step + o
        code = codes[src, 0, s]
        return tiles[:, src, s].reshape(B, B), code // 512, lax.rem(code, 512)

    @pl.loop(0, NT // step)
    def _(i):
        terms = []
        for o in range(step):
            for s in range(CAP):
                tile, row, col = fetch(i, o, s)
                term = lax.dot_general(
                    anoms[col], tile, (((1,), (1,)), ((), ())), preferred_element_type=F32
                )
                terms.append((row, term))
        total[pl.ds(i * 128, 128)] = jnp.zeros((128, LM, B), F32)
        for row, term in terms:
            modelled[row] += term

    observed_in.wait()
    weight_in.wait()
    for r in range(SOUND_DEV):
        factor = weight[r].astype(F32) / 8.0
        gap = modelled[r] - observed[:, r * B : (r + 1) * B]
        weighted[r] = (factor * gap).astype(BF16)
    weighted[SOUND_DEV] = jnp.zeros((LM, B), BF16)

    @pl.loop(0, NT // step)
    def _(i):
        terms = []
        for o in range(step):
            for s in range(CAP):
                tile, row, col = fetch(i, o, s)
                term = lax.dot_general(
                    weighted[row], tile, (((1,), (0,)), ((), ())), preferred_element_type=F32
                )
                terms.append((col, term))
        for col, term in terms:
            total[col] += term

    @pl.loop(0, NT)
    def _(i):
        out[pl.ds(i * 8, 8)] = total[pl.ds(i * 8, 8)].astype(BF16)


def local(codes, tiles, anoms, observed, weight):
    hbm = pl.BlockSpec(memory_space=pltpu.HBM)
    vmem = pl.BlockSpec(memory_space=pltpu.VMEM)
    dma = pltpu.SemaphoreType.DMA
    return pl.pallas_call(
        local_kernel,
        out_shape=jax.ShapeDtypeStruct((NT * FLUX_DEV, LM, B), BF16),
        in_specs=[pl.BlockSpec(memory_space=pltpu.SMEM), vmem, vmem, hbm, hbm],
        out_specs=vmem,
        scratch_shapes=[
            pltpu.VMEM((LM, SOUND_DEV * B), F32),
            pltpu.VMEM((SOUND_DEV, 1, B), jnp.int32),
            pltpu.VMEM((SOUND_DEV + 1, LM, B), F32),
            pltpu.VMEM((SOUND_DEV + 1, LM, B), BF16),
            pltpu.VMEM((NT * FLUX_DEV, LM, B), F32),
            dma, dma,
        ],
        compiler_params=pltpu.CompilerParams(vmem_limit_bytes=22 * 2**20),
        name="local",
    )(codes, tiles, anoms.reshape(NT * FLUX_DEV, LM, B), observed, weight)


NA = 5
NB = FLUX_DEV - NA
FAR_X = ((4, 3, 2, 1), (5, 6, 7, 0))
NEAR_X = (4, 5, 3, 6, 2, 7, 1, 0)
FAR_Z = ((2, 1), (3, 0))
NEAR_Z = (2, 1, 3, 0)


def gather_kernel(
    part, out,
    pa, pb, ra, rb, xa1, xa2, zb1, zb2, za1, za2, xb1, xb2,
    s_sib_a, r_sib_a, s_sib_b, r_sib_b, s_a2, r_a2, s_b4, r_b4,
    s_xa1, r_xa1, s_xa2, r_xa2, s_zb1, r_zb1, s_zb2, r_zb2, s_za, r_za, s_xb, r_xb,
):
    me = lax.axis_index("tile")
    q = lax.axis_index("mem")
    core = lax.rem(me, 2)
    x = lax.rem(me // 2, NX)
    z = me // 8

    def at_z(o):
        return lax.rem(z + o + NZ, NZ)

    def at_x(o):
        return lax.rem(x + o + NX, NX)

    def index(zz, xx, cc):
        return zz * 8 + xx * 2 + cc

    sibling = index(z, x, 1 - core)
    x_next = (index(z, at_x(1), core), index(z, at_x(-1), core))
    z_next = (index(at_z(1), x, core), index(at_z(-1), x, core))

    pending = []

    def send(src, dst, ssem, rsem, tile):
        cp = pltpu.make_async_remote_copy(
            src_ref=src, dst_ref=dst, send_sem=ssem, recv_sem=rsem,
            device_id={"tile": tile, "mem": q}, device_id_type=MESH,
        )
        cp.start()
        pending.append(cp)

    def wait_for(ref, sem):
        pltpu.make_async_copy(ref, ref, sem).wait()

    barrier = pltpu.get_barrier_semaphore()
    for t in (sibling, *x_next, *z_next):
        pl.semaphore_signal(barrier, inc=1, device_id={"tile": t, "mem": q}, device_id_type=MESH)
    pl.semaphore_wait(barrier, 5)

    for ox in NEAR_Z:
        xx = at_x(ox)
        send(part.at[at_z(4), xx, 1 - core, pl.ds(NA, NB)], rb.at[4, xx], s_b4.at[ox], r_b4.at[ox], sibling)
    for oz in NEAR_X:
        zz = at_z(oz)
        send(part.at[zz, at_x(2), 1 - core, pl.ds(0, NA)], ra.at[2, zz], s_a2.at[oz], r_a2.at[oz], sibling)
    for kind, d in (("b", 3), ("b", 5), ("a", 1), ("a", 3), ("b", 2), ("b", 6), ("b", 1), ("b", 7), ("a", 0), ("b", 0)):
        if kind == "a":
            send(part.at[:, at_x(d), 1 - core, pl.ds(0, NA)], ra.at[d], s_sib_a.at[d], r_sib_a.at[d], sibling)
        else:
            send(part.at[at_z(d), :, 1 - core, pl.ds(NA, NB)], rb.at[d], s_sib_b.at[d], r_sib_b.at[d], sibling)

    settled = set()

    def from_a(d, zz):
        if ("a", d) not in settled:
            settled.add(("a", d))
            if d != 2:
                wait_for(ra.at[d], r_sib_a.at[d])
        return [part.at[zz, at_x(d), core], ra.at[d, zz]]

    def from_b(d, xx):
        if ("b", d) not in settled:
            settled.add(("b", d))
            if d != 4:
                wait_for(rb.at[d], r_sib_b.at[d])
        return [part.at[at_z(d), xx, core, pl.ds(NA, NB)], rb.at[d, xx]]

    def total(dst, sources, first, last):
        @pl.loop(first, last)
        def _(b):
            value = None
            for s in sources:
                ref, start = s if isinstance(s, tuple) else (s, 0)
                v = ref[b - start].astype(F32)
                value = v if value is None else value + v
            dst[b] = value.astype(BF16)

    def result(base, sources, count):
        for b in range(count):
            value = None
            for s in sources:
                v = s[b].astype(F32)
                value = v if value is None else value + v
            out[:, (base + b) * B : (base + b + 1) * B] = value

    def a_far(k):
        for i in range(2):
            zz = at_z(FAR_X[i][k])
            wait_for(ra.at[2, zz], r_a2.at[FAR_X[i][k]])
            total(pa.at[2, zz], from_a(2, zz), 0, NA)
            send(pa.at[2, zz], xa1.at[i, k], s_xa1.at[i, k], r_xa1.at[i, k], x_next[i])

    def a_near(j):
        oz = NEAR_X[j]
        zz = at_z(oz)
        for i, d in enumerate((1, 3)):
            sources = from_a(d, zz)
            if oz in FAR_X[i]:
                k = FAR_X[i].index(oz)
                wait_for(xa1.at[i, k], r_xa1.at[i, k])
                sources.append(xa1.at[i, k])
            total(pa.at[d, zz], sources, 0, NA)
            send(pa.at[d, zz], xa2.at[i, j], s_xa2.at[i, j], r_xa2.at[i, j], x_next[i])

    half_a, half_b = (NA + 1) // 2, (NB + 1) // 2

    def a_own(oz):
        j = NEAR_X.index(oz)
        zz = at_z(oz)
        for i in range(2):
            wait_for(xa2.at[i, j], r_xa2.at[i, j])
        sources = [*from_a(0, zz), xa2.at[0, j], xa2.at[1, j]]
        mine = pa.at[0, zz]
        if oz == 4:
            total(mine, sources, 0, NA)
            for i, (first, size) in enumerate(((0, half_a), (half_a, NA - half_a))):
                piece = za1.at[pl.ds(first, size)]
                send(mine.at[pl.ds(first, size)], piece, s_za.at[i, 0], r_za.at[i, 0], z_next[i])
        elif oz in (3, 5):
            i = (3, 5).index(oz)
            first, size = ((0, half_a), (half_a, NA - half_a))[i]
            wait_for(za1.at[pl.ds(first, size)], r_za.at[i, 0])
            total(mine, [*sources, za1], first, first + size)
            total(mine, sources, *((half_a, NA), (0, half_a))[i])
            send(mine, za2.at[i, 0], s_za.at[i, 1], r_za.at[i, 1], z_next[i])
        elif oz != 0:
            i = 0 if oz < 4 else 1
            step = 4 - oz if i == 0 else oz - 4
            wait_for(za2.at[i, step - 2], r_za.at[i, step - 1])
            total(mine, [*sources, za2.at[i, step - 2]], 0, NA)
            send(mine, za2.at[i, step - 1], s_za.at[i, step], r_za.at[i, step], z_next[i])
        else:
            for i in range(2):
                wait_for(za2.at[i, 2], r_za.at[i, 3])
            result(0, [*sources, za2.at[0, 2], za2.at[1, 2]], NA)

    def b_far(k):
        for i in range(2):
            xx = at_x(FAR_Z[i][k])
            wait_for(rb.at[4, xx], r_b4.at[FAR_Z[i][k]])
            total(pb.at[4, xx], from_b(4, xx), 0, NB)
            send(pb.at[4, xx], zb1.at[i, k], s_zb1.at[i, k], r_zb1.at[i, k], z_next[i])

    def b_near(step, j):
        ox = NEAR_Z[j]
        xx = at_x(ox)
        for i, d in enumerate((4 - step, 4 + step)):
            sources = from_b(d, xx)
            if step > 1:
                wait_for(zb2.at[i, step - 2, j], r_zb2.at[i, step - 2, j])
                sources.append(zb2.at[i, step - 2, j])
            elif ox in FAR_Z[i]:
                k = FAR_Z[i].index(ox)
                wait_for(zb1.at[i, k], r_zb1.at[i, k])
                sources.append(zb1.at[i, k])
            total(pb.at[d, xx], sources, 0, NB)
            send(
                pb.at[d, xx], zb2.at[i, step - 1, j], s_zb2.at[i, step - 1, j], r_zb2.at[i, step - 1, j], z_next[i]
            )

    def b_own(ox):
        j = NEAR_Z.index(ox)
        xx = at_x(ox)
        for i in range(2):
            wait_for(zb2.at[i, 2, j], r_zb2.at[i, 2, j])
        sources = [*from_b(0, xx), zb2.at[0, 2, j], zb2.at[1, 2, j]]
        mine = pb.at[0, xx]
        halves = ((0, half_b), (half_b, NB - half_b))
        if ox == 2:
            total(mine, sources, 0, NB)
            for i, (first, size) in enumerate(halves):
                piece = xb1.at[pl.ds(first, size)]
                send(mine.at[pl.ds(first, size)], piece, s_xb.at[i, 0], r_xb.at[i, 0], x_next[i])
        elif ox != 0:
            i = (1, 3).index(ox)
            first, size = halves[i]
            wait_for(xb1.at[pl.ds(first, size)], r_xb.at[i, 0])
            total(mine, [*sources, xb1], first, first + size)
            total(mine, sources, *((half_b, NB), (0, half_b))[i])
            send(mine, xb2.at[i], s_xb.at[i, 1], r_xb.at[i, 1], x_next[i])
        else:
            for i in range(2):
                wait_for(xb2.at[i], r_xb.at[i, 1])
            result(NA, [*sources, xb2.at[0], xb2.at[1]], NB)

    events = [(5.0, b_far, (k,)) for k in range(2)] + [(5.1, a_far, (k,)) for k in range(4)]
    for j in range(8):
        events.append((8.3 + 1.65 * (j // 2), a_near, (j,)))
    for oz, when in ((4, 14.9), (5, 18.2), (3, 18.2), (6, 21.5), (2, 21.6), (7, 24.9), (1, 24.9), (0, 28.2)):
        events.append((when, a_own, (oz,)))
    for j in range(4):
        for step, when in ((1, min(7.7 + j, 8.7)), (2, 10.4 + j), (3, 13.1 + j)):
            events.append((when, b_near, (step, j)))
    for ox, when in ((2, 18.6), (1, 23.0), (3, 23.1), (0, 28.5)):
        events.append((when, b_own, (ox,)))
    for _, act, args in sorted(events, key=lambda e: e[0]):
        while len(pending) > 30:
            pending.pop(0).wait_send()
        act(*args)
    for cp in pending:
        cp.wait_send()


def gather(part):
    vmem = pl.BlockSpec(memory_space=pltpu.VMEM)
    dma = pltpu.SemaphoreType.DMA
    return pl.pallas_call(
        gather_kernel,
        out_shape=jax.ShapeDtypeStruct((LM, FLUX_DEV * B), F32),
        in_specs=[vmem],
        out_specs=vmem,
        scratch_shapes=[
            pltpu.VMEM((NX, NZ, NA, LM, B), BF16),
            pltpu.VMEM((NZ, NX, NB, LM, B), BF16),
            pltpu.VMEM((NX, NZ, NA, LM, B), BF16),
            pltpu.VMEM((NZ, NX, NB, LM, B), BF16),
            pltpu.VMEM((2, 4, NA, LM, B), BF16),
            pltpu.VMEM((2, NZ, NA, LM, B), BF16),
            pltpu.VMEM((2, 2, NB, LM, B), BF16),
            pltpu.VMEM((2, 3, NX, NB, LM, B), BF16),
            pltpu.VMEM((NA, LM, B), BF16),
            pltpu.VMEM((2, 3, NA, LM, B), BF16),
            pltpu.VMEM((NB, LM, B), BF16),
            pltpu.VMEM((2, NB, LM, B), BF16),
            dma((NX,)), dma((NX,)), dma((NZ,)), dma((NZ,)), dma((NZ,)), dma((NZ,)), dma((NX,)), dma((NX,)),
            dma((2, 4)), dma((2, 4)), dma((2, NZ)), dma((2, NZ)),
            dma((2, 2)), dma((2, 2)), dma((2, 3, NX)), dma((2, 3, NX)),
            dma((2, 4)), dma((2, 4)), dma((2, 2)), dma((2, 2)),
        ],
        compiler_params=pltpu.CompilerParams(
            collective_id=1, has_side_effects=True, vmem_limit_bytes=18 * 2**20
        ),
        name="gather",
    )(part.reshape(NZ, NX, 2, FLUX_DEV, LM, B))


def body(footprints, tile_row, tile_col, prior_flux, observed, precision_weight):
    pin = functools.partial(pltpu.with_memory_space_constraint, memory_space=pltpu.HBM)
    footprints, prior_flux, observed = pin(footprints), pin(prior_flux), pin(observed)
    tile_row, tile_col = pin(tile_row.reshape(1, B)), pin(tile_col.reshape(1, B))
    tiles, anoms, codes = spread(tile_row, tile_col, footprints, prior_flux)
    weight = pin(precision_weight.reshape(SOUND_DEV, 1, B))
    part = local(codes, tiles, anoms, observed, weight)
    return gather(part)


def solution(mesh):
    in_specs = (
        P("tile", None, None),
        P("tile"),
        P("tile"),
        P("mem", "tile"),
        P("mem", "tile"),
        P("tile"),
    )
    out_specs = P("mem", "tile")
    return jax.shard_map(body, mesh=mesh, in_specs=in_specs, out_specs=out_specs, check_vma=False)
```

```python
import functools

import jax
import jax.numpy as jnp
from jax import lax
from jax.experimental import pallas as pl
from jax.experimental.pallas import tpu as pltpu
from jax.sharding import PartitionSpec as P

MEMBERS = 256
FLUX_DEV = 8
SOUND_DEV = 16
NZ, NX, NY, NT = 8, 4, 4, 64
CAP = 3
B = 128
LM = 64
MESH = pl.DeviceIdType.MESH
F32, BF16 = jnp.float32, jnp.bfloat16


def route(row, col):
    shape = (B, B)
    down, across = lax.broadcasted_iota(jnp.int32, shape, 0), lax.broadcasted_iota(jnp.int32, shape, 1)

    def column(v):
        return jnp.sum(jnp.where(down == across, v, 0), axis=1, keepdims=True)

    owner = row // SOUND_DEV
    earlier = (column(owner) == owner) & (down < across)
    place = jnp.sum(earlier.astype(jnp.int32), axis=0, keepdims=True)
    slot = column(owner * CAP + place)
    index = lax.broadcasted_iota(jnp.int32, (B, 2 * B), 0)
    at = lax.broadcasted_iota(jnp.int32, (B, 2 * B), 1)
    source = jnp.sum(jnp.where(slot == at, index, 0), axis=0, keepdims=True)
    blocks = (row - owner * SOUND_DEV) * 512 + col - SOUND_DEV * 512
    mine = lax.broadcasted_iota(jnp.int32, (NT, B), 0) == owner
    lane = lax.broadcasted_iota(jnp.int32, (NT, B), 1)
    coded = jnp.full((NT, B), SOUND_DEV * 512, jnp.int32)
    for k in range(CAP):
        found = jnp.sum(jnp.where(mine & (place == k), blocks, 0), axis=1, keepdims=True)
        coded = coded + jnp.where(lane == k, found, 0)
    return source, coded


SPREAD_ORDER = (
    ("T", 0), ("T", 1), ("T", 7), ("A0",), ("T", 2), ("T", 6), ("Y1", 0), ("Y1", 1), ("Y1", 7), ("Y2", 0, 0),
    ("Y2", 1, 0), ("Z", 0, 1), ("X", 0, 0), ("X", 1, 0), ("Z", 1, 1), ("Y2", 0, 1), ("Y2", 1, 1), ("T", 3),
    ("T", 5), ("X", 0, 7), ("X", 1, 7), ("Y2", 0, 7), ("Y2", 1, 7), ("Y1", 2), ("Y1", 6), ("XL", 0),
    ("Z", 0, 2), ("X", 0, 1), ("X", 1, 1), ("Z", 1, 2), ("T", 4), ("XL", 7), ("Y2", 0, 2), ("Y2", 1, 2),
    ("X", 0, 6), ("X", 1, 6), ("XL", 1), ("Y2", 0, 6), ("Y2", 1, 6), ("X", 0, 2), ("X", 1, 2), ("Y1", 3),
    ("Y1", 5), ("Z", 0, 3), ("Z", 1, 3), ("XL", 6), ("XL", 2), ("Y2", 0, 3), ("Y2", 1, 3), ("X", 0, 5),
    ("X", 1, 5), ("X", 0, 3), ("X", 1, 3), ("Y2", 0, 5), ("Y2", 1, 5), ("Y1", 4), ("Z", 0, 4), ("XL", 5),
    ("XL", 3), ("X", 0, 4), ("X", 1, 4), ("Y2", 0, 4), ("Y2", 1, 4), ("XL", 4),
)


def spread_kernel(
    row_h, col_h, footprints, prior_h, tiles, anoms, codes,
    row, col, source_v, source, coded, prior, quarter, staged, sums, shard,
    s_row, s_fp, s_prior, s_sum, r_sum, s_tile, r_tile, s_code, r_code, s_y, r_y, s_y2, r_y2,
    s_local, s_z, r_z, s_x, r_x, s_x2, r_x2, s_sib, r_sib, came,
):
    me = lax.axis_index("tile")
    q = lax.axis_index("mem")
    core = lax.rem(me, 2)
    x = lax.rem(me // 2, NX)
    z = me // 8

    def at_z(o):
        return lax.rem(z + o + NZ, NZ)

    def at_x(o):
        return lax.rem(x + o + NX, NX)

    def at_y(o):
        return lax.rem(q + o + NY, NY)

    def index(zz, xx, cc):
        return zz * 8 + xx * 2 + cc

    def remote(src, dst, ssem, rsem, tile=None, mem=None):
        return pltpu.make_async_remote_copy(
            src_ref=src, dst_ref=dst, send_sem=ssem, recv_sem=rsem,
            device_id={"tile": me if tile is None else tile, "mem": q if mem is None else mem},
            device_id_type=MESH,
        )

    def wait_for(ref, sem):
        pltpu.make_async_copy(ref, ref, sem).wait()

    row_copy = pltpu.make_async_copy(row_h, row, s_row.at[0])
    row_copy.start()
    col_copy = pltpu.make_async_copy(col_h, col, s_row.at[1])
    col_copy.start()
    prior_copy = pltpu.make_async_copy(prior_h, prior, s_prior)
    prior_copy.start()
    fp_copy = pltpu.make_async_copy(
        footprints.at[:, pl.ds(pl.multiple_of(q * 32, 32), 32), :], quarter, s_fp
    )
    fp_copy.start()

    barrier = pltpu.get_barrier_semaphore()
    for o in range(1, 8):
        pl.semaphore_signal(
            barrier, inc=1, device_id={"tile": z * 8 + lax.rem(me + o, 8), "mem": q}, device_id_type=MESH
        )
    for o in range(1, NY):
        pl.semaphore_signal(barrier, inc=1, device_id={"tile": me, "mem": at_y(o)}, device_id_type=MESH)
    for o in (1, -1):
        pl.semaphore_signal(
            barrier, inc=1, device_id={"tile": index(at_z(o), x, core), "mem": q}, device_id_type=MESH
        )

    def tell(stage):
        for i, o in enumerate((1, -1)):
            pl.semaphore_signal(
                came.at[i, stage], inc=1, device_id={"tile": index(at_z(o), x, core), "mem": q}, device_id_type=MESH
            )

    def hear(stage):
        for i in range(2):
            pl.semaphore_wait(came.at[i, stage], 1)

    row_copy.wait()
    col_copy.wait()
    source_row, coded_rows = route(row[...], col[...])
    source_v[...] = source_row
    source_copy = pltpu.make_async_copy(source_v, source, s_row.at[2])
    source_copy.start()
    for t in range(NT):
        coded[t] = coded_rows[t : t + 1]
    prior_copy.wait()
    for j in range(FLUX_DEV):
        part = jnp.sum(prior[:, j * B : (j + 1) * B].astype(F32), axis=0, keepdims=True)
        sums[0, j : j + 1, :] = part
    pl.semaphore_wait(barrier, 7 + NY - 1 + 2)
    tell(1)

    sum_sends = []
    for o in range(1, NY):
        cp = remote(sums.at[0], sums.at[o], s_sum.at[o], r_sum.at[o], mem=at_y(o))
        cp.start()
        sum_sends.append(cp)
    fp_copy.wait()
    source_copy.wait()

    def send_tiles(dz):
        first = 1 if dz == 0 else 0
        if 1 <= dz <= 4:
            hear(dz)
            if dz < 4:
                tell(dz + 1)

        @pl.loop(first, 8)
        def _(o):
            t = at_z(dz) * 8 + lax.rem(me + o, 8)
            for s in range(CAP):
                staged[t, s] = quarter[source[0, t * CAP + s]]
            remote(staged.at[t], tiles.at[q, me], s_tile, r_tile.at[dz], tile=t).start()
            remote(coded.at[t], codes.at[me], s_code, r_code, tile=t).start()

        if dz == 0:
            for s in range(CAP):
                staged[me, s] = quarter[source[0, me * CAP + s]]
            pltpu.make_async_copy(staged.at[me], tiles.at[q, me], r_tile.at[0]).start()
            pltpu.make_async_copy(coded.at[me], codes.at[me], r_code).start()

    def group(quarter_index, dz, first=0, size=8):
        zs = at_z(-dz)
        return tiles.at[quarter_index, pl.ds(zs * 8 + first, size)]

    pending = []

    def go(cp):
        cp.start()
        pending.append(cp)

    def y_first(dz):
        wait_for(group(q, dz), r_tile.at[dz])
        for late in range(2):
            for i, to in enumerate((1, -1)):
                h = (i + late) % 2
                half = group(q, dz, 4 * h, 4)
                go(remote(half, half, s_y.at[i, h, dz], r_y.at[i, h, dz], mem=at_y(to)))

    def y_second(i, dz):
        from_, to = ((-1, 1), (1, -1))[i]
        half = group(at_y(from_), dz, 4 * i, 4)
        wait_for(half, r_y.at[i, i, dz])
        go(remote(half, half, s_y2.at[i, dz], r_y2.at[i, dz], mem=at_y(to)))

    def y_last(dz):
        for i in range(2):
            wait_for(group(at_y((-1, 1)[i]), dz, 4 - 4 * i, 4), r_y.at[i, 1 - i, dz])
            wait_for(group(at_y(2), dz, 4 * i, 4), r_y2.at[i, dz])

    def block(oz, ox, own_core=True):
        return anoms.at[index(at_z(oz), at_x(ox), core if own_core else 1 - core)]

    def to_sibling(oz, ox):
        go(
            remote(
                block(oz, ox), block(oz, ox), s_sib.at[ox % NX, oz % NZ], r_sib.at[ox % NX, oz % NZ],
                tile=index(z, x, 1 - core),
            )
        )

    def x_first(oz, src=None):
        b = block(oz, 0)
        src = b if src is None else src
        k = oz % NZ
        for late in range(2):
            for i, to in enumerate((1, -1)):
                h = (i + late) % 2
                part = pl.ds(4 * h, 4)
                go(remote(src.at[part], b.at[part], s_x.at[i, h, k], r_x.at[i, h, k], tile=index(z, at_x(to), core)))
        go(remote(src, b, s_sib.at[0, k], r_sib.at[0, k], tile=index(z, x, 1 - core)))

    def x_second(i, oz):
        k = oz % NZ
        from_, to = ((-1, 1), (1, -1))[i]
        half = block(oz, from_).at[pl.ds(4 * i, 4)]
        wait_for(half, r_x.at[i, i, k])
        go(remote(half, half, s_x2.at[i, k], r_x2.at[i, k], tile=index(z, at_x(to), core)))

    def x_last(oz):
        k = oz % NZ
        for i, from_ in enumerate((-1, 1)):
            wait_for(block(oz, from_).at[pl.ds(4 - 4 * i, 4)], r_x.at[i, 1 - i, k])
            to_sibling(oz, from_)
        for i in range(2):
            wait_for(block(oz, 2).at[pl.ds(4 * i, 4)], r_x2.at[i, k])
        to_sibling(oz, 2)

    def z_step(i, k):
        if k < 4:
            b = block((-k, k)[i], 0)
            wait_for(b, r_z.at[i, k])
            h = b if k < 3 else b.at[pl.ds(4 * i, 4)]
            go(remote(h, h, s_z.at[i, k + 1], r_z.at[i, k + 1], tile=index(at_z((1, -1)[i]), x, core)))
            x_first((-k, k)[i])
        else:
            b = block(4, 0)
            wait_for(b.at[pl.ds(0, 4)], r_z.at[0, 4])
            wait_for(b.at[pl.ds(4, 4)], r_z.at[1, 4])
            x_first(4)

    own_copy = pltpu.make_async_copy(shard, anoms.at[me], s_local)

    def send_shard():
        for cp in sum_sends:
            cp.wait()
        mean = (sums[0] + sums[1] + sums[2] + sums[3]) / MEMBERS
        for j in range(FLUX_DEV):
            shard[j] = (prior[:, j * B : (j + 1) * B].astype(F32) - mean[j : j + 1, :]).astype(BF16)
        own_copy.start()
        go(remote(shard, anoms.at[me], s_z.at[0, 1], r_z.at[0, 1], tile=index(at_z(1), x, core)))
        go(remote(shard, anoms.at[me], s_z.at[1, 1], r_z.at[1, 1], tile=index(at_z(-1), x, core)))
        x_first(0, shard)

    acts = {
        "T": send_tiles, "A0": send_shard, "Z": z_step, "X": x_second, "XL": x_last, "Y1": y_first, "Y2": y_second
    }
    for name, *numbers in SPREAD_ORDER:
        while len(pending) > 40:
            pending.pop(0).wait_send()
        acts[name](*numbers)
    for dz in (0, 1, 7, 2, 6, 3, 5, 4):
        y_last(dz)
    for oz in (0, 1, 7, 2, 6, 3, 5, 4):
        for ox in range(NX):
            wait_for(block(oz, ox, False), r_sib.at[ox, oz])
    wait_for(codes, r_code)
    own_copy.wait()
    for cp in pending:
        cp.wait_send()
    wait_for(staged.at[pl.ds(0, NT - 1)], s_tile)
    wait_for(codes.at[pl.ds(0, NT - 1)], s_code)


def spread(tile_row, tile_col, footprints, prior):
    hbm = pl.BlockSpec(memory_space=pltpu.HBM)
    vmem = pl.BlockSpec(memory_space=pltpu.VMEM)
    dma = pltpu.SemaphoreType.DMA
    return pl.pallas_call(
        spread_kernel,
        out_shape=(
            jax.ShapeDtypeStruct((NY, NT, CAP, 32, B), BF16),
            jax.ShapeDtypeStruct((NT, FLUX_DEV, LM, B), BF16),
            jax.ShapeDtypeStruct((NT, 1, B), jnp.int32),
        ),
        in_specs=[hbm, hbm, hbm, hbm],
        out_specs=(vmem, vmem, vmem),
        scratch_shapes=[
            pltpu.VMEM((1, B), jnp.int32),
            pltpu.VMEM((1, B), jnp.int32),
            pltpu.VMEM((1, 2 * B), jnp.int32),
            pltpu.SMEM((1, 2 * B), jnp.int32),
            pltpu.VMEM((NT, 1, B), jnp.int32),
            pltpu.VMEM((LM, FLUX_DEV * B), BF16),
            pltpu.VMEM((B, 32, B), BF16),
            pltpu.VMEM((NT, CAP, 32, B), BF16),
            pltpu.VMEM((NY, FLUX_DEV, B), F32),
            pltpu.VMEM((FLUX_DEV, LM, B), BF16),
            dma((3,)), dma, dma, dma((NY,)), dma((NY,)), dma, dma((NZ,)), dma, dma,
            dma((2, 2, NZ)), dma((2, 2, NZ)), dma((2, NZ)), dma((2, NZ)),
            dma, dma((2, 5)), dma((2, 5)), dma((2, 2, NZ)), dma((2, 2, NZ)), dma((2, NZ)), dma((2, NZ)),
            dma((NX, NZ)), dma((NX, NZ)), pltpu.SemaphoreType.REGULAR((2, 5)),
        ],
        compiler_params=pltpu.CompilerParams(
            collective_id=0, has_side_effects=True, vmem_limit_bytes=16 * 2**20
        ),
        name="spread",
    )(tile_row, tile_col, footprints, prior)


def local_kernel(
    codes_v, tiles, anoms, observed_h, weight_h, out,
    codes, s_codes, observed, weight, modelled, weighted, total, s_obs, s_weight,
):
    codes_in = pltpu.make_async_copy(codes_v, codes, s_codes)
    codes_in.start()
    observed_in = pltpu.make_async_copy(observed_h, observed, s_obs)
    observed_in.start()
    weight_in = pltpu.make_async_copy(weight_h, weight, s_weight)
    weight_in.start()
    modelled[...] = jnp.zeros_like(modelled)

    @pl.loop(0, NT)
    def _(i):
        total[pl.ds(i * 8, 8)] = jnp.zeros((8, LM, B), F32)

    codes_in.wait()
    step = 32

    def fetch(i, o, s):
        src = i * step + o
        code = codes[src, 0, s]
        return tiles[:, src, s].reshape(B, B), code // 512, lax.rem(code, 512)

    @pl.loop(0, NT // step)
    def _(i):
        terms = []
        for o in range(step):
            for s in range(CAP):
                tile, row, col = fetch(i, o, s)
                term = lax.dot_general(
                    anoms[col], tile, (((1,), (1,)), ((), ())), preferred_element_type=F32
                )
                terms.append((row, term))
        for row, term in terms:
            modelled[row] += term

    observed_in.wait()
    weight_in.wait()
    for r in range(SOUND_DEV):
        factor = weight[r].astype(F32) / 8.0
        gap = modelled[r] - observed[:, r * B : (r + 1) * B]
        weighted[r] = (factor * gap).astype(BF16)
    weighted[SOUND_DEV] = jnp.zeros((LM, B), BF16)

    @pl.loop(0, NT // step)
    def _(i):
        terms = []
        for o in range(step):
            for s in range(CAP):
                tile, row, col = fetch(i, o, s)
                term = lax.dot_general(
                    weighted[row], tile, (((1,), (0,)), ((), ())), preferred_element_type=F32
                )
                terms.append((col, term))
        for col, term in terms:
            total[col] += term

    @pl.loop(0, NT)
    def _(i):
        out[pl.ds(i * 8, 8)] = total[pl.ds(i * 8, 8)].astype(BF16)


def local(codes, tiles, anoms, observed, weight):
    hbm = pl.BlockSpec(memory_space=pltpu.HBM)
    vmem = pl.BlockSpec(memory_space=pltpu.VMEM)
    dma = pltpu.SemaphoreType.DMA
    return pl.pallas_call(
        local_kernel,
        out_shape=jax.ShapeDtypeStruct((NT * FLUX_DEV, LM, B), BF16),
        in_specs=[vmem, vmem, vmem, hbm, hbm],
        out_specs=vmem,
        scratch_shapes=[
            pltpu.SMEM((NT, 1, B), jnp.int32),
            dma,
            pltpu.VMEM((LM, SOUND_DEV * B), F32),
            pltpu.VMEM((SOUND_DEV, 1, B), jnp.int32),
            pltpu.VMEM((SOUND_DEV + 1, LM, B), F32),
            pltpu.VMEM((SOUND_DEV + 1, LM, B), BF16),
            pltpu.VMEM((NT * FLUX_DEV, LM, B), F32),
            dma, dma,
        ],
        compiler_params=pltpu.CompilerParams(vmem_limit_bytes=22 * 2**20),
        name="local",
    )(codes, tiles, anoms.reshape(NT * FLUX_DEV, LM, B), observed, weight)


NA = 5
NB = FLUX_DEV - NA
FAR_X = ((4, 3, 2, 1), (5, 6, 7, 0))
NEAR_X = (4, 5, 3, 6, 2, 7, 1, 0)
FAR_Z = ((2, 1), (3, 0))
NEAR_Z = (2, 1, 3, 0)

GATHER_ORDER = (
    ("b_far", 0), ("b_far", 1), ("a_far", 0), ("a_far", 1), ("a_far", 2), ("a_far", 3), ("b_near", 1, 0),
    ("b_near", 1, 2), ("a_near", 0), ("b_near", 1, 1), ("b_near", 1, 3), ("a_near", 1), ("b_near", 2, 0),
    ("b_near", 2, 2), ("a_near", 2), ("b_near", 2, 1), ("a_near", 3), ("b_near", 2, 3), ("b_near", 3, 0),
    ("a_own", 4), ("a_near", 4), ("b_near", 3, 1), ("a_near", 5), ("b_near", 3, 2), ("b_own", 2),
    ("a_own", 5), ("a_own", 3), ("a_near", 6), ("b_near", 3, 3), ("a_near", 7), ("a_own", 6), ("a_own", 2),
    ("b_own", 3), ("b_own", 1), ("a_own", 7), ("a_own", 1), ("b_own", 0), ("a_own", 0),
)


def gather_kernel(
    part, out,
    pa, pb, ra, rb, xa1, xa2, zb1, zb2, za1, za2, xb1, xb2,
    s_sib_a, r_sib_a, s_sib_b, r_sib_b, s_a2, r_a2, s_b4, r_b4,
    s_xa1, r_xa1, s_xa2, r_xa2, s_zb1, r_zb1, s_zb2, r_zb2, s_za, r_za, s_xb, r_xb,
):
    me = lax.axis_index("tile")
    q = lax.axis_index("mem")
    core = lax.rem(me, 2)
    x = lax.rem(me // 2, NX)
    z = me // 8

    def at_z(o):
        return lax.rem(z + o + NZ, NZ)

    def at_x(o):
        return lax.rem(x + o + NX, NX)

    def index(zz, xx, cc):
        return zz * 8 + xx * 2 + cc

    sibling = index(z, x, 1 - core)
    x_next = (index(z, at_x(1), core), index(z, at_x(-1), core))
    z_next = (index(at_z(1), x, core), index(at_z(-1), x, core))

    pending = []

    def send(src, dst, ssem, rsem, tile):
        cp = pltpu.make_async_remote_copy(
            src_ref=src, dst_ref=dst, send_sem=ssem, recv_sem=rsem,
            device_id={"tile": tile, "mem": q}, device_id_type=MESH,
        )
        cp.start()
        pending.append(cp)

    def wait_for(ref, sem):
        pltpu.make_async_copy(ref, ref, sem).wait()

    barrier = pltpu.get_barrier_semaphore()
    for t in (sibling, *x_next, *z_next):
        pl.semaphore_signal(barrier, inc=1, device_id={"tile": t, "mem": q}, device_id_type=MESH)
    pl.semaphore_wait(barrier, 5)

    for ox in NEAR_Z:
        xx = at_x(ox)
        send(part.at[at_z(4), xx, 1 - core, pl.ds(NA, NB)], rb.at[4, xx], s_b4.at[ox], r_b4.at[ox], sibling)
    for oz in NEAR_X:
        zz = at_z(oz)
        send(part.at[zz, at_x(2), 1 - core, pl.ds(0, NA)], ra.at[2, zz], s_a2.at[oz], r_a2.at[oz], sibling)
    for kind, d in (("b", 3), ("b", 5), ("a", 1), ("a", 3), ("b", 2), ("b", 6), ("b", 1), ("b", 7), ("a", 0), ("b", 0)):
        if kind == "a":
            send(part.at[:, at_x(d), 1 - core, pl.ds(0, NA)], ra.at[d], s_sib_a.at[d], r_sib_a.at[d], sibling)
        else:
            send(part.at[at_z(d), :, 1 - core, pl.ds(NA, NB)], rb.at[d], s_sib_b.at[d], r_sib_b.at[d], sibling)

    settled = set()

    def from_a(d, zz):
        if ("a", d) not in settled:
            settled.add(("a", d))
            if d != 2:
                wait_for(ra.at[d], r_sib_a.at[d])
        return [part.at[zz, at_x(d), core], ra.at[d, zz]]

    def from_b(d, xx):
        if ("b", d) not in settled:
            settled.add(("b", d))
            if d != 4:
                wait_for(rb.at[d], r_sib_b.at[d])
        return [part.at[at_z(d), xx, core, pl.ds(NA, NB)], rb.at[d, xx]]

    def total(dst, sources, first, last):
        @pl.loop(first, last)
        def _(b):
            value = None
            for s in sources:
                ref, start = s if isinstance(s, tuple) else (s, 0)
                v = ref[b - start].astype(F32)
                value = v if value is None else value + v
            dst[b] = value.astype(BF16)

    def result(base, sources, count):
        for b in range(count):
            value = None
            for s in sources:
                v = s[b].astype(F32)
                value = v if value is None else value + v
            out[:, (base + b) * B : (base + b + 1) * B] = value

    def a_far(k):
        for i in range(2):
            zz = at_z(FAR_X[i][k])
            wait_for(ra.at[2, zz], r_a2.at[FAR_X[i][k]])
            total(pa.at[2, zz], from_a(2, zz), 0, NA)
            send(pa.at[2, zz], xa1.at[i, k], s_xa1.at[i, k], r_xa1.at[i, k], x_next[i])

    def a_near(j):
        oz = NEAR_X[j]
        zz = at_z(oz)
        for i, d in enumerate((1, 3)):
            sources = from_a(d, zz)
            if oz in FAR_X[i]:
                k = FAR_X[i].index(oz)
                wait_for(xa1.at[i, k], r_xa1.at[i, k])
                sources.append(xa1.at[i, k])
            total(pa.at[d, zz], sources, 0, NA)
            send(pa.at[d, zz], xa2.at[i, j], s_xa2.at[i, j], r_xa2.at[i, j], x_next[i])

    half_a, half_b = (NA + 1) // 2, (NB + 1) // 2

    def a_own(oz):
        j = NEAR_X.index(oz)
        zz = at_z(oz)
        for i in range(2):
            wait_for(xa2.at[i, j], r_xa2.at[i, j])
        sources = [*from_a(0, zz), xa2.at[0, j], xa2.at[1, j]]
        mine = pa.at[0, zz]
        if oz == 4:
            total(mine, sources, 0, NA)
            for i, (first, size) in enumerate(((0, half_a), (half_a, NA - half_a))):
                piece = za1.at[pl.ds(first, size)]
                send(mine.at[pl.ds(first, size)], piece, s_za.at[i, 0], r_za.at[i, 0], z_next[i])
        elif oz in (3, 5):
            i = (3, 5).index(oz)
            first, size = ((0, half_a), (half_a, NA - half_a))[i]
            wait_for(za1.at[pl.ds(first, size)], r_za.at[i, 0])
            total(mine, [*sources, za1], first, first + size)
            total(mine, sources, *((half_a, NA), (0, half_a))[i])
            send(mine, za2.at[i, 0], s_za.at[i, 1], r_za.at[i, 1], z_next[i])
        elif oz != 0:
            i = 0 if oz < 4 else 1
            step = 4 - oz if i == 0 else oz - 4
            wait_for(za2.at[i, step - 2], r_za.at[i, step - 1])
            total(mine, [*sources, za2.at[i, step - 2]], 0, NA)
            send(mine, za2.at[i, step - 1], s_za.at[i, step], r_za.at[i, step], z_next[i])
        else:
            for i in range(2):
                wait_for(za2.at[i, 2], r_za.at[i, 3])
            result(0, [*sources, za2.at[0, 2], za2.at[1, 2]], NA)

    def b_far(k):
        for i in range(2):
            xx = at_x(FAR_Z[i][k])
            wait_for(rb.at[4, xx], r_b4.at[FAR_Z[i][k]])
            total(pb.at[4, xx], from_b(4, xx), 0, NB)
            send(pb.at[4, xx], zb1.at[i, k], s_zb1.at[i, k], r_zb1.at[i, k], z_next[i])

    def b_near(step, j):
        ox = NEAR_Z[j]
        xx = at_x(ox)
        for i, d in enumerate((4 - step, 4 + step)):
            sources = from_b(d, xx)
            if step > 1:
                wait_for(zb2.at[i, step - 2, j], r_zb2.at[i, step - 2, j])
                sources.append(zb2.at[i, step - 2, j])
            elif ox in FAR_Z[i]:
                k = FAR_Z[i].index(ox)
                wait_for(zb1.at[i, k], r_zb1.at[i, k])
                sources.append(zb1.at[i, k])
            total(pb.at[d, xx], sources, 0, NB)
            send(
                pb.at[d, xx], zb2.at[i, step - 1, j], s_zb2.at[i, step - 1, j], r_zb2.at[i, step - 1, j], z_next[i]
            )

    def b_own(ox):
        j = NEAR_Z.index(ox)
        xx = at_x(ox)
        for i in range(2):
            wait_for(zb2.at[i, 2, j], r_zb2.at[i, 2, j])
        sources = [*from_b(0, xx), zb2.at[0, 2, j], zb2.at[1, 2, j]]
        mine = pb.at[0, xx]
        halves = ((0, half_b), (half_b, NB - half_b))
        if ox == 2:
            total(mine, sources, 0, NB)
            for i, (first, size) in enumerate(halves):
                piece = xb1.at[pl.ds(first, size)]
                send(mine.at[pl.ds(first, size)], piece, s_xb.at[i, 0], r_xb.at[i, 0], x_next[i])
        elif ox != 0:
            i = (1, 3).index(ox)
            first, size = halves[i]
            wait_for(xb1.at[pl.ds(first, size)], r_xb.at[i, 0])
            total(mine, [*sources, xb1], first, first + size)
            total(mine, sources, *((half_b, NB), (0, half_b))[i])
            send(mine, xb2.at[i], s_xb.at[i, 1], r_xb.at[i, 1], x_next[i])
        else:
            for i in range(2):
                wait_for(xb2.at[i], r_xb.at[i, 1])
            result(NA, [*sources, xb2.at[0], xb2.at[1]], NB)

    acts = {"a_far": a_far, "a_near": a_near, "a_own": a_own, "b_far": b_far, "b_near": b_near, "b_own": b_own}
    for name, *numbers in GATHER_ORDER:
        while len(pending) > 30:
            pending.pop(0).wait_send()
        acts[name](*numbers)
    for cp in pending:
        cp.wait_send()


def gather(part):
    vmem = pl.BlockSpec(memory_space=pltpu.VMEM)
    dma = pltpu.SemaphoreType.DMA
    return pl.pallas_call(
        gather_kernel,
        out_shape=jax.ShapeDtypeStruct((LM, FLUX_DEV * B), F32),
        in_specs=[vmem],
        out_specs=vmem,
        scratch_shapes=[
            pltpu.VMEM((NX, NZ, NA, LM, B), BF16),
            pltpu.VMEM((NZ, NX, NB, LM, B), BF16),
            pltpu.VMEM((NX, NZ, NA, LM, B), BF16),
            pltpu.VMEM((NZ, NX, NB, LM, B), BF16),
            pltpu.VMEM((2, 4, NA, LM, B), BF16),
            pltpu.VMEM((2, NZ, NA, LM, B), BF16),
            pltpu.VMEM((2, 2, NB, LM, B), BF16),
            pltpu.VMEM((2, 3, NX, NB, LM, B), BF16),
            pltpu.VMEM((NA, LM, B), BF16),
            pltpu.VMEM((2, 3, NA, LM, B), BF16),
            pltpu.VMEM((NB, LM, B), BF16),
            pltpu.VMEM((2, NB, LM, B), BF16),
            dma((NX,)), dma((NX,)), dma((NZ,)), dma((NZ,)), dma((NZ,)), dma((NZ,)), dma((NX,)), dma((NX,)),
            dma((2, 4)), dma((2, 4)), dma((2, NZ)), dma((2, NZ)),
            dma((2, 2)), dma((2, 2)), dma((2, 3, NX)), dma((2, 3, NX)),
            dma((2, 4)), dma((2, 4)), dma((2, 2)), dma((2, 2)),
        ],
        compiler_params=pltpu.CompilerParams(
            collective_id=1, has_side_effects=True, vmem_limit_bytes=18 * 2**20
        ),
        name="gather",
    )(part.reshape(NZ, NX, 2, FLUX_DEV, LM, B))


def body(footprints, tile_row, tile_col, prior_flux, observed, precision_weight):
    pin = functools.partial(pltpu.with_memory_space_constraint, memory_space=pltpu.HBM)
    footprints, prior_flux, observed = pin(footprints), pin(prior_flux), pin(observed)
    tile_row, tile_col = pin(tile_row.reshape(1, B)), pin(tile_col.reshape(1, B))
    tiles, anoms, codes = spread(tile_row, tile_col, footprints, prior_flux)
    weight = pin(precision_weight.reshape(SOUND_DEV, 1, B))
    part = local(codes, tiles, anoms, observed, weight)
    return gather(part)


def solution(mesh):
    in_specs = (
        P("tile", None, None),
        P("tile"),
        P("tile"),
        P("mem", "tile"),
        P("mem", "tile"),
        P("tile"),
    )
    out_specs = P("mem", "tile")
    return jax.shard_map(body, mesh=mesh, in_specs=in_specs, out_specs=out_specs, check_vma=False)
```

```python
import functools

import jax
import jax.numpy as jnp
from jax import lax
from jax.experimental import pallas as pl
from jax.experimental.pallas import tpu as pltpu
from jax.sharding import PartitionSpec as P

MEMBERS = 256
FLUX_DEV = 8
SOUND_DEV = 16
NZ, NX, NY, NT = 8, 4, 4, 64
CAP = 3
B = 128
LM = 64
MESH = pl.DeviceIdType.MESH
F32, BF16 = jnp.float32, jnp.bfloat16


def route(row, col):
    shape = (B, B)
    down, across = lax.broadcasted_iota(jnp.int32, shape, 0), lax.broadcasted_iota(jnp.int32, shape, 1)

    def column(v):
        return jnp.sum(jnp.where(down == across, v, 0), axis=1, keepdims=True)

    owner = row // SOUND_DEV
    earlier = (column(owner) == owner) & (down < across)
    place = jnp.sum(earlier.astype(jnp.int32), axis=0, keepdims=True)
    slot = column(owner * CAP + place)
    index = lax.broadcasted_iota(jnp.int32, (B, 2 * B), 0)
    at = lax.broadcasted_iota(jnp.int32, (B, 2 * B), 1)
    source = jnp.sum(jnp.where(slot == at, index, 0), axis=0, keepdims=True)
    blocks = (row - owner * SOUND_DEV) * 512 + col - SOUND_DEV * 512
    mine = lax.broadcasted_iota(jnp.int32, (NT, B), 0) == owner
    lane = lax.broadcasted_iota(jnp.int32, (NT, B), 1)
    coded = jnp.full((NT, B), SOUND_DEV * 512, jnp.int32)
    for k in range(CAP):
        found = jnp.sum(jnp.where(mine & (place == k), blocks, 0), axis=1, keepdims=True)
        coded = coded + jnp.where(lane == k, found, 0)
    return source, coded


SPREAD_ORDER = (
    ("T", 0), ("T", 1), ("T", 7), ("A0",), ("T", 2), ("T", 6), ("Y1", 0), ("Y1", 1), ("Y1", 7), ("Y2", 0, 0),
    ("Y2", 1, 0), ("Z", 0, 1), ("X", 0, 0), ("X", 1, 0), ("Z", 1, 1), ("Y2", 0, 1), ("Y2", 1, 1), ("T", 3),
    ("T", 5), ("X", 0, 7), ("X", 1, 7), ("Y2", 0, 7), ("Y2", 1, 7), ("Y1", 2), ("Y1", 6), ("XL", 0),
    ("Z", 0, 2), ("X", 0, 1), ("X", 1, 1), ("Z", 1, 2), ("T", 4), ("XL", 7), ("Y2", 0, 2), ("Y2", 1, 2),
    ("X", 0, 6), ("X", 1, 6), ("XL", 1), ("Y2", 0, 6), ("Y2", 1, 6), ("X", 0, 2), ("X", 1, 2), ("Y1", 3),
    ("Y1", 5), ("Z", 0, 3), ("Z", 1, 3), ("XL", 6), ("XL", 2), ("Y2", 0, 3), ("Y2", 1, 3), ("X", 0, 5),
    ("X", 1, 5), ("X", 0, 3), ("X", 1, 3), ("Y2", 0, 5), ("Y2", 1, 5), ("Y1", 4), ("Z", 0, 4), ("XL", 5),
    ("XL", 3), ("X", 0, 4), ("X", 1, 4), ("Y2", 0, 4), ("Y2", 1, 4), ("XL", 4),
)


def spread_kernel(
    row_h, col_h, footprints, prior_h, tiles, anoms, codes,
    row, col, source_v, source, coded, prior, quarter, staged, sums, shard,
    s_row, s_fp, s_prior, s_sum, r_sum, s_tile, r_tile, s_code, r_code, s_y, r_y, s_y2, r_y2,
    s_local, s_z, r_z, s_x, r_x, s_x2, r_x2, s_sib, r_sib, came,
):
    me = lax.axis_index("tile")
    q = lax.axis_index("mem")
    core = lax.rem(me, 2)
    x = lax.rem(me // 2, NX)
    z = me // 8

    def at_z(o):
        return lax.rem(z + o + NZ, NZ)

    def at_x(o):
        return lax.rem(x + o + NX, NX)

    def at_y(o):
        return lax.rem(q + o + NY, NY)

    def index(zz, xx, cc):
        return zz * 8 + xx * 2 + cc

    def remote(src, dst, ssem, rsem, tile=None, mem=None):
        return pltpu.make_async_remote_copy(
            src_ref=src, dst_ref=dst, send_sem=ssem, recv_sem=rsem,
            device_id={"tile": me if tile is None else tile, "mem": q if mem is None else mem},
            device_id_type=MESH,
        )

    def wait_for(ref, sem):
        pltpu.make_async_copy(ref, ref, sem).wait()

    row_copy = pltpu.make_async_copy(row_h, row, s_row.at[0])
    row_copy.start()
    col_copy = pltpu.make_async_copy(col_h, col, s_row.at[1])
    col_copy.start()
    prior_copy = pltpu.make_async_copy(prior_h, prior, s_prior)
    prior_copy.start()
    fp_copy = pltpu.make_async_copy(
        footprints.at[:, pl.ds(pl.multiple_of(q * 32, 32), 32), :], quarter, s_fp
    )
    fp_copy.start()

    barrier = pltpu.get_barrier_semaphore()
    for o in range(1, 8):
        pl.semaphore_signal(
            barrier, inc=1, device_id={"tile": z * 8 + lax.rem(me + o, 8), "mem": q}, device_id_type=MESH
        )
    for o in range(1, NY):
        pl.semaphore_signal(barrier, inc=1, device_id={"tile": me, "mem": at_y(o)}, device_id_type=MESH)
    for o in (1, -1):
        pl.semaphore_signal(
            barrier, inc=1, device_id={"tile": index(at_z(o), x, core), "mem": q}, device_id_type=MESH
        )

    def tell(stage):
        for i, o in enumerate((1, -1)):
            pl.semaphore_signal(
                came.at[i, stage], inc=1, device_id={"tile": index(at_z(o), x, core), "mem": q}, device_id_type=MESH
            )

    def hear(stage):
        for i in range(2):
            pl.semaphore_wait(came.at[i, stage], 1)

    row_copy.wait()
    col_copy.wait()
    source_row, coded_rows = route(row[...], col[...])
    source_v[...] = source_row
    source_copy = pltpu.make_async_copy(source_v, source, s_row.at[2])
    source_copy.start()
    for t in range(NT):
        coded[t] = coded_rows[t : t + 1]
    prior_copy.wait()
    for j in range(FLUX_DEV):
        part = jnp.sum(prior[:, j * B : (j + 1) * B].astype(F32), axis=0, keepdims=True)
        sums[0, j : j + 1, :] = part
    pl.semaphore_wait(barrier, 7 + NY - 1 + 2)
    tell(1)

    sum_sends = []
    for o in range(1, NY):
        cp = remote(sums.at[0], sums.at[o], s_sum.at[o], r_sum.at[o], mem=at_y(o))
        cp.start()
        sum_sends.append(cp)
    fp_copy.wait()
    source_copy.wait()

    def send_tiles(dz):
        first = 1 if dz == 0 else 0
        if 1 <= dz <= 4:
            hear(dz)
            if dz < 4:
                tell(dz + 1)

        @pl.loop(first, 8)
        def _(o):
            t = at_z(dz) * 8 + lax.rem(me + o, 8)
            for s in range(CAP):
                staged[t, s] = quarter[source[0, t * CAP + s]]
            remote(staged.at[t], tiles.at[q, me], s_tile, r_tile.at[dz], tile=t).start()
            remote(coded.at[t], codes.at[me], s_code, r_code, tile=t).start()

        if dz == 0:
            for s in range(CAP):
                staged[me, s] = quarter[source[0, me * CAP + s]]
            pltpu.make_async_copy(staged.at[me], tiles.at[q, me], r_tile.at[0]).start()
            pltpu.make_async_copy(coded.at[me], codes.at[me], r_code).start()

    def group(quarter_index, dz, first=0, size=8):
        zs = at_z(-dz)
        return tiles.at[quarter_index, pl.ds(zs * 8 + first, size)]

    pending = []

    def go(cp):
        cp.start()
        pending.append(cp)

    def y_first(dz):
        wait_for(group(q, dz), r_tile.at[dz])
        for late in range(2):
            for i, to in enumerate((1, -1)):
                h = (i + late) % 2
                half = group(q, dz, 4 * h, 4)
                go(remote(half, half, s_y.at[i, h, dz], r_y.at[i, h, dz], mem=at_y(to)))

    def y_second(i, dz):
        from_, to = ((-1, 1), (1, -1))[i]
        half = group(at_y(from_), dz, 4 * i, 4)
        wait_for(half, r_y.at[i, i, dz])
        go(remote(half, half, s_y2.at[i, dz], r_y2.at[i, dz], mem=at_y(to)))

    def y_last(dz):
        for i in range(2):
            wait_for(group(at_y((-1, 1)[i]), dz, 4 - 4 * i, 4), r_y.at[i, 1 - i, dz])
            wait_for(group(at_y(2), dz, 4 * i, 4), r_y2.at[i, dz])

    def block(oz, ox, own_core=True):
        return anoms.at[index(at_z(oz), at_x(ox), core if own_core else 1 - core)]

    def to_sibling(oz, ox):
        go(
            remote(
                block(oz, ox), block(oz, ox), s_sib.at[ox % NX, oz % NZ], r_sib.at[ox % NX, oz % NZ],
                tile=index(z, x, 1 - core),
            )
        )

    def x_first(oz, src=None):
        b = block(oz, 0)
        src = b if src is None else src
        k = oz % NZ
        for late in range(2):
            for i, to in enumerate((1, -1)):
                h = (i + late) % 2
                part = pl.ds(4 * h, 4)
                go(remote(src.at[part], b.at[part], s_x.at[i, h, k], r_x.at[i, h, k], tile=index(z, at_x(to), core)))
        go(remote(src, b, s_sib.at[0, k], r_sib.at[0, k], tile=index(z, x, 1 - core)))

    def x_second(i, oz):
        k = oz % NZ
        from_, to = ((-1, 1), (1, -1))[i]
        half = block(oz, from_).at[pl.ds(4 * i, 4)]
        wait_for(half, r_x.at[i, i, k])
        go(remote(half, half, s_x2.at[i, k], r_x2.at[i, k], tile=index(z, at_x(to), core)))

    def x_last(oz):
        k = oz % NZ
        for i, from_ in enumerate((-1, 1)):
            wait_for(block(oz, from_).at[pl.ds(4 - 4 * i, 4)], r_x.at[i, 1 - i, k])
            to_sibling(oz, from_)
        for i in range(2):
            wait_for(block(oz, 2).at[pl.ds(4 * i, 4)], r_x2.at[i, k])
        to_sibling(oz, 2)

    def z_step(i, k):
        if k < 4:
            b = block((-k, k)[i], 0)
            wait_for(b, r_z.at[i, k])
            h = b if k < 3 else b.at[pl.ds(4 * i, 4)]
            go(remote(h, h, s_z.at[i, k + 1], r_z.at[i, k + 1], tile=index(at_z((1, -1)[i]), x, core)))
            x_first((-k, k)[i])
        else:
            b = block(4, 0)
            wait_for(b.at[pl.ds(0, 4)], r_z.at[0, 4])
            wait_for(b.at[pl.ds(4, 4)], r_z.at[1, 4])
            x_first(4)

    own_copy = pltpu.make_async_copy(shard, anoms.at[me], s_local)

    def send_shard():
        for cp in sum_sends:
            cp.wait()
        mean = (sums[0] + sums[1] + sums[2] + sums[3]) / MEMBERS
        for j in range(FLUX_DEV):
            shard[j] = (prior[:, j * B : (j + 1) * B].astype(F32) - mean[j : j + 1, :]).astype(BF16)
        own_copy.start()
        go(remote(shard, anoms.at[me], s_z.at[0, 1], r_z.at[0, 1], tile=index(at_z(1), x, core)))
        go(remote(shard, anoms.at[me], s_z.at[1, 1], r_z.at[1, 1], tile=index(at_z(-1), x, core)))
        x_first(0, shard)

    acts = {
        "T": send_tiles, "A0": send_shard, "Z": z_step, "X": x_second, "XL": x_last, "Y1": y_first, "Y2": y_second
    }
    for name, *numbers in SPREAD_ORDER:
        while len(pending) > 40:
            pending.pop(0).wait_send()
        acts[name](*numbers)
    for dz in (0, 1, 7, 2, 6, 3, 5, 4):
        y_last(dz)
    for oz in (0, 1, 7, 2, 6, 3, 5, 4):
        for ox in range(NX):
            wait_for(block(oz, ox, False), r_sib.at[ox, oz])
    wait_for(codes, r_code)
    own_copy.wait()
    for cp in pending:
        cp.wait_send()
    wait_for(staged.at[pl.ds(0, NT - 1)], s_tile)
    wait_for(codes.at[pl.ds(0, NT - 1)], s_code)


def spread(tile_row, tile_col, footprints, prior):
    hbm = pl.BlockSpec(memory_space=pltpu.HBM)
    vmem = pl.BlockSpec(memory_space=pltpu.VMEM)
    dma = pltpu.SemaphoreType.DMA
    return pl.pallas_call(
        spread_kernel,
        out_shape=(
            jax.ShapeDtypeStruct((NY, NT, CAP, 32, B), BF16),
            jax.ShapeDtypeStruct((NT, FLUX_DEV, LM, B), BF16),
            jax.ShapeDtypeStruct((NT, 1, B), jnp.int32),
        ),
        in_specs=[hbm, hbm, hbm, hbm],
        out_specs=(vmem, vmem, vmem),
        scratch_shapes=[
            pltpu.VMEM((1, B), jnp.int32),
            pltpu.VMEM((1, B), jnp.int32),
            pltpu.VMEM((1, 2 * B), jnp.int32),
            pltpu.SMEM((1, 2 * B), jnp.int32),
            pltpu.VMEM((NT, 1, B), jnp.int32),
            pltpu.VMEM((LM, FLUX_DEV * B), BF16),
            pltpu.VMEM((B, 32, B), BF16),
            pltpu.VMEM((NT, CAP, 32, B), BF16),
            pltpu.VMEM((NY, FLUX_DEV, B), F32),
            pltpu.VMEM((FLUX_DEV, LM, B), BF16),
            dma((3,)), dma, dma, dma((NY,)), dma((NY,)), dma, dma((NZ,)), dma, dma,
            dma((2, 2, NZ)), dma((2, 2, NZ)), dma((2, NZ)), dma((2, NZ)),
            dma, dma((2, 5)), dma((2, 5)), dma((2, 2, NZ)), dma((2, 2, NZ)), dma((2, NZ)), dma((2, NZ)),
            dma((NX, NZ)), dma((NX, NZ)), pltpu.SemaphoreType.REGULAR((2, 5)),
        ],
        compiler_params=pltpu.CompilerParams(
            collective_id=0, has_side_effects=True, vmem_limit_bytes=16 * 2**20
        ),
        name="spread",
    )(tile_row, tile_col, footprints, prior)


def local_kernel(
    codes_v, tiles, anoms, observed_h, weight_h, out,
    codes, s_codes, observed, weight, modelled, weighted, total, s_obs, s_weight,
):
    codes_in = pltpu.make_async_copy(codes_v, codes, s_codes)
    codes_in.start()
    observed_in = pltpu.make_async_copy(observed_h, observed, s_obs)
    observed_in.start()
    weight_in = pltpu.make_async_copy(weight_h, weight, s_weight)
    weight_in.start()
    modelled[...] = jnp.zeros_like(modelled)

    @pl.loop(0, NT)
    def _(i):
        total[pl.ds(i * 8, 8)] = jnp.zeros((8, LM, B), F32)

    codes_in.wait()
    step = 32

    def fetch(i, o, s):
        src = i * step + o
        code = codes[src, 0, s]
        return tiles[:, src, s].reshape(B, B), code // 512, lax.rem(code, 512)

    @pl.loop(0, NT // step)
    def _(i):
        terms = []
        for o in range(step):
            for s in range(CAP):
                tile, row, col = fetch(i, o, s)
                term = lax.dot_general(
                    anoms[col], tile, (((1,), (1,)), ((), ())), preferred_element_type=F32
                )
                terms.append((row, term))
        for row, term in terms:
            modelled[row] += term

    observed_in.wait()
    weight_in.wait()
    for r in range(SOUND_DEV):
        factor = weight[r].astype(F32) / 8.0
        gap = modelled[r] - observed[:, r * B : (r + 1) * B]
        weighted[r] = (factor * gap).astype(BF16)
    weighted[SOUND_DEV] = jnp.zeros((LM, B), BF16)

    @pl.loop(0, NT // step)
    def _(i):
        terms = []
        for o in range(step):
            for s in range(CAP):
                tile, row, col = fetch(i, o, s)
                term = lax.dot_general(
                    weighted[row], tile, (((1,), (0,)), ((), ())), preferred_element_type=F32
                )
                terms.append((col, term))
        for col, term in terms:
            total[col] += term

    @pl.loop(0, NT // 4)
    def _(i):
        out[pl.ds(i * 32, 32)] = total[pl.ds(i * 32, 32)].astype(BF16)


def local(codes, tiles, anoms, observed, weight):
    hbm = pl.BlockSpec(memory_space=pltpu.HBM)
    vmem = pl.BlockSpec(memory_space=pltpu.VMEM)
    dma = pltpu.SemaphoreType.DMA
    return pl.pallas_call(
        local_kernel,
        out_shape=jax.ShapeDtypeStruct((NT * FLUX_DEV, LM, B), BF16),
        in_specs=[vmem, vmem, vmem, hbm, hbm],
        out_specs=vmem,
        scratch_shapes=[
            pltpu.SMEM((NT, 1, B), jnp.int32),
            dma,
            pltpu.VMEM((LM, SOUND_DEV * B), F32),
            pltpu.VMEM((SOUND_DEV, 1, B), jnp.int32),
            pltpu.VMEM((SOUND_DEV + 1, LM, B), F32),
            pltpu.VMEM((SOUND_DEV + 1, LM, B), BF16),
            pltpu.VMEM((NT * FLUX_DEV, LM, B), F32),
            dma, dma,
        ],
        compiler_params=pltpu.CompilerParams(vmem_limit_bytes=22 * 2**20),
        name="local",
    )(codes, tiles, anoms.reshape(NT * FLUX_DEV, LM, B), observed, weight)


NA = 5
NB = FLUX_DEV - NA
FAR_X = ((4, 3, 2, 1), (5, 6, 7, 0))
NEAR_X = (4, 5, 3, 6, 2, 7, 1, 0)
FAR_Z = ((2, 1), (3, 0))
NEAR_Z = (2, 1, 3, 0)

GATHER_ORDER = (
    ("b_far", 0), ("b_far", 1), ("a_far", 0), ("a_far", 1), ("a_far", 2), ("a_far", 3), ("b_near", 1, 0),
    ("b_near", 1, 2), ("a_near", 0), ("b_near", 1, 1), ("b_near", 1, 3), ("a_near", 1), ("b_near", 2, 0),
    ("b_near", 2, 2), ("a_near", 2), ("b_near", 2, 1), ("a_near", 3), ("b_near", 2, 3), ("b_near", 3, 0),
    ("a_own", 4), ("a_near", 4), ("b_near", 3, 1), ("a_near", 5), ("b_near", 3, 2), ("b_own", 2),
    ("a_own", 5), ("a_own", 3), ("a_near", 6), ("b_near", 3, 3), ("a_near", 7), ("a_own", 6), ("a_own", 2),
    ("b_own", 3), ("b_own", 1), ("a_own", 7), ("a_own", 1), ("b_own", 0), ("a_own", 0),
)


def gather_kernel(
    part, out,
    pa, pb, ra, rb, xa1, xa2, zb1, zb2, za1, za2, xb1, xb2,
    s_sib_a, r_sib_a, s_sib_b, r_sib_b, s_a2, r_a2, s_b4, r_b4,
    s_xa1, r_xa1, s_xa2, r_xa2, s_zb1, r_zb1, s_zb2, r_zb2, s_za, r_za, s_xb, r_xb,
):
    me = lax.axis_index("tile")
    q = lax.axis_index("mem")
    core = lax.rem(me, 2)
    x = lax.rem(me // 2, NX)
    z = me // 8

    def at_z(o):
        return lax.rem(z + o + NZ, NZ)

    def at_x(o):
        return lax.rem(x + o + NX, NX)

    def index(zz, xx, cc):
        return zz * 8 + xx * 2 + cc

    sibling = index(z, x, 1 - core)
    x_next = (index(z, at_x(1), core), index(z, at_x(-1), core))
    z_next = (index(at_z(1), x, core), index(at_z(-1), x, core))

    pending = []

    def send(src, dst, ssem, rsem, tile):
        cp = pltpu.make_async_remote_copy(
            src_ref=src, dst_ref=dst, send_sem=ssem, recv_sem=rsem,
            device_id={"tile": tile, "mem": q}, device_id_type=MESH,
        )
        cp.start()
        pending.append(cp)

    def wait_for(ref, sem):
        pltpu.make_async_copy(ref, ref, sem).wait()

    barrier = pltpu.get_barrier_semaphore()
    for t in (sibling, *x_next, *z_next):
        pl.semaphore_signal(barrier, inc=1, device_id={"tile": t, "mem": q}, device_id_type=MESH)
    pl.semaphore_wait(barrier, 5)

    for ox in NEAR_Z:
        xx = at_x(ox)
        send(part.at[at_z(4), xx, 1 - core, pl.ds(NA, NB)], rb.at[4, xx], s_b4.at[ox], r_b4.at[ox], sibling)
    for oz in NEAR_X:
        zz = at_z(oz)
        send(part.at[zz, at_x(2), 1 - core, pl.ds(0, NA)], ra.at[2, zz], s_a2.at[oz], r_a2.at[oz], sibling)
    for kind, d in (("b", 3), ("b", 5), ("a", 1), ("a", 3), ("b", 2), ("b", 6), ("b", 1), ("b", 7), ("a", 0), ("b", 0)):
        if kind == "a":
            send(part.at[:, at_x(d), 1 - core, pl.ds(0, NA)], ra.at[d], s_sib_a.at[d], r_sib_a.at[d], sibling)
        else:
            send(part.at[at_z(d), :, 1 - core, pl.ds(NA, NB)], rb.at[d], s_sib_b.at[d], r_sib_b.at[d], sibling)

    settled = set()

    def from_a(d, zz):
        if ("a", d) not in settled:
            settled.add(("a", d))
            if d != 2:
                wait_for(ra.at[d], r_sib_a.at[d])
        return [part.at[zz, at_x(d), core], ra.at[d, zz]]

    def from_b(d, xx):
        if ("b", d) not in settled:
            settled.add(("b", d))
            if d != 4:
                wait_for(rb.at[d], r_sib_b.at[d])
        return [part.at[at_z(d), xx, core, pl.ds(NA, NB)], rb.at[d, xx]]

    def total(dst, sources, first, last):
        @pl.loop(first, last)
        def _(b):
            value = None
            for s in sources:
                ref, start = s if isinstance(s, tuple) else (s, 0)
                v = ref[b - start].astype(F32)
                value = v if value is None else value + v
            dst[b] = value.astype(BF16)

    def result(base, sources, count):
        for b in range(count):
            value = None
            for s in sources:
                v = s[b].astype(F32)
                value = v if value is None else value + v
            out[:, (base + b) * B : (base + b + 1) * B] = value

    def a_far(k):
        for i in range(2):
            zz = at_z(FAR_X[i][k])
            wait_for(ra.at[2, zz], r_a2.at[FAR_X[i][k]])
            total(pa.at[2, zz], from_a(2, zz), 0, NA)
            send(pa.at[2, zz], xa1.at[i, k], s_xa1.at[i, k], r_xa1.at[i, k], x_next[i])

    def a_near(j):
        oz = NEAR_X[j]
        zz = at_z(oz)
        for i, d in enumerate((1, 3)):
            sources = from_a(d, zz)
            if oz in FAR_X[i]:
                k = FAR_X[i].index(oz)
                wait_for(xa1.at[i, k], r_xa1.at[i, k])
                sources.append(xa1.at[i, k])
            total(pa.at[d, zz], sources, 0, NA)
            send(pa.at[d, zz], xa2.at[i, j], s_xa2.at[i, j], r_xa2.at[i, j], x_next[i])

    half_a, half_b = (NA + 1) // 2, (NB + 1) // 2

    def a_own(oz):
        j = NEAR_X.index(oz)
        zz = at_z(oz)
        for i in range(2):
            wait_for(xa2.at[i, j], r_xa2.at[i, j])
        sources = [*from_a(0, zz), xa2.at[0, j], xa2.at[1, j]]
        mine = pa.at[0, zz]
        if oz == 4:
            total(mine, sources, 0, NA)
            for i, (first, size) in enumerate(((0, half_a), (half_a, NA - half_a))):
                piece = za1.at[pl.ds(first, size)]
                send(mine.at[pl.ds(first, size)], piece, s_za.at[i, 0], r_za.at[i, 0], z_next[i])
        elif oz in (3, 5):
            i = (3, 5).index(oz)
            first, size = ((0, half_a), (half_a, NA - half_a))[i]
            wait_for(za1.at[pl.ds(first, size)], r_za.at[i, 0])
            total(mine, [*sources, za1], first, first + size)
            total(mine, sources, *((half_a, NA), (0, half_a))[i])
            send(mine, za2.at[i, 0], s_za.at[i, 1], r_za.at[i, 1], z_next[i])
        elif oz != 0:
            i = 0 if oz < 4 else 1
            step = 4 - oz if i == 0 else oz - 4
            wait_for(za2.at[i, step - 2], r_za.at[i, step - 1])
            total(mine, [*sources, za2.at[i, step - 2]], 0, NA)
            send(mine, za2.at[i, step - 1], s_za.at[i, step], r_za.at[i, step], z_next[i])
        else:
            for i in range(2):
                wait_for(za2.at[i, 2], r_za.at[i, 3])
            result(0, [*sources, za2.at[0, 2], za2.at[1, 2]], NA)

    def b_far(k):
        for i in range(2):
            xx = at_x(FAR_Z[i][k])
            wait_for(rb.at[4, xx], r_b4.at[FAR_Z[i][k]])
            total(pb.at[4, xx], from_b(4, xx), 0, NB)
            send(pb.at[4, xx], zb1.at[i, k], s_zb1.at[i, k], r_zb1.at[i, k], z_next[i])

    def b_near(step, j):
        ox = NEAR_Z[j]
        xx = at_x(ox)
        for i, d in enumerate((4 - step, 4 + step)):
            sources = from_b(d, xx)
            if step > 1:
                wait_for(zb2.at[i, step - 2, j], r_zb2.at[i, step - 2, j])
                sources.append(zb2.at[i, step - 2, j])
            elif ox in FAR_Z[i]:
                k = FAR_Z[i].index(ox)
                wait_for(zb1.at[i, k], r_zb1.at[i, k])
                sources.append(zb1.at[i, k])
            total(pb.at[d, xx], sources, 0, NB)
            send(
                pb.at[d, xx], zb2.at[i, step - 1, j], s_zb2.at[i, step - 1, j], r_zb2.at[i, step - 1, j], z_next[i]
            )

    def b_own(ox):
        j = NEAR_Z.index(ox)
        xx = at_x(ox)
        for i in range(2):
            wait_for(zb2.at[i, 2, j], r_zb2.at[i, 2, j])
        sources = [*from_b(0, xx), zb2.at[0, 2, j], zb2.at[1, 2, j]]
        mine = pb.at[0, xx]
        halves = ((0, half_b), (half_b, NB - half_b))
        if ox == 2:
            total(mine, sources, 0, NB)
            for i, (first, size) in enumerate(halves):
                piece = xb1.at[pl.ds(first, size)]
                send(mine.at[pl.ds(first, size)], piece, s_xb.at[i, 0], r_xb.at[i, 0], x_next[i])
        elif ox != 0:
            i = (1, 3).index(ox)
            first, size = halves[i]
            wait_for(xb1.at[pl.ds(first, size)], r_xb.at[i, 0])
            total(mine, [*sources, xb1], first, first + size)
            total(mine, sources, *((half_b, NB), (0, half_b))[i])
            send(mine, xb2.at[i], s_xb.at[i, 1], r_xb.at[i, 1], x_next[i])
        else:
            for i in range(2):
                wait_for(xb2.at[i], r_xb.at[i, 1])
            result(NA, [*sources, xb2.at[0], xb2.at[1]], NB)

    acts = {"a_far": a_far, "a_near": a_near, "a_own": a_own, "b_far": b_far, "b_near": b_near, "b_own": b_own}
    for name, *numbers in GATHER_ORDER:
        while len(pending) > 30:
            pending.pop(0).wait_send()
        acts[name](*numbers)
    for cp in pending:
        cp.wait_send()


def gather(part):
    vmem = pl.BlockSpec(memory_space=pltpu.VMEM)
    dma = pltpu.SemaphoreType.DMA
    return pl.pallas_call(
        gather_kernel,
        out_shape=jax.ShapeDtypeStruct((LM, FLUX_DEV * B), F32),
        in_specs=[vmem],
        out_specs=vmem,
        scratch_shapes=[
            pltpu.VMEM((NX, NZ, NA, LM, B), BF16),
            pltpu.VMEM((NZ, NX, NB, LM, B), BF16),
            pltpu.VMEM((NX, NZ, NA, LM, B), BF16),
            pltpu.VMEM((NZ, NX, NB, LM, B), BF16),
            pltpu.VMEM((2, 4, NA, LM, B), BF16),
            pltpu.VMEM((2, NZ, NA, LM, B), BF16),
            pltpu.VMEM((2, 2, NB, LM, B), BF16),
            pltpu.VMEM((2, 3, NX, NB, LM, B), BF16),
            pltpu.VMEM((NA, LM, B), BF16),
            pltpu.VMEM((2, 3, NA, LM, B), BF16),
            pltpu.VMEM((NB, LM, B), BF16),
            pltpu.VMEM((2, NB, LM, B), BF16),
            dma((NX,)), dma((NX,)), dma((NZ,)), dma((NZ,)), dma((NZ,)), dma((NZ,)), dma((NX,)), dma((NX,)),
            dma((2, 4)), dma((2, 4)), dma((2, NZ)), dma((2, NZ)),
            dma((2, 2)), dma((2, 2)), dma((2, 3, NX)), dma((2, 3, NX)),
            dma((2, 4)), dma((2, 4)), dma((2, 2)), dma((2, 2)),
        ],
        compiler_params=pltpu.CompilerParams(
            collective_id=1, has_side_effects=True, vmem_limit_bytes=18 * 2**20
        ),
        name="gather",
    )(part.reshape(NZ, NX, 2, FLUX_DEV, LM, B))


def body(footprints, tile_row, tile_col, prior_flux, observed, precision_weight):
    pin = functools.partial(pltpu.with_memory_space_constraint, memory_space=pltpu.HBM)
    footprints, prior_flux, observed = pin(footprints), pin(prior_flux), pin(observed)
    tile_row, tile_col = pin(tile_row.reshape(1, B)), pin(tile_col.reshape(1, B))
    tiles, anoms, codes = spread(tile_row, tile_col, footprints, prior_flux)
    weight = pin(precision_weight.reshape(SOUND_DEV, 1, B))
    part = local(codes, tiles, anoms, observed, weight)
    return gather(part)


def solution(mesh):
    in_specs = (
        P("tile", None, None),
        P("tile"),
        P("tile"),
        P("mem", "tile"),
        P("mem", "tile"),
        P("tile"),
    )
    out_specs = P("mem", "tile")
    return jax.shard_map(body, mesh=mesh, in_specs=in_specs, out_specs=out_specs, check_vma=False)
```

```python
import functools

import jax
import jax.numpy as jnp
from jax import lax
from jax.experimental import pallas as pl
from jax.experimental.pallas import tpu as pltpu
from jax.sharding import PartitionSpec as P

MEMBERS = 256
FLUX_DEV = 8
SOUND_DEV = 16
NZ, NX, NY, NT = 8, 4, 4, 64
CAP = 3
B = 128
LM = 64
MESH = pl.DeviceIdType.MESH
F32, BF16 = jnp.float32, jnp.bfloat16


def route(row, col):
    shape = (B, B)
    down, across = lax.broadcasted_iota(jnp.int32, shape, 0), lax.broadcasted_iota(jnp.int32, shape, 1)

    def column(v):
        return jnp.sum(jnp.where(down == across, v, 0), axis=1, keepdims=True)

    owner = row // SOUND_DEV
    earlier = (column(owner) == owner) & (down < across)
    place = jnp.sum(earlier.astype(jnp.int32), axis=0, keepdims=True)
    slot = column(owner * CAP + place)
    index = lax.broadcasted_iota(jnp.int32, (B, 2 * B), 0)
    at = lax.broadcasted_iota(jnp.int32, (B, 2 * B), 1)
    source = jnp.sum(jnp.where(slot == at, index, 0), axis=0, keepdims=True)
    blocks = (row - owner * SOUND_DEV) * 512 + col - SOUND_DEV * 512
    mine = lax.broadcasted_iota(jnp.int32, (NT, B), 0) == owner
    lane = lax.broadcasted_iota(jnp.int32, (NT, B), 1)
    coded = jnp.full((NT, B), SOUND_DEV * 512, jnp.int32)
    for k in range(CAP):
        found = jnp.sum(jnp.where(mine & (place == k), blocks, 0), axis=1, keepdims=True)
        coded = coded + jnp.where(lane == k, found, 0)
    return source, coded


SPREAD_ORDER = (
    ("T", 0), ("T", 1), ("T", 7), ("A0",), ("T", 2), ("T", 6), ("Y1", 0), ("Y1", 1), ("Y2", 0, 0),
    ("Y2", 1, 0), ("Z", 0, 1), ("X", 0, 0), ("X", 1, 0), ("Z", 1, 1), ("Y1", 7), ("Y2", 0, 1), ("Y2", 1, 1),
    ("T", 3), ("T", 5), ("X", 0, 7), ("X", 1, 7), ("Y1", 2), ("XL", 0), ("Y2", 0, 7), ("Y2", 1, 7),
    ("Z", 0, 2), ("X", 0, 1), ("X", 1, 1), ("Z", 1, 2), ("T", 4), ("Y1", 6), ("Y2", 0, 2), ("Y2", 1, 2),
    ("XL", 7), ("X", 0, 6), ("X", 1, 6), ("XL", 1), ("Y2", 0, 6), ("Y2", 1, 6), ("X", 0, 2), ("X", 1, 2),
    ("Y1", 3), ("Z", 0, 3), ("Z", 1, 3), ("Y1", 5), ("XL", 6), ("XL", 2), ("Y2", 0, 3), ("Y2", 1, 3),
    ("X", 0, 5), ("X", 1, 5), ("X", 0, 3), ("X", 1, 3), ("Y2", 0, 5), ("Y2", 1, 5), ("Y1", 4), ("Z", 0, 4),
    ("XL", 5), ("XL", 3), ("X", 0, 4), ("X", 1, 4), ("Y2", 0, 4), ("Y2", 1, 4), ("XL", 4),
)


def spread_kernel(
    row_h, col_h, footprints, prior_h, tiles, anoms, codes,
    row, col, source_v, source, coded, prior, quarter, staged, sums, shard,
    s_row, s_fp, s_prior, s_sum, r_sum, s_tile, r_tile, s_code, r_code, s_y, r_y, s_y2, r_y2,
    s_local, s_z, r_z, s_x, r_x, s_x2, r_x2, s_sib, r_sib, came,
):
    me = lax.axis_index("tile")
    q = lax.axis_index("mem")
    core = lax.rem(me, 2)
    x = lax.rem(me // 2, NX)
    z = me // 8

    def at_z(o):
        return lax.rem(z + o + NZ, NZ)

    def at_x(o):
        return lax.rem(x + o + NX, NX)

    def at_y(o):
        return lax.rem(q + o + NY, NY)

    def index(zz, xx, cc):
        return zz * 8 + xx * 2 + cc

    def remote(src, dst, ssem, rsem, tile=None, mem=None):
        return pltpu.make_async_remote_copy(
            src_ref=src, dst_ref=dst, send_sem=ssem, recv_sem=rsem,
            device_id={"tile": me if tile is None else tile, "mem": q if mem is None else mem},
            device_id_type=MESH,
        )

    def wait_for(ref, sem):
        pltpu.make_async_copy(ref, ref, sem).wait()

    row_copy = pltpu.make_async_copy(row_h, row, s_row.at[0])
    row_copy.start()
    col_copy = pltpu.make_async_copy(col_h, col, s_row.at[1])
    col_copy.start()
    prior_copy = pltpu.make_async_copy(prior_h, prior, s_prior)
    prior_copy.start()
    fp_copy = pltpu.make_async_copy(
        footprints.at[:, pl.ds(pl.multiple_of(q * 32, 32), 32), :], quarter, s_fp
    )
    fp_copy.start()

    barrier = pltpu.get_barrier_semaphore()
    for o in range(1, 8):
        pl.semaphore_signal(
            barrier, inc=1, device_id={"tile": z * 8 + lax.rem(me + o, 8), "mem": q}, device_id_type=MESH
        )
    for o in range(1, NY):
        pl.semaphore_signal(barrier, inc=1, device_id={"tile": me, "mem": at_y(o)}, device_id_type=MESH)
    for o in (1, -1):
        pl.semaphore_signal(
            barrier, inc=1, device_id={"tile": index(at_z(o), x, core), "mem": q}, device_id_type=MESH
        )

    def tell(stage):
        for i, o in enumerate((1, -1)):
            pl.semaphore_signal(
                came.at[i, stage], inc=1, device_id={"tile": index(at_z(o), x, core), "mem": q}, device_id_type=MESH
            )

    def hear(stage):
        for i in range(2):
            pl.semaphore_wait(came.at[i, stage], 1)

    row_copy.wait()
    col_copy.wait()
    source_row, coded_rows = route(row[...], col[...])
    source_v[...] = source_row
    source_copy = pltpu.make_async_copy(source_v, source, s_row.at[2])
    source_copy.start()
    for t in range(NT):
        coded[t] = coded_rows[t : t + 1]
    prior_copy.wait()
    for j in range(FLUX_DEV):
        part = jnp.sum(prior[:, j * B : (j + 1) * B].astype(F32), axis=0, keepdims=True)
        sums[0, j : j + 1, :] = part
    pl.semaphore_wait(barrier, 7 + NY - 1 + 2)
    tell(1)

    sum_sends = []
    for o in range(1, NY):
        cp = remote(sums.at[0], sums.at[o], s_sum.at[o], r_sum.at[o], mem=at_y(o))
        cp.start()
        sum_sends.append(cp)
    fp_copy.wait()
    source_copy.wait()

    def send_tiles(dz):
        first = 1 if dz == 0 else 0
        if 1 <= dz <= 4:
            hear(dz)
            if dz < 4:
                tell(dz + 1)

        @pl.loop(first, 8)
        def _(o):
            t = at_z(dz) * 8 + lax.rem(me + o, 8)
            for s in range(CAP):
                staged[t, s] = quarter[source[0, t * CAP + s]]
            remote(staged.at[t], tiles.at[q, me], s_tile, r_tile.at[dz], tile=t).start()
            remote(coded.at[t], codes.at[me], s_code, r_code, tile=t).start()

        if dz == 0:
            for s in range(CAP):
                staged[me, s] = quarter[source[0, me * CAP + s]]
            pltpu.make_async_copy(staged.at[me], tiles.at[q, me], r_tile.at[0]).start()
            pltpu.make_async_copy(coded.at[me], codes.at[me], r_code).start()

    def group(quarter_index, dz, first=0, size=8):
        zs = at_z(-dz)
        return tiles.at[quarter_index, pl.ds(zs * 8 + first, size)]

    pending = []

    def go(cp):
        cp.start()
        pending.append(cp)

    def y_first(dz):
        wait_for(group(q, dz), r_tile.at[dz])
        for late in range(2):
            for i, to in enumerate((1, -1)):
                h = (i + late) % 2
                half = group(q, dz, 4 * h, 4)
                go(remote(half, half, s_y.at[i, h, dz], r_y.at[i, h, dz], mem=at_y(to)))

    def y_second(i, dz):
        from_, to = ((-1, 1), (1, -1))[i]
        half = group(at_y(from_), dz, 4 * i, 4)
        wait_for(half, r_y.at[i, i, dz])
        go(remote(half, half, s_y2.at[i, dz], r_y2.at[i, dz], mem=at_y(to)))

    def y_last(dz):
        for i in range(2):
            wait_for(group(at_y((-1, 1)[i]), dz, 4 - 4 * i, 4), r_y.at[i, 1 - i, dz])
            wait_for(group(at_y(2), dz, 4 * i, 4), r_y2.at[i, dz])

    def block(oz, ox, own_core=True):
        return anoms.at[index(at_z(oz), at_x(ox), core if own_core else 1 - core)]

    def to_sibling(oz, ox):
        go(
            remote(
                block(oz, ox), block(oz, ox), s_sib.at[ox % NX, oz % NZ], r_sib.at[ox % NX, oz % NZ],
                tile=index(z, x, 1 - core),
            )
        )

    def x_first(oz, src=None):
        b = block(oz, 0)
        src = b if src is None else src
        k = oz % NZ
        for late in range(2):
            for i, to in enumerate((1, -1)):
                h = (i + late) % 2
                part = pl.ds(4 * h, 4)
                go(remote(src.at[part], b.at[part], s_x.at[i, h, k], r_x.at[i, h, k], tile=index(z, at_x(to), core)))
        go(remote(src, b, s_sib.at[0, k], r_sib.at[0, k], tile=index(z, x, 1 - core)))

    def x_second(i, oz):
        k = oz % NZ
        from_, to = ((-1, 1), (1, -1))[i]
        half = block(oz, from_).at[pl.ds(4 * i, 4)]
        wait_for(half, r_x.at[i, i, k])
        go(remote(half, half, s_x2.at[i, k], r_x2.at[i, k], tile=index(z, at_x(to), core)))

    def x_last(oz):
        k = oz % NZ
        for i, from_ in enumerate((-1, 1)):
            wait_for(block(oz, from_).at[pl.ds(4 - 4 * i, 4)], r_x.at[i, 1 - i, k])
            to_sibling(oz, from_)
        for i in range(2):
            wait_for(block(oz, 2).at[pl.ds(4 * i, 4)], r_x2.at[i, k])
        to_sibling(oz, 2)

    def z_step(i, k):
        if k < 4:
            b = block((-k, k)[i], 0)
            wait_for(b, r_z.at[i, k])
            h = b if k < 3 else b.at[pl.ds(4 * i, 4)]
            go(remote(h, h, s_z.at[i, k + 1], r_z.at[i, k + 1], tile=index(at_z((1, -1)[i]), x, core)))
            x_first((-k, k)[i])
        else:
            b = block(4, 0)
            wait_for(b.at[pl.ds(0, 4)], r_z.at[0, 4])
            wait_for(b.at[pl.ds(4, 4)], r_z.at[1, 4])
            x_first(4)

    own_copy = pltpu.make_async_copy(shard, anoms.at[me], s_local)

    def send_shard():
        for cp in sum_sends:
            cp.wait()
        mean = (sums[0] + sums[1] + sums[2] + sums[3]) / MEMBERS
        for j in range(FLUX_DEV):
            shard[j] = (prior[:, j * B : (j + 1) * B].astype(F32) - mean[j : j + 1, :]).astype(BF16)
        own_copy.start()
        go(remote(shard, anoms.at[me], s_z.at[0, 1], r_z.at[0, 1], tile=index(at_z(1), x, core)))
        go(remote(shard, anoms.at[me], s_z.at[1, 1], r_z.at[1, 1], tile=index(at_z(-1), x, core)))
        x_first(0, shard)

    acts = {
        "T": send_tiles, "A0": send_shard, "Z": z_step, "X": x_second, "XL": x_last, "Y1": y_first, "Y2": y_second
    }
    for name, *numbers in SPREAD_ORDER:
        while len(pending) > 40:
            pending.pop(0).wait_send()
        acts[name](*numbers)
    for dz in (0, 1, 7, 2, 6, 3, 5, 4):
        y_last(dz)
    for oz in (0, 1, 7, 2, 6, 3, 5, 4):
        for ox in range(NX):
            wait_for(block(oz, ox, False), r_sib.at[ox, oz])
    wait_for(codes, r_code)
    own_copy.wait()
    for cp in pending:
        cp.wait_send()
    wait_for(staged.at[pl.ds(0, NT - 1)], s_tile)
    wait_for(codes.at[pl.ds(0, NT - 1)], s_code)


def spread(tile_row, tile_col, footprints, prior):
    hbm = pl.BlockSpec(memory_space=pltpu.HBM)
    vmem = pl.BlockSpec(memory_space=pltpu.VMEM)
    dma = pltpu.SemaphoreType.DMA
    return pl.pallas_call(
        spread_kernel,
        out_shape=(
            jax.ShapeDtypeStruct((NY, NT, CAP, 32, B), BF16),
            jax.ShapeDtypeStruct((NT, FLUX_DEV, LM, B), BF16),
            jax.ShapeDtypeStruct((NT, 1, B), jnp.int32),
        ),
        in_specs=[hbm, hbm, hbm, hbm],
        out_specs=(vmem, vmem, vmem),
        scratch_shapes=[
            pltpu.VMEM((1, B), jnp.int32),
            pltpu.VMEM((1, B), jnp.int32),
            pltpu.VMEM((1, 2 * B), jnp.int32),
            pltpu.SMEM((1, 2 * B), jnp.int32),
            pltpu.VMEM((NT, 1, B), jnp.int32),
            pltpu.VMEM((LM, FLUX_DEV * B), BF16),
            pltpu.VMEM((B, 32, B), BF16),
            pltpu.VMEM((NT, CAP, 32, B), BF16),
            pltpu.VMEM((NY, FLUX_DEV, B), F32),
            pltpu.VMEM((FLUX_DEV, LM, B), BF16),
            dma((3,)), dma, dma, dma((NY,)), dma((NY,)), dma, dma((NZ,)), dma, dma,
            dma((2, 2, NZ)), dma((2, 2, NZ)), dma((2, NZ)), dma((2, NZ)),
            dma, dma((2, 5)), dma((2, 5)), dma((2, 2, NZ)), dma((2, 2, NZ)), dma((2, NZ)), dma((2, NZ)),
            dma((NX, NZ)), dma((NX, NZ)), pltpu.SemaphoreType.REGULAR((2, 5)),
        ],
        compiler_params=pltpu.CompilerParams(
            collective_id=0, has_side_effects=True, vmem_limit_bytes=16 * 2**20
        ),
        name="spread",
    )(tile_row, tile_col, footprints, prior)


def local_kernel(
    codes_v, tiles, anoms, observed_h, weight_h, out,
    codes, s_codes, observed, weight, modelled, weighted, total, s_obs, s_weight,
):
    codes_in = pltpu.make_async_copy(codes_v, codes, s_codes)
    codes_in.start()
    observed_in = pltpu.make_async_copy(observed_h, observed, s_obs)
    observed_in.start()
    weight_in = pltpu.make_async_copy(weight_h, weight, s_weight)
    weight_in.start()
    modelled[...] = jnp.zeros_like(modelled)

    @pl.loop(0, NT)
    def _(i):
        total[pl.ds(i * 8, 8)] = jnp.zeros((8, LM, B), F32)

    codes_in.wait()
    step = 32

    def fetch(i, o, s):
        src = i * step + o
        code = codes[src, 0, s]
        return tiles[:, src, s].reshape(B, B), code // 512, lax.rem(code, 512)

    @pl.loop(0, NT // step)
    def _(i):
        terms = []
        for o in range(step):
            for s in range(CAP):
                tile, row, col = fetch(i, o, s)
                term = lax.dot_general(
                    anoms[col], tile, (((1,), (1,)), ((), ())), preferred_element_type=F32
                )
                terms.append((row, term))
        for row, term in terms:
            modelled[row] += term

    observed_in.wait()
    weight_in.wait()
    for r in range(SOUND_DEV):
        factor = weight[r].astype(F32) / 8.0
        gap = modelled[r] - observed[:, r * B : (r + 1) * B]
        weighted[r] = (factor * gap).astype(BF16)
    weighted[SOUND_DEV] = jnp.zeros((LM, B), BF16)

    @pl.loop(0, NT // step)
    def _(i):
        terms = []
        for o in range(step):
            for s in range(CAP):
                tile, row, col = fetch(i, o, s)
                term = lax.dot_general(
                    weighted[row], tile, (((1,), (0,)), ((), ())), preferred_element_type=F32
                )
                terms.append((col, term))
        for col, term in terms:
            total[col] += term

    @pl.loop(0, NT // 4)
    def _(i):
        out[pl.ds(i * 32, 32)] = total[pl.ds(i * 32, 32)].astype(BF16)


def local(codes, tiles, anoms, observed, weight):
    hbm = pl.BlockSpec(memory_space=pltpu.HBM)
    vmem = pl.BlockSpec(memory_space=pltpu.VMEM)
    dma = pltpu.SemaphoreType.DMA
    return pl.pallas_call(
        local_kernel,
        out_shape=jax.ShapeDtypeStruct((NT * FLUX_DEV, LM, B), BF16),
        in_specs=[vmem, vmem, vmem, hbm, hbm],
        out_specs=vmem,
        scratch_shapes=[
            pltpu.SMEM((NT, 1, B), jnp.int32),
            dma,
            pltpu.VMEM((LM, SOUND_DEV * B), F32),
            pltpu.VMEM((SOUND_DEV, 1, B), jnp.int32),
            pltpu.VMEM((SOUND_DEV + 1, LM, B), F32),
            pltpu.VMEM((SOUND_DEV + 1, LM, B), BF16),
            pltpu.VMEM((NT * FLUX_DEV, LM, B), F32),
            dma, dma,
        ],
        compiler_params=pltpu.CompilerParams(vmem_limit_bytes=22 * 2**20),
        name="local",
    )(codes, tiles, anoms.reshape(NT * FLUX_DEV, LM, B), observed, weight)


NA = 5
NB = FLUX_DEV - NA
FAR_X = ((4, 3, 2, 1), (5, 6, 7, 0))
NEAR_X = (4, 5, 3, 6, 2, 7, 1, 0)
FAR_Z = ((2, 1), (3, 0))
NEAR_Z = (2, 1, 3, 0)

GATHER_ORDER = (
    ("b_far", 0), ("b_far", 1), ("a_far", 0), ("a_far", 1), ("a_far", 2), ("a_far", 3), ("b_near", 1, 0),
    ("b_near", 1, 2), ("a_near", 0), ("b_near", 1, 1), ("b_near", 1, 3), ("a_near", 1), ("b_near", 2, 0),
    ("b_near", 2, 2), ("a_near", 2), ("b_near", 2, 1), ("a_near", 3), ("b_near", 2, 3), ("b_near", 3, 0),
    ("a_own", 4), ("a_near", 4), ("b_near", 3, 1), ("a_near", 5), ("b_near", 3, 2), ("b_own", 2),
    ("a_own", 5), ("a_own", 3), ("a_near", 6), ("b_near", 3, 3), ("a_near", 7), ("a_own", 6), ("a_own", 2),
    ("b_own", 3), ("b_own", 1), ("a_own", 7), ("a_own", 1), ("b_own", 0), ("a_own", 0),
)


def gather_kernel(
    part, out,
    pa, pb, ra, rb, xa1, xa2, zb1, zb2, za1, za2, xb1, xb2,
    s_sib_a, r_sib_a, s_sib_b, r_sib_b, s_a2, r_a2, s_b4, r_b4,
    s_xa1, r_xa1, s_xa2, r_xa2, s_zb1, r_zb1, s_zb2, r_zb2, s_za, r_za, s_xb, r_xb,
):
    me = lax.axis_index("tile")
    q = lax.axis_index("mem")
    core = lax.rem(me, 2)
    x = lax.rem(me // 2, NX)
    z = me // 8

    def at_z(o):
        return lax.rem(z + o + NZ, NZ)

    def at_x(o):
        return lax.rem(x + o + NX, NX)

    def index(zz, xx, cc):
        return zz * 8 + xx * 2 + cc

    sibling = index(z, x, 1 - core)
    x_next = (index(z, at_x(1), core), index(z, at_x(-1), core))
    z_next = (index(at_z(1), x, core), index(at_z(-1), x, core))

    pending = []

    def send(src, dst, ssem, rsem, tile):
        cp = pltpu.make_async_remote_copy(
            src_ref=src, dst_ref=dst, send_sem=ssem, recv_sem=rsem,
            device_id={"tile": tile, "mem": q}, device_id_type=MESH,
        )
        cp.start()
        pending.append(cp)

    def wait_for(ref, sem):
        pltpu.make_async_copy(ref, ref, sem).wait()

    barrier = pltpu.get_barrier_semaphore()
    for t in (sibling, *x_next, *z_next):
        pl.semaphore_signal(barrier, inc=1, device_id={"tile": t, "mem": q}, device_id_type=MESH)
    pl.semaphore_wait(barrier, 5)

    for ox in NEAR_Z:
        xx = at_x(ox)
        send(part.at[at_z(4), xx, 1 - core, pl.ds(NA, NB)], rb.at[4, xx], s_b4.at[ox], r_b4.at[ox], sibling)
    for oz in NEAR_X:
        zz = at_z(oz)
        send(part.at[zz, at_x(2), 1 - core, pl.ds(0, NA)], ra.at[2, zz], s_a2.at[oz], r_a2.at[oz], sibling)
    for kind, d in (("b", 3), ("b", 5), ("a", 1), ("a", 3), ("b", 2), ("b", 6), ("b", 1), ("b", 7), ("a", 0), ("b", 0)):
        if kind == "a":
            send(part.at[:, at_x(d), 1 - core, pl.ds(0, NA)], ra.at[d], s_sib_a.at[d], r_sib_a.at[d], sibling)
        else:
            send(part.at[at_z(d), :, 1 - core, pl.ds(NA, NB)], rb.at[d], s_sib_b.at[d], r_sib_b.at[d], sibling)

    settled = set()

    def from_a(d, zz):
        if ("a", d) not in settled:
            settled.add(("a", d))
            if d != 2:
                wait_for(ra.at[d], r_sib_a.at[d])
        return [part.at[zz, at_x(d), core], ra.at[d, zz]]

    def from_b(d, xx):
        if ("b", d) not in settled:
            settled.add(("b", d))
            if d != 4:
                wait_for(rb.at[d], r_sib_b.at[d])
        return [part.at[at_z(d), xx, core, pl.ds(NA, NB)], rb.at[d, xx]]

    def total(dst, sources, first, last):
        @pl.loop(first, last)
        def _(b):
            value = None
            for s in sources:
                ref, start = s if isinstance(s, tuple) else (s, 0)
                v = ref[b - start].astype(F32)
                value = v if value is None else value + v
            dst[b] = value.astype(BF16)

    def result(base, sources, count):
        for b in range(count):
            value = None
            for s in sources:
                v = s[b].astype(F32)
                value = v if value is None else value + v
            out[:, (base + b) * B : (base + b + 1) * B] = value

    def a_far(k):
        for i in range(2):
            zz = at_z(FAR_X[i][k])
            wait_for(ra.at[2, zz], r_a2.at[FAR_X[i][k]])
            total(pa.at[2, zz], from_a(2, zz), 0, NA)
            send(pa.at[2, zz], xa1.at[i, k], s_xa1.at[i, k], r_xa1.at[i, k], x_next[i])

    def a_near(j):
        oz = NEAR_X[j]
        zz = at_z(oz)
        for i, d in enumerate((1, 3)):
            sources = from_a(d, zz)
            if oz in FAR_X[i]:
                k = FAR_X[i].index(oz)
                wait_for(xa1.at[i, k], r_xa1.at[i, k])
                sources.append(xa1.at[i, k])
            total(pa.at[d, zz], sources, 0, NA)
            send(pa.at[d, zz], xa2.at[i, j], s_xa2.at[i, j], r_xa2.at[i, j], x_next[i])

    half_a, half_b = (NA + 1) // 2, (NB + 1) // 2

    def a_own(oz):
        j = NEAR_X.index(oz)
        zz = at_z(oz)
        for i in range(2):
            wait_for(xa2.at[i, j], r_xa2.at[i, j])
        sources = [*from_a(0, zz), xa2.at[0, j], xa2.at[1, j]]
        mine = pa.at[0, zz]
        if oz == 4:
            total(mine, sources, 0, NA)
            for i, (first, size) in enumerate(((0, half_a), (half_a, NA - half_a))):
                piece = za1.at[pl.ds(first, size)]
                send(mine.at[pl.ds(first, size)], piece, s_za.at[i, 0], r_za.at[i, 0], z_next[i])
        elif oz in (3, 5):
            i = (3, 5).index(oz)
            first, size = ((0, half_a), (half_a, NA - half_a))[i]
            wait_for(za1.at[pl.ds(first, size)], r_za.at[i, 0])
            total(mine, [*sources, za1], first, first + size)
            total(mine, sources, *((half_a, NA), (0, half_a))[i])
            send(mine, za2.at[i, 0], s_za.at[i, 1], r_za.at[i, 1], z_next[i])
        elif oz != 0:
            i = 0 if oz < 4 else 1
            step = 4 - oz if i == 0 else oz - 4
            wait_for(za2.at[i, step - 2], r_za.at[i, step - 1])
            total(mine, [*sources, za2.at[i, step - 2]], 0, NA)
            send(mine, za2.at[i, step - 1], s_za.at[i, step], r_za.at[i, step], z_next[i])
        else:
            for i in range(2):
                wait_for(za2.at[i, 2], r_za.at[i, 3])
            result(0, [*sources, za2.at[0, 2], za2.at[1, 2]], NA)

    def b_far(k):
        for i in range(2):
            xx = at_x(FAR_Z[i][k])
            wait_for(rb.at[4, xx], r_b4.at[FAR_Z[i][k]])
            total(pb.at[4, xx], from_b(4, xx), 0, NB)
            send(pb.at[4, xx], zb1.at[i, k], s_zb1.at[i, k], r_zb1.at[i, k], z_next[i])

    def b_near(step, j):
        ox = NEAR_Z[j]
        xx = at_x(ox)
        for i, d in enumerate((4 - step, 4 + step)):
            sources = from_b(d, xx)
            if step > 1:
                wait_for(zb2.at[i, step - 2, j], r_zb2.at[i, step - 2, j])
                sources.append(zb2.at[i, step - 2, j])
            elif ox in FAR_Z[i]:
                k = FAR_Z[i].index(ox)
                wait_for(zb1.at[i, k], r_zb1.at[i, k])
                sources.append(zb1.at[i, k])
            total(pb.at[d, xx], sources, 0, NB)
            send(
                pb.at[d, xx], zb2.at[i, step - 1, j], s_zb2.at[i, step - 1, j], r_zb2.at[i, step - 1, j], z_next[i]
            )

    def b_own(ox):
        j = NEAR_Z.index(ox)
        xx = at_x(ox)
        for i in range(2):
            wait_for(zb2.at[i, 2, j], r_zb2.at[i, 2, j])
        sources = [*from_b(0, xx), zb2.at[0, 2, j], zb2.at[1, 2, j]]
        mine = pb.at[0, xx]
        halves = ((0, half_b), (half_b, NB - half_b))
        if ox == 2:
            total(mine, sources, 0, NB)
            for i, (first, size) in enumerate(halves):
                piece = xb1.at[pl.ds(first, size)]
                send(mine.at[pl.ds(first, size)], piece, s_xb.at[i, 0], r_xb.at[i, 0], x_next[i])
        elif ox != 0:
            i = (1, 3).index(ox)
            first, size = halves[i]
            wait_for(xb1.at[pl.ds(first, size)], r_xb.at[i, 0])
            total(mine, [*sources, xb1], first, first + size)
            total(mine, sources, *((half_b, NB), (0, half_b))[i])
            send(mine, xb2.at[i], s_xb.at[i, 1], r_xb.at[i, 1], x_next[i])
        else:
            for i in range(2):
                wait_for(xb2.at[i], r_xb.at[i, 1])
            result(NA, [*sources, xb2.at[0], xb2.at[1]], NB)

    acts = {"a_far": a_far, "a_near": a_near, "a_own": a_own, "b_far": b_far, "b_near": b_near, "b_own": b_own}
    for name, *numbers in GATHER_ORDER:
        while len(pending) > 30:
            pending.pop(0).wait_send()
        acts[name](*numbers)
    for cp in pending:
        cp.wait_send()


def gather(part):
    vmem = pl.BlockSpec(memory_space=pltpu.VMEM)
    dma = pltpu.SemaphoreType.DMA
    return pl.pallas_call(
        gather_kernel,
        out_shape=jax.ShapeDtypeStruct((LM, FLUX_DEV * B), F32),
        in_specs=[vmem],
        out_specs=vmem,
        scratch_shapes=[
            pltpu.VMEM((NX, NZ, NA, LM, B), BF16),
            pltpu.VMEM((NZ, NX, NB, LM, B), BF16),
            pltpu.VMEM((NX, NZ, NA, LM, B), BF16),
            pltpu.VMEM((NZ, NX, NB, LM, B), BF16),
            pltpu.VMEM((2, 4, NA, LM, B), BF16),
            pltpu.VMEM((2, NZ, NA, LM, B), BF16),
            pltpu.VMEM((2, 2, NB, LM, B), BF16),
            pltpu.VMEM((2, 3, NX, NB, LM, B), BF16),
            pltpu.VMEM((NA, LM, B), BF16),
            pltpu.VMEM((2, 3, NA, LM, B), BF16),
            pltpu.VMEM((NB, LM, B), BF16),
            pltpu.VMEM((2, NB, LM, B), BF16),
            dma((NX,)), dma((NX,)), dma((NZ,)), dma((NZ,)), dma((NZ,)), dma((NZ,)), dma((NX,)), dma((NX,)),
            dma((2, 4)), dma((2, 4)), dma((2, NZ)), dma((2, NZ)),
            dma((2, 2)), dma((2, 2)), dma((2, 3, NX)), dma((2, 3, NX)),
            dma((2, 4)), dma((2, 4)), dma((2, 2)), dma((2, 2)),
        ],
        compiler_params=pltpu.CompilerParams(
            collective_id=1, has_side_effects=True, vmem_limit_bytes=18 * 2**20
        ),
        name="gather",
    )(part.reshape(NZ, NX, 2, FLUX_DEV, LM, B))


def body(footprints, tile_row, tile_col, prior_flux, observed, precision_weight):
    pin = functools.partial(pltpu.with_memory_space_constraint, memory_space=pltpu.HBM)
    footprints, prior_flux, observed = pin(footprints), pin(prior_flux), pin(observed)
    tile_row, tile_col = pin(tile_row.reshape(1, B)), pin(tile_col.reshape(1, B))
    tiles, anoms, codes = spread(tile_row, tile_col, footprints, prior_flux)
    weight = pin(precision_weight.reshape(SOUND_DEV, 1, B))
    part = local(codes, tiles, anoms, observed, weight)
    return gather(part)


def solution(mesh):
    in_specs = (
        P("tile", None, None),
        P("tile"),
        P("tile"),
        P("mem", "tile"),
        P("mem", "tile"),
        P("tile"),
    )
    out_specs = P("mem", "tile")
    return jax.shard_map(body, mesh=mesh, in_specs=in_specs, out_specs=out_specs, check_vma=False)
```

```python
import functools

import jax
import jax.numpy as jnp
from jax import lax
from jax.experimental import pallas as pl
from jax.experimental.pallas import tpu as pltpu
from jax.sharding import PartitionSpec as P

MEMBERS = 256
FLUX_DEV = 8
SOUND_DEV = 16
NZ, NX, NY, NT = 8, 4, 4, 64
CAP = 3
B = 128
LM = 64
MESH = pl.DeviceIdType.MESH
F32, BF16 = jnp.float32, jnp.bfloat16


def route(row, col):
    shape = (B, B)
    down, across = lax.broadcasted_iota(jnp.int32, shape, 0), lax.broadcasted_iota(jnp.int32, shape, 1)

    def column(v):
        return jnp.sum(jnp.where(down == across, v, 0), axis=1, keepdims=True)

    owner = row // SOUND_DEV
    earlier = (column(owner) == owner) & (down < across)
    place = jnp.sum(earlier.astype(jnp.int32), axis=0, keepdims=True)
    slot = column(owner * CAP + place)
    index = lax.broadcasted_iota(jnp.int32, (B, 2 * B), 0)
    at = lax.broadcasted_iota(jnp.int32, (B, 2 * B), 1)
    source = jnp.sum(jnp.where(slot == at, index, 0), axis=0, keepdims=True)
    blocks = (row - owner * SOUND_DEV) * 512 + col - SOUND_DEV * 512
    mine = lax.broadcasted_iota(jnp.int32, (NT, B), 0) == owner
    lane = lax.broadcasted_iota(jnp.int32, (NT, B), 1)
    coded = jnp.full((NT, B), SOUND_DEV * 512, jnp.int32)
    for k in range(CAP):
        found = jnp.sum(jnp.where(mine & (place == k), blocks, 0), axis=1, keepdims=True)
        coded = coded + jnp.where(lane == k, found, 0)
    return source, coded


SPREAD_ORDER = (
    ("T", 0), ("T", 1), ("T", 7), ("A0",), ("T", 2), ("T", 6), ("Y1", 0), ("Y1", 1), ("Y2", 0, 0),
    ("Y2", 1, 0), ("Z", 0, 1), ("X", 0, 0), ("X", 1, 0), ("Z", 1, 1), ("Y1", 7), ("Y2", 0, 1), ("Y2", 1, 1),
    ("T", 3), ("T", 5), ("X", 0, 7), ("X", 1, 7), ("Y1", 2), ("XL", 0), ("Y2", 0, 7), ("Y2", 1, 7),
    ("Z", 0, 2), ("X", 0, 1), ("X", 1, 1), ("Z", 1, 2), ("T", 4), ("Y1", 6), ("Y2", 0, 2), ("Y2", 1, 2),
    ("XL", 7), ("X", 0, 6), ("X", 1, 6), ("XL", 1), ("Y2", 0, 6), ("Y2", 1, 6), ("X", 0, 2), ("X", 1, 2),
    ("Y1", 3), ("Z", 0, 3), ("Z", 1, 3), ("Y1", 5), ("XL", 6), ("XL", 2), ("Y2", 0, 3), ("Y2", 1, 3),
    ("X", 0, 5), ("X", 1, 5), ("X", 0, 3), ("X", 1, 3), ("Y2", 0, 5), ("Y2", 1, 5), ("Y1", 4), ("Z", 0, 4),
    ("XL", 5), ("XL", 3), ("X", 0, 4), ("X", 1, 4), ("Y2", 0, 4), ("Y2", 1, 4), ("XL", 4),
)


def spread_kernel(
    row_h, col_h, footprints, prior_h, tiles, anoms, codes,
    row, col, source_v, source, coded, prior, quarter, staged, sums, shard,
    s_row, s_fp, s_prior, s_sum, r_sum, s_tile, r_tile, s_code, r_code, s_y, r_y, s_y2, r_y2,
    s_local, s_z, r_z, s_x, r_x, s_x2, r_x2, s_sib, r_sib, came,
):
    me = lax.axis_index("tile")
    q = lax.axis_index("mem")
    core = lax.rem(me, 2)
    x = lax.rem(me // 2, NX)
    z = me // 8

    def at_z(o):
        return lax.rem(z + o + NZ, NZ)

    def at_x(o):
        return lax.rem(x + o + NX, NX)

    def at_y(o):
        return lax.rem(q + o + NY, NY)

    def index(zz, xx, cc):
        return zz * 8 + xx * 2 + cc

    def remote(src, dst, ssem, rsem, tile=None, mem=None):
        return pltpu.make_async_remote_copy(
            src_ref=src, dst_ref=dst, send_sem=ssem, recv_sem=rsem,
            device_id={"tile": me if tile is None else tile, "mem": q if mem is None else mem},
            device_id_type=MESH,
        )

    def wait_for(ref, sem):
        pltpu.make_async_copy(ref, ref, sem).wait()

    row_copy = pltpu.make_async_copy(row_h, row, s_row.at[0])
    row_copy.start()
    col_copy = pltpu.make_async_copy(col_h, col, s_row.at[1])
    col_copy.start()
    prior_copy = pltpu.make_async_copy(prior_h, prior, s_prior)
    prior_copy.start()
    fp_copy = pltpu.make_async_copy(
        footprints.at[:, pl.ds(pl.multiple_of(q * 32, 32), 32), :], quarter, s_fp
    )
    fp_copy.start()

    barrier = pltpu.get_barrier_semaphore()
    for o in range(1, 8):
        pl.semaphore_signal(
            barrier, inc=1, device_id={"tile": z * 8 + lax.rem(me + o, 8), "mem": q}, device_id_type=MESH
        )
    for o in range(1, NY):
        pl.semaphore_signal(barrier, inc=1, device_id={"tile": me, "mem": at_y(o)}, device_id_type=MESH)
    for o in (1, -1):
        pl.semaphore_signal(
            barrier, inc=1, device_id={"tile": index(at_z(o), x, core), "mem": q}, device_id_type=MESH
        )

    def tell(stage):
        for i, o in enumerate((1, -1)):
            pl.semaphore_signal(
                came.at[i, stage], inc=1, device_id={"tile": index(at_z(o), x, core), "mem": q}, device_id_type=MESH
            )

    def hear(stage):
        for i in range(2):
            pl.semaphore_wait(came.at[i, stage], 1)

    row_copy.wait()
    col_copy.wait()
    source_row, coded_rows = route(row[...], col[...])
    source_v[...] = source_row
    source_copy = pltpu.make_async_copy(source_v, source, s_row.at[2])
    source_copy.start()
    for t in range(NT):
        coded[t] = coded_rows[t : t + 1]
    prior_copy.wait()
    for j in range(FLUX_DEV):
        part = jnp.sum(prior[:, j * B : (j + 1) * B].astype(F32), axis=0, keepdims=True)
        sums[0, j : j + 1, :] = part
    pl.semaphore_wait(barrier, 7 + NY - 1 + 2)
    tell(1)

    sum_sends = []
    for o in range(1, NY):
        cp = remote(sums.at[0], sums.at[o], s_sum.at[o], r_sum.at[o], mem=at_y(o))
        cp.start()
        sum_sends.append(cp)
    fp_copy.wait()
    source_copy.wait()

    def send_tiles(dz):
        first = 1 if dz == 0 else 0
        if 1 <= dz <= 4:
            hear(dz)
            if dz < 4:
                tell(dz + 1)

        @pl.loop(first, 8)
        def _(o):
            t = at_z(dz) * 8 + lax.rem(me + o, 8)
            for s in range(CAP):
                staged[t, s] = quarter[source[0, t * CAP + s]]
            remote(staged.at[t], tiles.at[q, me], s_tile, r_tile.at[dz], tile=t).start()
            remote(coded.at[t], codes.at[me], s_code, r_code, tile=t).start()

        if dz == 0:
            for s in range(CAP):
                staged[me, s] = quarter[source[0, me * CAP + s]]
            pltpu.make_async_copy(staged.at[me], tiles.at[q, me], r_tile.at[0]).start()
            pltpu.make_async_copy(coded.at[me], codes.at[me], r_code).start()

    def group(quarter_index, dz, first=0, size=8):
        zs = at_z(-dz)
        return tiles.at[quarter_index, pl.ds(zs * 8 + first, size)]

    pending = []

    def go(cp):
        cp.start()
        pending.append(cp)

    def y_first(dz):
        wait_for(group(q, dz), r_tile.at[dz])
        for late in range(2):
            for i, to in enumerate((1, -1)):
                h = (i + late) % 2
                half = group(q, dz, 4 * h, 4)
                go(remote(half, half, s_y.at[i, h, dz], r_y.at[i, h, dz], mem=at_y(to)))

    def y_second(i, dz):
        from_, to = ((-1, 1), (1, -1))[i]
        half = group(at_y(from_), dz, 4 * i, 4)
        wait_for(half, r_y.at[i, i, dz])
        go(remote(half, half, s_y2.at[i, dz], r_y2.at[i, dz], mem=at_y(to)))

    def y_last(dz):
        for i in range(2):
            wait_for(group(at_y((-1, 1)[i]), dz, 4 - 4 * i, 4), r_y.at[i, 1 - i, dz])
            wait_for(group(at_y(2), dz, 4 * i, 4), r_y2.at[i, dz])

    def block(oz, ox, own_core=True):
        return anoms.at[index(at_z(oz), at_x(ox), core if own_core else 1 - core)]

    def to_sibling(oz, ox):
        go(
            remote(
                block(oz, ox), block(oz, ox), s_sib.at[ox % NX, oz % NZ], r_sib.at[ox % NX, oz % NZ],
                tile=index(z, x, 1 - core),
            )
        )

    def x_first(oz, src=None):
        b = block(oz, 0)
        src = b if src is None else src
        k = oz % NZ
        for late in range(2):
            for i, to in enumerate((1, -1)):
                h = (i + late) % 2
                part = pl.ds(4 * h, 4)
                go(remote(src.at[part], b.at[part], s_x.at[i, h, k], r_x.at[i, h, k], tile=index(z, at_x(to), core)))
        go(remote(src, b, s_sib.at[0, k], r_sib.at[0, k], tile=index(z, x, 1 - core)))

    def x_second(i, oz):
        k = oz % NZ
        from_, to = ((-1, 1), (1, -1))[i]
        half = block(oz, from_).at[pl.ds(4 * i, 4)]
        wait_for(half, r_x.at[i, i, k])
        go(remote(half, half, s_x2.at[i, k], r_x2.at[i, k], tile=index(z, at_x(to), core)))

    def x_last(oz):
        k = oz % NZ
        for i, from_ in enumerate((-1, 1)):
            wait_for(block(oz, from_).at[pl.ds(4 - 4 * i, 4)], r_x.at[i, 1 - i, k])
            to_sibling(oz, from_)
        for i in range(2):
            wait_for(block(oz, 2).at[pl.ds(4 * i, 4)], r_x2.at[i, k])
        to_sibling(oz, 2)

    def z_step(i, k):
        if k < 4:
            b = block((-k, k)[i], 0)
            wait_for(b, r_z.at[i, k])
            h = b if k < 3 else b.at[pl.ds(4 * i, 4)]
            go(remote(h, h, s_z.at[i, k + 1], r_z.at[i, k + 1], tile=index(at_z((1, -1)[i]), x, core)))
            x_first((-k, k)[i])
        else:
            b = block(4, 0)
            wait_for(b.at[pl.ds(0, 4)], r_z.at[0, 4])
            wait_for(b.at[pl.ds(4, 4)], r_z.at[1, 4])
            x_first(4)

    own_copy = pltpu.make_async_copy(shard, anoms.at[me], s_local)

    def send_shard():
        for cp in sum_sends:
            cp.wait()
        mean = (sums[0] + sums[1] + sums[2] + sums[3]) / MEMBERS
        for j in range(FLUX_DEV):
            shard[j] = (prior[:, j * B : (j + 1) * B].astype(F32) - mean[j : j + 1, :]).astype(BF16)
        own_copy.start()
        go(remote(shard, anoms.at[me], s_z.at[0, 1], r_z.at[0, 1], tile=index(at_z(1), x, core)))
        go(remote(shard, anoms.at[me], s_z.at[1, 1], r_z.at[1, 1], tile=index(at_z(-1), x, core)))
        x_first(0, shard)

    acts = {
        "T": send_tiles, "A0": send_shard, "Z": z_step, "X": x_second, "XL": x_last, "Y1": y_first, "Y2": y_second
    }
    for name, *numbers in SPREAD_ORDER:
        acts[name](*numbers)
    for dz in (0, 1, 7, 2, 6, 3, 5, 4):
        y_last(dz)
    for oz in (0, 1, 7, 2, 6, 3, 5, 4):
        for ox in range(NX):
            wait_for(block(oz, ox, False), r_sib.at[ox, oz])
    wait_for(codes, r_code)
    own_copy.wait()
    for cp in pending:
        cp.wait_send()
    wait_for(staged.at[pl.ds(0, NT - 1)], s_tile)
    wait_for(codes.at[pl.ds(0, NT - 1)], s_code)


def spread(tile_row, tile_col, footprints, prior):
    hbm = pl.BlockSpec(memory_space=pltpu.HBM)
    vmem = pl.BlockSpec(memory_space=pltpu.VMEM)
    dma = pltpu.SemaphoreType.DMA
    return pl.pallas_call(
        spread_kernel,
        out_shape=(
            jax.ShapeDtypeStruct((NY, NT, CAP, 32, B), BF16),
            jax.ShapeDtypeStruct((NT, FLUX_DEV, LM, B), BF16),
            jax.ShapeDtypeStruct((NT, 1, B), jnp.int32),
        ),
        in_specs=[hbm, hbm, hbm, hbm],
        out_specs=(vmem, vmem, vmem),
        scratch_shapes=[
            pltpu.VMEM((1, B), jnp.int32),
            pltpu.VMEM((1, B), jnp.int32),
            pltpu.VMEM((1, 2 * B), jnp.int32),
            pltpu.SMEM((1, 2 * B), jnp.int32),
            pltpu.VMEM((NT, 1, B), jnp.int32),
            pltpu.VMEM((LM, FLUX_DEV * B), BF16),
            pltpu.VMEM((B, 32, B), BF16),
            pltpu.VMEM((NT, CAP, 32, B), BF16),
            pltpu.VMEM((NY, FLUX_DEV, B), F32),
            pltpu.VMEM((FLUX_DEV, LM, B), BF16),
            dma((3,)), dma, dma, dma((NY,)), dma((NY,)), dma, dma((NZ,)), dma, dma,
            dma((2, 2, NZ)), dma((2, 2, NZ)), dma((2, NZ)), dma((2, NZ)),
            dma, dma((2, 5)), dma((2, 5)), dma((2, 2, NZ)), dma((2, 2, NZ)), dma((2, NZ)), dma((2, NZ)),
            dma((NX, NZ)), dma((NX, NZ)), pltpu.SemaphoreType.REGULAR((2, 5)),
        ],
        compiler_params=pltpu.CompilerParams(
            collective_id=0, has_side_effects=True, vmem_limit_bytes=16 * 2**20
        ),
        name="spread",
    )(tile_row, tile_col, footprints, prior)


def local_kernel(
    codes_v, tiles, anoms, observed_h, weight_h, out,
    codes, s_codes, observed, weight, modelled, weighted, total, s_obs, s_weight,
):
    codes_in = pltpu.make_async_copy(codes_v, codes, s_codes)
    codes_in.start()
    observed_in = pltpu.make_async_copy(observed_h, observed, s_obs)
    observed_in.start()
    weight_in = pltpu.make_async_copy(weight_h, weight, s_weight)
    weight_in.start()
    modelled[...] = jnp.zeros_like(modelled)

    @pl.loop(0, NT)
    def _(i):
        total[pl.ds(i * 8, 8)] = jnp.zeros((8, LM, B), F32)

    codes_in.wait()
    step = 32

    def fetch(i, o, s):
        src = i * step + o
        code = codes[src, 0, s]
        return tiles[:, src, s].reshape(B, B), code // 512, lax.rem(code, 512)

    @pl.loop(0, NT // step)
    def _(i):
        terms = []
        for o in range(step):
            for s in range(CAP):
                tile, row, col = fetch(i, o, s)
                term = lax.dot_general(
                    anoms[col], tile, (((1,), (1,)), ((), ())), preferred_element_type=F32
                )
                terms.append((row, term))
        for row, term in terms:
            modelled[row] += term

    observed_in.wait()
    weight_in.wait()
    for r in range(SOUND_DEV):
        factor = weight[r].astype(F32) / 8.0
        gap = modelled[r] - observed[:, r * B : (r + 1) * B]
        weighted[r] = (factor * gap).astype(BF16)
    weighted[SOUND_DEV] = jnp.zeros((LM, B), BF16)

    @pl.loop(0, NT // step)
    def _(i):
        terms = []
        for o in range(step):
            for s in range(CAP):
                tile, row, col = fetch(i, o, s)
                term = lax.dot_general(
                    weighted[row], tile, (((1,), (0,)), ((), ())), preferred_element_type=F32
                )
                terms.append((col, term))
        for col, term in terms:
            total[col] += term

    @pl.loop(0, NT // 4)
    def _(i):
        out[pl.ds(i * 32, 32)] = total[pl.ds(i * 32, 32)].astype(BF16)


def local(codes, tiles, anoms, observed, weight):
    hbm = pl.BlockSpec(memory_space=pltpu.HBM)
    vmem = pl.BlockSpec(memory_space=pltpu.VMEM)
    dma = pltpu.SemaphoreType.DMA
    return pl.pallas_call(
        local_kernel,
        out_shape=jax.ShapeDtypeStruct((NT * FLUX_DEV, LM, B), BF16),
        in_specs=[vmem, vmem, vmem, hbm, hbm],
        out_specs=vmem,
        scratch_shapes=[
            pltpu.SMEM((NT, 1, B), jnp.int32),
            dma,
            pltpu.VMEM((LM, SOUND_DEV * B), F32),
            pltpu.VMEM((SOUND_DEV, 1, B), jnp.int32),
            pltpu.VMEM((SOUND_DEV + 1, LM, B), F32),
            pltpu.VMEM((SOUND_DEV + 1, LM, B), BF16),
            pltpu.VMEM((NT * FLUX_DEV, LM, B), F32),
            dma, dma,
        ],
        compiler_params=pltpu.CompilerParams(vmem_limit_bytes=22 * 2**20),
        name="local",
    )(codes, tiles, anoms.reshape(NT * FLUX_DEV, LM, B), observed, weight)


NA = 5
NB = FLUX_DEV - NA
FAR_X = ((4, 3, 2, 1), (5, 6, 7, 0))
NEAR_X = (4, 5, 3, 6, 2, 7, 1, 0)
FAR_Z = ((2, 1), (3, 0))
NEAR_Z = (2, 1, 3, 0)

GATHER_ORDER = (
    ("b_far", 0), ("b_far", 1), ("a_far", 0), ("a_far", 1), ("a_far", 2), ("a_far", 3), ("b_near", 1, 0),
    ("b_near", 1, 2), ("a_near", 0), ("b_near", 1, 1), ("b_near", 1, 3), ("a_near", 1), ("b_near", 2, 0),
    ("b_near", 2, 2), ("a_near", 2), ("b_near", 2, 1), ("a_near", 3), ("b_near", 2, 3), ("b_near", 3, 0),
    ("a_own", 4), ("a_near", 4), ("b_near", 3, 1), ("a_near", 5), ("b_near", 3, 2), ("b_own", 2),
    ("a_own", 5), ("a_own", 3), ("a_near", 6), ("b_near", 3, 3), ("a_near", 7), ("a_own", 6), ("a_own", 2),
    ("b_own", 3), ("b_own", 1), ("a_own", 7), ("a_own", 1), ("b_own", 0), ("a_own", 0),
)


def gather_kernel(
    part, out,
    pa, pb, ra, rb, xa1, xa2, zb1, zb2, za1, za2, xb1, xb2,
    s_sib_a, r_sib_a, s_sib_b, r_sib_b, s_a2, r_a2, s_b4, r_b4,
    s_xa1, r_xa1, s_xa2, r_xa2, s_zb1, r_zb1, s_zb2, r_zb2, s_za, r_za, s_xb, r_xb,
):
    me = lax.axis_index("tile")
    q = lax.axis_index("mem")
    core = lax.rem(me, 2)
    x = lax.rem(me // 2, NX)
    z = me // 8

    def at_z(o):
        return lax.rem(z + o + NZ, NZ)

    def at_x(o):
        return lax.rem(x + o + NX, NX)

    def index(zz, xx, cc):
        return zz * 8 + xx * 2 + cc

    sibling = index(z, x, 1 - core)
    x_next = (index(z, at_x(1), core), index(z, at_x(-1), core))
    z_next = (index(at_z(1), x, core), index(at_z(-1), x, core))

    pending = []

    def send(src, dst, ssem, rsem, tile):
        cp = pltpu.make_async_remote_copy(
            src_ref=src, dst_ref=dst, send_sem=ssem, recv_sem=rsem,
            device_id={"tile": tile, "mem": q}, device_id_type=MESH,
        )
        cp.start()
        pending.append(cp)

    def wait_for(ref, sem):
        pltpu.make_async_copy(ref, ref, sem).wait()

    barrier = pltpu.get_barrier_semaphore()
    for t in (sibling, *x_next, *z_next):
        pl.semaphore_signal(barrier, inc=1, device_id={"tile": t, "mem": q}, device_id_type=MESH)
    pl.semaphore_wait(barrier, 5)

    for ox in NEAR_Z:
        xx = at_x(ox)
        send(part.at[at_z(4), xx, 1 - core, pl.ds(NA, NB)], rb.at[4, xx], s_b4.at[ox], r_b4.at[ox], sibling)
    for oz in NEAR_X:
        zz = at_z(oz)
        send(part.at[zz, at_x(2), 1 - core, pl.ds(0, NA)], ra.at[2, zz], s_a2.at[oz], r_a2.at[oz], sibling)
    for kind, d in (("b", 3), ("b", 5), ("a", 1), ("a", 3), ("b", 2), ("b", 6), ("b", 1), ("b", 7), ("a", 0), ("b", 0)):
        if kind == "a":
            send(part.at[:, at_x(d), 1 - core, pl.ds(0, NA)], ra.at[d], s_sib_a.at[d], r_sib_a.at[d], sibling)
        else:
            send(part.at[at_z(d), :, 1 - core, pl.ds(NA, NB)], rb.at[d], s_sib_b.at[d], r_sib_b.at[d], sibling)

    settled = set()

    def from_a(d, zz):
        if ("a", d) not in settled:
            settled.add(("a", d))
            if d != 2:
                wait_for(ra.at[d], r_sib_a.at[d])
        return [part.at[zz, at_x(d), core], ra.at[d, zz]]

    def from_b(d, xx):
        if ("b", d) not in settled:
            settled.add(("b", d))
            if d != 4:
                wait_for(rb.at[d], r_sib_b.at[d])
        return [part.at[at_z(d), xx, core, pl.ds(NA, NB)], rb.at[d, xx]]

    def total(dst, sources, first, last):
        @pl.loop(first, last)
        def _(b):
            value = None
            for s in sources:
                ref, start = s if isinstance(s, tuple) else (s, 0)
                v = ref[b - start].astype(F32)
                value = v if value is None else value + v
            dst[b] = value.astype(BF16)

    def result(base, sources, count):
        for b in range(count):
            value = None
            for s in sources:
                v = s[b].astype(F32)
                value = v if value is None else value + v
            out[:, (base + b) * B : (base + b + 1) * B] = value

    def a_far(k):
        for i in range(2):
            zz = at_z(FAR_X[i][k])
            wait_for(ra.at[2, zz], r_a2.at[FAR_X[i][k]])
            total(pa.at[2, zz], from_a(2, zz), 0, NA)
            send(pa.at[2, zz], xa1.at[i, k], s_xa1.at[i, k], r_xa1.at[i, k], x_next[i])

    def a_near(j):
        oz = NEAR_X[j]
        zz = at_z(oz)
        for i, d in enumerate((1, 3)):
            sources = from_a(d, zz)
            if oz in FAR_X[i]:
                k = FAR_X[i].index(oz)
                wait_for(xa1.at[i, k], r_xa1.at[i, k])
                sources.append(xa1.at[i, k])
            total(pa.at[d, zz], sources, 0, NA)
            send(pa.at[d, zz], xa2.at[i, j], s_xa2.at[i, j], r_xa2.at[i, j], x_next[i])

    half_a, half_b = (NA + 1) // 2, (NB + 1) // 2

    def a_own(oz):
        j = NEAR_X.index(oz)
        zz = at_z(oz)
        for i in range(2):
            wait_for(xa2.at[i, j], r_xa2.at[i, j])
        sources = [*from_a(0, zz), xa2.at[0, j], xa2.at[1, j]]
        mine = pa.at[0, zz]
        if oz == 4:
            total(mine, sources, 0, NA)
            for i, (first, size) in enumerate(((0, half_a), (half_a, NA - half_a))):
                piece = za1.at[pl.ds(first, size)]
                send(mine.at[pl.ds(first, size)], piece, s_za.at[i, 0], r_za.at[i, 0], z_next[i])
        elif oz in (3, 5):
            i = (3, 5).index(oz)
            first, size = ((0, half_a), (half_a, NA - half_a))[i]
            wait_for(za1.at[pl.ds(first, size)], r_za.at[i, 0])
            total(mine, [*sources, za1], first, first + size)
            total(mine, sources, *((half_a, NA), (0, half_a))[i])
            send(mine, za2.at[i, 0], s_za.at[i, 1], r_za.at[i, 1], z_next[i])
        elif oz != 0:
            i = 0 if oz < 4 else 1
            step = 4 - oz if i == 0 else oz - 4
            wait_for(za2.at[i, step - 2], r_za.at[i, step - 1])
            total(mine, [*sources, za2.at[i, step - 2]], 0, NA)
            send(mine, za2.at[i, step - 1], s_za.at[i, step], r_za.at[i, step], z_next[i])
        else:
            for i in range(2):
                wait_for(za2.at[i, 2], r_za.at[i, 3])
            result(0, [*sources, za2.at[0, 2], za2.at[1, 2]], NA)

    def b_far(k):
        for i in range(2):
            xx = at_x(FAR_Z[i][k])
            wait_for(rb.at[4, xx], r_b4.at[FAR_Z[i][k]])
            total(pb.at[4, xx], from_b(4, xx), 0, NB)
            send(pb.at[4, xx], zb1.at[i, k], s_zb1.at[i, k], r_zb1.at[i, k], z_next[i])

    def b_near(step, j):
        ox = NEAR_Z[j]
        xx = at_x(ox)
        for i, d in enumerate((4 - step, 4 + step)):
            sources = from_b(d, xx)
            if step > 1:
                wait_for(zb2.at[i, step - 2, j], r_zb2.at[i, step - 2, j])
                sources.append(zb2.at[i, step - 2, j])
            elif ox in FAR_Z[i]:
                k = FAR_Z[i].index(ox)
                wait_for(zb1.at[i, k], r_zb1.at[i, k])
                sources.append(zb1.at[i, k])
            total(pb.at[d, xx], sources, 0, NB)
            send(
                pb.at[d, xx], zb2.at[i, step - 1, j], s_zb2.at[i, step - 1, j], r_zb2.at[i, step - 1, j], z_next[i]
            )

    def b_own(ox):
        j = NEAR_Z.index(ox)
        xx = at_x(ox)
        for i in range(2):
            wait_for(zb2.at[i, 2, j], r_zb2.at[i, 2, j])
        sources = [*from_b(0, xx), zb2.at[0, 2, j], zb2.at[1, 2, j]]
        mine = pb.at[0, xx]
        halves = ((0, half_b), (half_b, NB - half_b))
        if ox == 2:
            total(mine, sources, 0, NB)
            for i, (first, size) in enumerate(halves):
                piece = xb1.at[pl.ds(first, size)]
                send(mine.at[pl.ds(first, size)], piece, s_xb.at[i, 0], r_xb.at[i, 0], x_next[i])
        elif ox != 0:
            i = (1, 3).index(ox)
            first, size = halves[i]
            wait_for(xb1.at[pl.ds(first, size)], r_xb.at[i, 0])
            total(mine, [*sources, xb1], first, first + size)
            total(mine, sources, *((half_b, NB), (0, half_b))[i])
            send(mine, xb2.at[i], s_xb.at[i, 1], r_xb.at[i, 1], x_next[i])
        else:
            for i in range(2):
                wait_for(xb2.at[i], r_xb.at[i, 1])
            result(NA, [*sources, xb2.at[0], xb2.at[1]], NB)

    acts = {"a_far": a_far, "a_near": a_near, "a_own": a_own, "b_far": b_far, "b_near": b_near, "b_own": b_own}
    for name, *numbers in GATHER_ORDER:
        while len(pending) > 30:
            pending.pop(0).wait_send()
        acts[name](*numbers)
    for cp in pending:
        cp.wait_send()


def gather(part):
    vmem = pl.BlockSpec(memory_space=pltpu.VMEM)
    dma = pltpu.SemaphoreType.DMA
    return pl.pallas_call(
        gather_kernel,
        out_shape=jax.ShapeDtypeStruct((LM, FLUX_DEV * B), F32),
        in_specs=[vmem],
        out_specs=vmem,
        scratch_shapes=[
            pltpu.VMEM((NX, NZ, NA, LM, B), BF16),
            pltpu.VMEM((NZ, NX, NB, LM, B), BF16),
            pltpu.VMEM((NX, NZ, NA, LM, B), BF16),
            pltpu.VMEM((NZ, NX, NB, LM, B), BF16),
            pltpu.VMEM((2, 4, NA, LM, B), BF16),
            pltpu.VMEM((2, NZ, NA, LM, B), BF16),
            pltpu.VMEM((2, 2, NB, LM, B), BF16),
            pltpu.VMEM((2, 3, NX, NB, LM, B), BF16),
            pltpu.VMEM((NA, LM, B), BF16),
            pltpu.VMEM((2, 3, NA, LM, B), BF16),
            pltpu.VMEM((NB, LM, B), BF16),
            pltpu.VMEM((2, NB, LM, B), BF16),
            dma((NX,)), dma((NX,)), dma((NZ,)), dma((NZ,)), dma((NZ,)), dma((NZ,)), dma((NX,)), dma((NX,)),
            dma((2, 4)), dma((2, 4)), dma((2, NZ)), dma((2, NZ)),
            dma((2, 2)), dma((2, 2)), dma((2, 3, NX)), dma((2, 3, NX)),
            dma((2, 4)), dma((2, 4)), dma((2, 2)), dma((2, 2)),
        ],
        compiler_params=pltpu.CompilerParams(
            collective_id=1, has_side_effects=True, vmem_limit_bytes=18 * 2**20
        ),
        name="gather",
    )(part.reshape(NZ, NX, 2, FLUX_DEV, LM, B))


def body(footprints, tile_row, tile_col, prior_flux, observed, precision_weight):
    pin = functools.partial(pltpu.with_memory_space_constraint, memory_space=pltpu.HBM)
    footprints, prior_flux, observed = pin(footprints), pin(prior_flux), pin(observed)
    tile_row, tile_col = pin(tile_row.reshape(1, B)), pin(tile_col.reshape(1, B))
    tiles, anoms, codes = spread(tile_row, tile_col, footprints, prior_flux)
    weight = pin(precision_weight.reshape(SOUND_DEV, 1, B))
    part = local(codes, tiles, anoms, observed, weight)
    return gather(part)


def solution(mesh):
    in_specs = (
        P("tile", None, None),
        P("tile"),
        P("tile"),
        P("mem", "tile"),
        P("mem", "tile"),
        P("tile"),
    )
    out_specs = P("mem", "tile")
    return jax.shard_map(body, mesh=mesh, in_specs=in_specs, out_specs=out_specs, check_vma=False)
```
